512 devices in a mesh: dp: 128 (over y, z, core), term: 4 (over x).
Axes of the slice: x: 4, y: 8, z: 8, core: 2. Of those that a mesh axis runs over, the one named last changes fastest.
Arguments:
- hidden: bfloat16 [128, 256, 768], P('dp'), may hold values from -100 to 100, as said below
- segment_ids: int32 [128, 256], replicated, may hold values from 0 to 3, never falling along the last dimension, each value on 1 to 160 neighbouring positions
- block_lists: int32 [512, 128], replicated, may hold values from 0 to 255, all different within a row
- doc_ids: int32 [512], replicated, may hold values from 0 to 511, each once
- attn_gain: float32 [768], replicated, may hold values from 0.1 to 1.9
- qkv_weight: bfloat16 [3, 768, 768], P(None, None, 'term'), may hold values from -0.21875 to 0.21875
- attn_out: bfloat16 [768, 768], P('term'), may hold values from -0.21875 to 0.21875
- mlp_gain: float32 [768], replicated, may hold values from 0.1 to 1.9
- ffn_in: bfloat16 [2, 768, 1152], P(None, None, 'term'), may hold values from -0.21875 to 0.21875
- ffn_out: bfloat16 [1152, 768], P('term'), may hold values from -0.1875 to 0.1875
- final_gain: float32 [768], replicated, may hold values from 0.1 to 1.9
- head_dense: bfloat16 [768, 768], replicated, may hold values from -0.21875 to 0.21875
- head_gain: float32 [768], replicated, may hold values from 0.1 to 1.9
- decoder: bfloat16 [4, 8, 128, 8, 768], P('term', None, 'dp'), may hold values from -0.21875 to 0.21875
- decoder_bias: bfloat16 [4, 8, 128, 8], P('term', None, 'dp'), may hold values from -5 to 5
Outputs:
- postings: float32 [4, 8, 128, 8, 512], P('term', None, 'dp')
The draws below stay inside these ranges and needn't reach their ends.
Inputs may be any that keep to these rules, and one draw needn't show every extreme that they name: `hidden`: every token has its own scale, and every feature its own scale. `segment_ids`: each row's numbers never fall and each of 0 to 3 appears; a passage has 1 to 160 tokens, and some passage of each row has exactly 160. `block_lists`: a passage lists 128 different blocks; every block is listed by some passage. `doc_ids`: each column appears once.
All inputs are finite; a program needn't handle non-finite values.
Results may differ from the reference program's by a relative error of at most 0.0035.
Values may be sent and summed in bfloat16 or wider, within the bound.
No kernel may reach another device: no remote copies, remote signals or barrier semaphores. Data moves between devices by JAX's collectives and lax.ppermute only.
A program may use at most 128 MiB of HBM per device.

```python
import math
import jax
import jax.numpy as jnp
import numpy as np
from jax import lax

D = 768
HEADS = 12
FF = 1152
VOCAB = 32768
BLOCK = 128
LISTED = 128
HALF_WIN = 64
GROUPS = 8
TOK_DEV = 256
PASS_DEV = 4
HEAD_DIM = 64
ROWS = 128
PASSAGES = 512
NBLK = 256
SPAN = 8
MOST_LEN = 160
N_DP = 128
N_TERM = 4


def draw_hidden(key, part):
    key_base, key_rows, key_cols = jax.random.split(key, 3)
    row_scale = jnp.exp(jax.random.uniform(key_rows, (ROWS, TOK_DEV, 1), jnp.float32, math.log(0.3), math.log(3.0)))
    col_scale = jnp.exp(jax.random.uniform(key_cols, (1, 1, D), jnp.float32, math.log(0.4), math.log(4.0)))
    base_draw = jnp.clip(jax.random.normal(key_base, (ROWS, TOK_DEV, D), jnp.float32), -5.0, 5.0)
    return (base_draw * row_scale * col_scale).astype(jnp.bfloat16)


def shard_levels(own_key, extent, cuts, least, high):
    def one(axis_at, shards_of):
        draws = jax.random.uniform(jax.random.fold_in(jax.random.fold_in(own_key, 6), axis_at), (shards_of,), jnp.float32, least / len(cuts), high / len(cuts))
        return jnp.repeat(jnp.exp(draws), extent[axis_at] // shards_of).reshape((-1,) + (1,) * (len(extent) - axis_at - 1))

    level = one(*cuts[0])
    for cut in cuts[1:]:
        level = level * one(*cut)
    return level


def distinct(stream_key, rows, number_of, top, lift):
    order = jax.random.permutation(jax.random.fold_in(stream_key, 1), number_of)
    favour = order
    for power in range(3):
        favour = favour * favour // number_of
    favour = favour * lift // number_of
    lots = jax.random.randint(jax.random.fold_in(stream_key, 2), (rows, number_of), 0, 4096) + favour
    sure = jax.random.permutation(jax.random.fold_in(stream_key, 3), rows)[jnp.arange(number_of) % rows]
    lots = jnp.where(jnp.arange(rows)[:, None] == sure[None, :], 1 << 14, lots)
    score = lots * number_of + jnp.arange(number_of)
    return lax.top_k(score.astype(jnp.int32), top)[1].astype(jnp.int32)


def split_up(number_of, total, reach, skew):
    portions = [(1 << 20) // math.isqrt(standing ** skew) + 1 for standing in range(2, number_of + 1)]
    rest, holding = total - reach - (number_of - 1), [1] * (number_of - 1)
    while rest > 0:
        candidates = [i for i in range(number_of - 1) if holding[i] < reach]
        pool, budget = sum([portions[i] for i in candidates]), rest
        for i in candidates:
            extra = min(reach - holding[i], max(1, budget * portions[i] // pool), rest)
            holding[i] = holding[i] + extra
            rest = rest - extra
    return np.array([reach] + holding)


def uneven_parts(stream_key, count, total, limit, skew):
    if count == 2:
        one = jax.random.randint(stream_key, (), max(1, total - limit), min(limit, total - 1) + 1)
        return jnp.stack([one, total - one])
    tallies = jnp.asarray(split_up(count, total, limit, skew), jnp.int32)
    twos = (count - 1) // 2
    donor, sink = tallies[1:1 + 2 * twos:2], tallies[2:2 + 2 * twos:2]
    room = jnp.minimum(donor - 1, limit - sink)
    passed = jax.random.randint(jax.random.fold_in(stream_key, 1), (twos,), 0, 1 << 20) % (room + 1)
    tallies = tallies.at[1:1 + 2 * twos:2].set(donor - passed).at[2:2 + 2 * twos:2].set(sink + passed)
    return tallies[jax.random.permutation(jax.random.fold_in(stream_key, 2), count)]


def normal_values(key, extent, width, reach, pieces=(), held_as=jnp.bfloat16):
    array = width * jax.random.normal(key, extent, jnp.float32)
    if pieces:
        array = array * shard_levels(key, extent, pieces, -0.22, 0.18)
    return jnp.clip(array, -reach, reach).astype(held_as)


def setup_inputs(seed: int = 0) -> dict:
    keys = jax.random.split(jax.random.key(seed), 16)
    return {
        "hidden": draw_hidden(jax.random.fold_in(keys[15], 71), 0),
        "segment_ids": jax.vmap(lambda own: jnp.searchsorted(jnp.cumsum(uneven_parts(own, PASS_DEV, TOK_DEV, MOST_LEN, 2)), jnp.arange(TOK_DEV), side="right"))(jax.random.split(keys[1], ROWS)).reshape((ROWS, TOK_DEV)).astype(jnp.int32),
        "block_lists": distinct(keys[2], PASSAGES, NBLK, LISTED, 8192),
        "doc_ids": jax.random.permutation(keys[3], PASSAGES).astype(jnp.int32),
        "attn_gain": jnp.clip(1.0 + 0.18 * jax.random.normal(keys[4], (D,), jnp.float32), 0.1, 1.9),
        "qkv_weight": normal_values(keys[5], (3, D, D), D ** -0.5, 0.21875, ((2, 4),)),
        "attn_out": normal_values(keys[6], (D, D), D ** -0.5, 0.21875, ((0, 4),)),
        "mlp_gain": jnp.clip(1.0 + 0.18 * jax.random.normal(keys[7], (D,), jnp.float32), 0.1, 1.9),
        "ffn_in": normal_values(keys[8], (2, D, FF), D ** -0.5, 0.21875, ((2, 4),)),
        "ffn_out": normal_values(keys[9], (FF, D), FF ** -0.5, 0.1875, ((0, 4),)),
        "final_gain": jnp.clip(1.0 + 0.18 * jax.random.normal(keys[10], (D,), jnp.float32), 0.1, 1.9),
        "head_dense": normal_values(keys[11], (D, D), D ** -0.5, 0.21875),
        "head_gain": jnp.clip(1.0 + 0.18 * jax.random.normal(keys[12], (D,), jnp.float32), 0.1, 1.9),
        "decoder": normal_values(keys[13], (N_TERM, GROUPS, N_DP, SPAN, D), D ** -0.5, 0.21875, ((0, 4), (2, 128))),
        "decoder_bias": normal_values(keys[14], (N_TERM, GROUPS, N_DP, SPAN), 1.0, 5.0, ((0, 4), (2, 128))),
    }


def layer_norm(values, gain_vec):
    average = lax.optimization_barrier(jnp.mean(values, axis=-1, keepdims=True))
    centered = values - average
    spread = lax.optimization_barrier(jnp.mean(centered * centered, axis=-1, keepdims=True))
    return centered * lax.rsqrt(spread + 1e-05) * gain_vec

def rotary(values, positions):
    half_dim = values.shape[-1] // 2
    frequency = 10000.0 ** (-2.0 * jnp.arange(half_dim, dtype=jnp.float32) / values.shape[-1])
    angles = positions.astype(jnp.float32)[:, None] * frequency[None, :]
    cosine = jnp.cos(angles)[:, None, :]
    sine_part = jnp.sin(angles)[:, None, :]
    first_half = values[..., :half_dim]
    second = values[..., half_dim:]
    return jnp.concatenate([first_half * cosine - second * sine_part, second * cosine + first_half * sine_part], axis=-1)

def reference(hidden, segment_ids, block_lists, doc_ids, attn_gain, qkv_weight, attn_out, mlp_gain, ffn_in, ffn_out, final_gain, head_dense, head_gain, decoder, decoder_bias):
    table = decoder.reshape(VOCAB, D)
    biases = decoder_bias.reshape(VOCAB).astype(jnp.float32)
    lists_by_row = block_lists.reshape(ROWS, PASS_DEV, LISTED)

    def one_row(inputs):
        tokens, segments, own_lists = inputs
        token_index = jnp.arange(TOK_DEV, dtype=jnp.int32)
        positions = token_index - lax.optimization_barrier(jnp.sum((segments[None, :] < segments[:, None]).astype(jnp.int32), axis=1))
        allowed = (segments[:, None] == segments[None, :]) & (jnp.abs(token_index[:, None] - token_index[None, :]) <= HALF_WIN)
        normed = layer_norm(tokens.astype(jnp.float32), attn_gain).astype(jnp.bfloat16)

        def project(which_slot):
            return jnp.dot(normed, qkv_weight[which_slot], preferred_element_type=jnp.float32).reshape(TOK_DEV, HEADS, HEAD_DIM)
        queries = rotary(project(0), positions).astype(jnp.bfloat16)
        key_rows = rotary(project(1), positions).astype(jnp.bfloat16)
        values = project(2).astype(jnp.bfloat16)
        scores = jnp.einsum('qhd,khd->hqk', queries.astype(jnp.float32), key_rows.astype(jnp.float32)) * HEAD_DIM ** (-0.5)
        raised = jnp.where(allowed[None], jnp.exp(scores), 0.0)
        probabilities = (raised / lax.optimization_barrier(jnp.sum(raised, axis=-1, keepdims=True))).astype(jnp.bfloat16)
        context = jnp.einsum('hqk,khd->qhd', probabilities.astype(jnp.float32), values.astype(jnp.float32))
        context = context.astype(jnp.bfloat16).reshape(TOK_DEV, D)
        after_attn = tokens.astype(jnp.float32) + jnp.dot(context, attn_out, preferred_element_type=jnp.float32)
        mixed_in = layer_norm(after_attn, mlp_gain).astype(jnp.bfloat16)
        inner_up = jnp.dot(mixed_in, ffn_in[0], preferred_element_type=jnp.float32)
        gate_part = jnp.dot(mixed_in, ffn_in[1], preferred_element_type=jnp.float32)
        activated = (jax.nn.gelu(inner_up, approximate=False) * gate_part).astype(jnp.bfloat16)
        after_ffn = after_attn + jnp.dot(activated, ffn_out, preferred_element_type=jnp.float32)
        normed_out = layer_norm(after_ffn, final_gain).astype(jnp.bfloat16)
        dense_out = jnp.dot(normed_out, head_dense, preferred_element_type=jnp.float32)
        headed = layer_norm(jax.nn.gelu(dense_out, approximate=False), head_gain).astype(jnp.bfloat16)
        logits = lax.dot_general(headed, table, (((1,), (1,)), ((), ())), preferred_element_type=jnp.float32) + biases[None, :]
        activity = jnp.log1p(jnp.maximum(logits, 0.0))
        maxima = jnp.stack([lax.optimization_barrier(jnp.max(jnp.where(segments[:, None] == passage, activity, 0.0), axis=0)) for passage in range(PASS_DEV)])
        listed = jnp.any(own_lists[:, :, None] == jnp.arange(NBLK, dtype=jnp.int32)[None, None, :], axis=1)
        active = jnp.repeat(listed.astype(jnp.float32), BLOCK, axis=1)
        return maxima * active
    pooled = lax.map(one_row, (hidden, segment_ids, lists_by_row)).reshape(PASSAGES, VOCAB)
    placed = jnp.zeros((VOCAB, PASSAGES), jnp.float32).at[:, doc_ids].set(pooled.T)
    return placed.reshape(N_TERM, GROUPS, N_DP, SPAN, PASSAGES)
```

```python
import functools

import jax
import jax.numpy as jnp
import numpy as np
from jax import lax
from jax.experimental import pallas as pl
from jax.experimental.pallas import tpu as pltpu
from jax.sharding import Mesh
from jax.sharding import PartitionSpec as P

BLOCK = 128
HALF_WIN = 64
PASS_DEV = 4
HEAD_DIM = 64
HALF_HEAD = 32
LOWEST = -3.0e38

NT = (((1,), (1,)), ((), ()))
TN = (((0,), (0,)), ((), ()))


def rotary_table(length):
    frequency = 10000.0 ** (-2.0 * np.arange(HALF_HEAD, dtype=np.float64) / HEAD_DIM)
    angles = frequency[:, None] * np.arange(length, dtype=np.float64)[None, :]
    terms = []
    for whole in (np.cos(angles), np.sin(angles)):
        rest = whole.astype(np.float32)
        for _ in range(3):
            term = rest.astype(jnp.bfloat16)
            terms.append(term)
            rest = rest - term.astype(np.float32)
    return np.concatenate(terms, axis=0)


def layer_norm(values, gain_row):
    average = jnp.mean(values, axis=-1, keepdims=True)
    centered = values - average
    spread = jnp.mean(centered * centered, axis=-1, keepdims=True)
    return centered * lax.rsqrt(spread + 1e-05) * gain_row


def gelu(values):
    return 0.5 * values * (1.0 + lax.erf(values * np.float32(0.5**0.5)))


def matmul(left, right, dims):
    return lax.dot_general(left, right, dims, preferred_element_type=jnp.float32)


def attention_kernel(row_ref, hidden_ref, segment_ref, gain_ref, weight_ref, table_ref, out_ref):
    length = hidden_ref.shape[0]
    head_width = weight_ref.shape[1]
    segments = segment_ref[pl.ds(row_ref[0], 1), :]
    starts = jnp.zeros_like(segments)
    for passage in range(PASS_DEV - 1):
        held = jnp.sum((segments == passage).astype(jnp.int32), axis=1, keepdims=True)
        starts = starts + jnp.where(segments > passage, held, 0)
    lane = lax.broadcasted_iota(jnp.int32, (1, length), 1)
    positions = lane - starts
    sublane = lax.broadcasted_iota(jnp.int32, (length, length), 0)
    chosen = (sublane == positions).astype(jnp.float32).astype(jnp.bfloat16)
    parts = matmul(table_ref[...], chosen, (((1,), (0,)), ((), ())))
    part = [parts[i * HALF_HEAD : (i + 1) * HALF_HEAD] for i in range(6)]
    cosine = part[0] + part[1] + part[2]
    sine = part[3] + part[4] + part[5]
    lengths = jnp.zeros_like(segments)
    for passage in range(PASS_DEV):
        held = jnp.sum((segments == passage).astype(jnp.int32), axis=1, keepdims=True)
        lengths = jnp.where(segments == passage, held, lengths)
    low = jnp.maximum(starts, lane - HALF_WIN)
    high = jnp.minimum(starts + lengths - 1, lane + HALF_WIN)
    allowed = (sublane >= low) & (sublane <= high)

    normed = layer_norm(hidden_ref[...].astype(jnp.float32), gain_ref[...]).astype(jnp.bfloat16)
    queries = matmul(weight_ref[0], normed, NT)
    key_cols = matmul(weight_ref[1], normed, NT)
    values = matmul(weight_ref[2], normed, NT).astype(jnp.bfloat16)

    def rotate(block):
        first, second = block[:HALF_HEAD], block[HALF_HEAD:]
        turned = jnp.concatenate(
            [first * cosine - second * sine, second * cosine + first * sine], axis=0
        )
        return turned.astype(jnp.bfloat16)

    for head in range(head_width // HEAD_DIM):
        at = slice(head * HEAD_DIM, (head + 1) * HEAD_DIM)
        scores = matmul(rotate(key_cols[at]), rotate(queries[at]), TN) * np.float32(HEAD_DIM**-0.5)
        raised = jnp.where(allowed, jnp.exp(scores), 0.0)
        probabilities = (raised / jnp.sum(raised, axis=0, keepdims=True)).astype(jnp.bfloat16)
        context = matmul(values[at], probabilities, (((1,), (0,)), ((), ()))).astype(jnp.bfloat16)
        for copy in range(out_ref.shape[0]):
            out_ref[copy, at, :] = context


def inner_kernel(hidden_ref, context_ref, out_weight_ref, gain_ref, in_ref, after_ref, inner_ref):
    attended = matmul(context_ref[...], out_weight_ref[...], TN)
    after_attn = hidden_ref[...].astype(jnp.float32) + attended
    after_ref[...] = after_attn
    mixed = layer_norm(after_attn, gain_ref[...]).astype(jnp.bfloat16)
    inner_up = matmul(in_ref[0], mixed, NT)
    gate_part = matmul(in_ref[1], mixed, NT)
    activated = (gelu(inner_up) * gate_part).astype(jnp.bfloat16)
    for copy in range(inner_ref.shape[0]):
        inner_ref[copy] = activated


def head_kernel(after_ref, inner_ref, down_ref, final_ref, dense_ref, head_ref, out_ref):
    after_ffn = after_ref[...] + matmul(inner_ref[...], down_ref[...], TN)
    normed = layer_norm(after_ffn, final_ref[...]).astype(jnp.bfloat16)
    dense = matmul(normed, dense_ref[...], (((1,), (0,)), ((), ())))
    out_ref[...] = layer_norm(gelu(dense), head_ref[...]).astype(jnp.bfloat16)


def pool_kernel(
    row_ref, own_ref, core_ref, far_ref, far_core_ref, segment_ref, table_ref, out_ref, where_ref
):
    rows = (own_ref, core_ref, far_ref, far_core_ref)

    @pl.when(pl.program_id(0) == 0)
    def _():
        listed = [segment_ref[pl.ds(row_ref[r], 1), :] for r in range(len(rows))]
        stacked = jnp.concatenate(listed + listed, axis=0)
        columns = jnp.transpose(stacked)
        for r in range(len(rows)):
            where_ref[r] = jnp.broadcast_to(columns[:, r : r + 1], where_ref.shape[1:])

    width = where_ref.shape[2]
    terms = table_ref.shape[0]
    table = table_ref[...]
    maxima = []
    for r, row in enumerate(rows):
        logits = matmul(row[...], table, NT)
        for passage in range(PASS_DEV):
            inside = where_ref[r] == passage
            pieces = [
                jnp.max(
                    jnp.where(inside, logits[:, at : at + width], LOWEST), axis=0, keepdims=True
                )
                for at in range(0, terms, width)
            ]
            maxima.append(jnp.concatenate(pieces, axis=1))
    half = len(maxima) // 2
    low = jnp.concatenate(maxima[:half], axis=0)
    high = jnp.concatenate(maxima[half:], axis=0)
    own_terms = out_ref.shape[2] // 2
    for slot in range(out_ref.shape[0]):
        at = slice(slot * own_terms, (slot + 1) * own_terms)
        out_ref[slot] = jnp.concatenate([low[:, at], high[:, at]], axis=1)


def place_kernel(maxima_ref, bias_ref, listed_ref, docs_ref, out_ref):
    raw = maxima_ref[...] + bias_ref[...]
    weighted = jnp.log1p(jnp.maximum(raw, 0.0)) * listed_ref[...]
    own_terms, passages = out_ref.shape
    columns = lax.broadcasted_iota(jnp.int32, (weighted.shape[0], passages), 1)
    terms = []
    rest = weighted
    for _ in range(3):
        terms.append(rest.astype(jnp.bfloat16))
        rest = rest - terms[-1].astype(jnp.float32)
    placed = jnp.zeros((own_terms, passages), jnp.float32)
    for half in range(2):
        place = (docs_ref[half] == columns).astype(jnp.float32).astype(jnp.bfloat16)
        at = slice(half * own_terms, (half + 1) * own_terms)
        sums = [matmul(term, place, TN)[at] for term in terms]
        placed = placed + (sums[0] + sums[1] + sums[2])
    out_ref[...] = placed


def vmem():
    return pl.BlockSpec(memory_space=pltpu.VMEM)


def smem():
    return pl.BlockSpec(memory_space=pltpu.SMEM)


def grant(mib):
    return pltpu.CompilerParams(vmem_limit_bytes=mib << 20)


def cost(flops, nbytes):
    return pl.CostEstimate(flops=flops, bytes_accessed=nbytes, transcendentals=0)


def exchange(copies, axis):
    return lax.all_to_all(copies, axis, split_axis=0, concat_axis=0, tiled=True)


def gather_by_exchange(block, axis):
    return exchange(jnp.broadcast_to(block[None], (lax.axis_size(axis),) + block.shape), axis)


def swap(block, axis):
    return lax.ppermute(block, axis, [(0, 1), (1, 0)])


def on_device(
    hidden,
    segment_ids,
    block_lists,
    doc_ids,
    attn_gain,
    qkv_weight,
    attn_out,
    mlp_gain,
    ffn_in,
    ffn_out,
    final_gain,
    head_dense,
    head_gain,
    decoder,
    decoder_bias,
):
    near = ("y", "zh")
    slices = lax.axis_size(near)
    slice_index = lax.axis_index(near)
    near_row = lax.axis_index(("zl", "core"))
    rows_here = lax.axis_size(("zl", "core"))
    row_index = slice_index * rows_here + near_row
    tensor = lax.axis_size("term")
    tokens = hidden[0]
    length, width = tokens.shape
    groups, span = decoder.shape[1], decoder.shape[3]
    own_terms = groups * span
    head_width = qkv_weight.shape[2]
    hidden_units = ffn_in.shape[2]
    passages = block_lists.shape[0]
    near_rows = jnp.stack([jnp.bitwise_xor(near_row, d) for d in range(rows_here)])
    row_ids = slice_index * rows_here + near_rows

    own_slice = decoder.reshape(own_terms, width)
    part = gather_by_exchange(own_slice, "zh").reshape(-1, width)
    out_weight = gather_by_exchange(attn_out, "term").reshape(-1, width)

    context = pl.pallas_call(
        attention_kernel,
        out_shape=jax.ShapeDtypeStruct((tensor, head_width, length), jnp.bfloat16),
        in_specs=[smem()] + [vmem()] * 5,
        out_specs=vmem(),
        cost_estimate=cost(1200000000, 60000000),
        compiler_params=grant(20),
        name="attention",
    )(
        row_ids,
        tokens,
        segment_ids,
        attn_gain[None],
        jnp.swapaxes(qkv_weight, 1, 2),
        jnp.asarray(rotary_table(length)),
    )
    context, part, out_weight = lax.optimization_barrier((context, part, out_weight))
    table = lax.all_gather(part, "y", axis=0, tiled=True)
    all_context = exchange(context, "term").reshape(-1, length)
    down_weight = gather_by_exchange(ffn_out, "term").reshape(-1, width)
    after_attn, inner = pl.pallas_call(
        inner_kernel,
        out_shape=(
            jax.ShapeDtypeStruct((length, width), jnp.float32),
            jax.ShapeDtypeStruct((tensor, hidden_units, length), jnp.bfloat16),
        ),
        in_specs=[vmem()] * 5,
        out_specs=(vmem(), vmem()),
        cost_estimate=cost(600000000, 4000000),
        compiler_params=grant(20),
        name="inner",
    )(tokens, all_context, out_weight, mlp_gain[None], jnp.swapaxes(ffn_in, 1, 2))
    inner, down_weight = lax.optimization_barrier((inner, down_weight))
    all_inner = exchange(inner, "term").reshape(-1, length)
    headed = pl.pallas_call(
        head_kernel,
        out_shape=jax.ShapeDtypeStruct((length, width), jnp.bfloat16),
        in_specs=[vmem()] * 6,
        out_specs=vmem(),
        cost_estimate=cost(800000000, 5000000),
        compiler_params=grant(20),
        name="head",
    )(after_attn, all_inner, down_weight, final_gain[None], head_dense, head_gain[None])

    far = swap(headed, "zl")
    core = swap(headed, "core")
    far_core = swap(far, "core")
    terms_here = slices * own_terms
    step = 256
    pooled = pl.pallas_call(
        pool_kernel,
        out_shape=jax.ShapeDtypeStruct((slices, 2 * PASS_DEV, 2 * own_terms), jnp.float32),
        grid=(terms_here // step,),
        in_specs=[smem()]
        + [pl.BlockSpec((length, width), lambda j: (0, 0))] * rows_here
        + [
            pl.BlockSpec(segment_ids.shape, lambda j: (0, 0)),
            pl.BlockSpec((step, width), lambda j: (j, 0)),
        ],
        out_specs=pl.BlockSpec(
            (step // own_terms, 2 * PASS_DEV, 2 * own_terms), lambda j: (j, 0, 0)
        ),
        scratch_shapes=[pltpu.VMEM((rows_here, length, 128), jnp.int32)],
        cost_estimate=cost(3300000000, 6000000),
        compiler_params=grant(56),
        name="pool",
    )(row_ids, headed, core, far, far_core, segment_ids, table)
    received = exchange(pooled, near)

    bias = decoder_bias.reshape(1, own_terms).astype(jnp.float32)
    dp_count = slices * rows_here
    first_block = (lax.axis_index("term") * groups * dp_count * span + row_index * span) // BLOCK
    own_blocks = first_block + jnp.arange(groups, dtype=jnp.int32) * (dp_count * span // BLOCK)
    listed = jnp.any(block_lists[:, :, None] == own_blocks[None, None, :], axis=1)
    by_row = listed.astype(jnp.float32).reshape(slices, rows_here, PASS_DEV, groups)
    listed = jnp.stack([by_row[:, near_rows[d]] for d in range(rows_here)], axis=1)
    listed = jnp.repeat(listed, span, axis=3).reshape(slices, 2, 2 * PASS_DEV, own_terms)
    listed = jnp.transpose(listed, (0, 2, 1, 3)).reshape(slices * 2 * PASS_DEV, 2 * own_terms)
    docs = doc_ids.reshape(slices, rows_here, PASS_DEV)
    docs = jnp.stack([docs[:, near_rows[d]] for d in range(rows_here)], axis=1)
    docs = jnp.transpose(docs.reshape(slices, 2, 2 * PASS_DEV), (1, 0, 2)).reshape(2, -1, 1)
    placed = pl.pallas_call(
        place_kernel,
        out_shape=jax.ShapeDtypeStruct((own_terms, passages), jnp.float32),
        in_specs=[vmem()] * 4,
        out_specs=vmem(),
        cost_estimate=cost(200000000, 1000000),
        compiler_params=grant(16),
        name="place",
    )(
        received.reshape(-1, 2 * own_terms),
        jnp.concatenate([bias, bias], axis=1),
        listed,
        docs,
    )
    return placed.reshape(1, groups, 1, span, passages)


def solution(mesh):
    shape = (8, 4, 2, 2, mesh.devices.shape[1])
    fine = Mesh(mesh.devices.reshape(shape), ("y", "zh", "zl", "core", "term"))
    dp = ("y", "zh", "zl", "core")
    in_specs = (
        P(dp, None, None),
        P(),
        P(),
        P(),
        P(),
        P(None, None, "term"),
        P("term", None),
        P(),
        P(None, None, "term"),
        P("term", None),
        P(),
        P(),
        P(),
        P("term", None, dp, None, None),
        P("term", None, dp, None),
    )
    out_specs = P("term", None, dp, None, None)
    return jax.shard_map(
        on_device, mesh=fine, in_specs=in_specs, out_specs=out_specs, check_vma=False
    )
```

```python
import functools

import jax
import jax.numpy as jnp
import numpy as np
from jax import lax
from jax.experimental import pallas as pl
from jax.experimental.pallas import tpu as pltpu
from jax.sharding import Mesh
from jax.sharding import PartitionSpec as P

BLOCK = 128
HALF_WIN = 64
PASS_DEV = 4
HEAD_DIM = 64
HALF_HEAD = 32
SPAN = 8
NEAR = 4
LOWEST = -3.0e38
NEAR_AT, TERM_AT, BLOCK_AT, STRIDE_AT = 4, 5, 6, 7

NT = (((1,), (1,)), ((), ()))
TN = (((0,), (0,)), ((), ()))


def rotary_table(length):
    frequency = 10000.0 ** (-2.0 * np.arange(HALF_HEAD, dtype=np.float64) / HEAD_DIM)
    angles = frequency[:, None] * np.arange(length, dtype=np.float64)[None, :]
    terms = []
    for whole in (np.cos(angles), np.sin(angles)):
        rest = whole.astype(np.float32)
        for _ in range(3):
            term = rest.astype(jnp.bfloat16)
            terms.append(term)
            rest = rest - term.astype(np.float32)
    return np.concatenate(terms, axis=0)


def layer_norm(values, gain_row):
    average = jnp.mean(values, axis=-1, keepdims=True)
    centered = values - average
    spread = jnp.mean(centered * centered, axis=-1, keepdims=True)
    return centered * lax.rsqrt(spread + 1e-05) * gain_row


def gelu(values):
    return 0.5 * values * (1.0 + lax.erf(values * np.float32(0.5**0.5)))


def matmul(left, right, dims):
    return lax.dot_general(left, right, dims, preferred_element_type=jnp.float32)


def attention_kernel(
    row_ref, hidden_ref, segment_ref, gain_ref, weight_ref, table_ref, out_weight_ref, out_ref
):
    out_weight = out_weight_ref[...]
    length = hidden_ref.shape[0]
    head_width = weight_ref.shape[1]
    segments = segment_ref[pl.ds(row_ref[0], 1), :]
    starts = jnp.zeros_like(segments)
    for passage in range(PASS_DEV - 1):
        held = jnp.sum((segments == passage).astype(jnp.int32), axis=1, keepdims=True)
        starts = starts + jnp.where(segments > passage, held, 0)
    lane = lax.broadcasted_iota(jnp.int32, (1, length), 1)
    positions = lane - starts
    sublane = lax.broadcasted_iota(jnp.int32, (length, length), 0)
    chosen = (sublane == positions).astype(jnp.float32).astype(jnp.bfloat16)
    parts = matmul(table_ref[...], chosen, (((1,), (0,)), ((), ())))
    part = [parts[i * HALF_HEAD : (i + 1) * HALF_HEAD] for i in range(6)]
    cosine = part[0] + part[1] + part[2]
    sine = part[3] + part[4] + part[5]
    lengths = jnp.zeros_like(segments)
    for passage in range(PASS_DEV):
        held = jnp.sum((segments == passage).astype(jnp.int32), axis=1, keepdims=True)
        lengths = jnp.where(segments == passage, held, lengths)
    low = jnp.maximum(starts, lane - HALF_WIN)
    high = jnp.minimum(starts + lengths - 1, lane + HALF_WIN)
    allowed = (sublane >= low) & (sublane <= high)

    normed = layer_norm(hidden_ref[...].astype(jnp.float32), gain_ref[...]).astype(jnp.bfloat16)
    queries = matmul(weight_ref[0], normed, NT)
    key_cols = matmul(weight_ref[1], normed, NT)
    values = matmul(weight_ref[2], normed, NT).astype(jnp.bfloat16)

    def rotate(block):
        first, second = block[:HALF_HEAD], block[HALF_HEAD:]
        turned = jnp.concatenate(
            [first * cosine - second * sine, second * cosine + first * sine], axis=0
        )
        return turned.astype(jnp.bfloat16)

    for head in range(head_width // HEAD_DIM):
        at = slice(head * HEAD_DIM, (head + 1) * HEAD_DIM)
        scores = matmul(rotate(key_cols[at]), rotate(queries[at]), TN) * np.float32(HEAD_DIM**-0.5)
        raised = jnp.where(allowed, jnp.exp(scores), 0.0)
        probabilities = (raised / jnp.sum(raised, axis=0, keepdims=True)).astype(jnp.bfloat16)
        context = matmul(values[at], probabilities, (((1,), (0,)), ((), ()))).astype(jnp.bfloat16)
        for copy in range(out_ref.shape[0]):
            out_ref[copy, at, :length] = context
    for copy in range(out_ref.shape[0]):
        out_ref[copy, :, length:] = out_weight


def inner_kernel(hidden_ref, merged_ref, gain_ref, in_ref, after_ref, inner_ref):
    length = hidden_ref.shape[0]
    attended = matmul(merged_ref[:, :length], merged_ref[:, length:], TN)
    after_attn = hidden_ref[...].astype(jnp.float32) + attended
    after_ref[...] = after_attn
    mixed = layer_norm(after_attn, gain_ref[...]).astype(jnp.bfloat16)
    inner_up = matmul(in_ref[0], mixed, NT)
    gate_part = matmul(in_ref[1], mixed, NT)
    activated = (gelu(inner_up) * gate_part).astype(jnp.bfloat16)
    for copy in range(inner_ref.shape[0]):
        inner_ref[copy] = activated


def head_kernel(
    ids_ref, after_ref, inner_ref, *refs
):
    downs, (final_ref, dense_ref, head_ref, out_ref) = refs[:-4], refs[-4:]
    after_ffn = after_ref[...]
    for d, down_ref in enumerate(downs):
        shard = jnp.bitwise_xor(ids_ref[TERM_AT], d)
        after_ffn = after_ffn + matmul(inner_ref[shard], down_ref[...], TN)
    normed = layer_norm(after_ffn, final_ref[...]).astype(jnp.bfloat16)
    dense = matmul(normed, dense_ref[...], (((1,), (0,)), ((), ())))
    out_ref[...] = layer_norm(gelu(dense), head_ref[...]).astype(jnp.bfloat16)


def prep_kernel(ids_ref, segment_ref, list_ref, docs_ref, bounds_ref, mask_ref):
    segments = segment_ref[...]
    slot = lax.broadcasted_iota(jnp.int32, bounds_ref.shape, 1)
    bounds = jnp.zeros(bounds_ref.shape, jnp.int32)
    for passage in range(1, PASS_DEV + 1):
        before = jnp.sum((segments < passage).astype(jnp.int32), axis=1, keepdims=True)
        bounds = jnp.where(slot == passage, before, bounds)
    bounds_ref[...] = bounds
    own_terms, passages = mask_ref.shape
    groups = own_terms // SPAN
    stride = ids_ref[STRIDE_AT]
    blocks = list_ref[...] - ids_ref[BLOCK_AT]
    bits = jnp.zeros(blocks.shape, jnp.float32)
    for group in range(groups):
        bits = jnp.where(blocks == group * stride, np.float32(2**group), bits)
    ones = jnp.ones((SPAN, bits.shape[1]), jnp.bfloat16)
    codes = matmul(ones, bits.astype(jnp.bfloat16), NT).astype(jnp.bfloat16)
    columns = lax.broadcasted_iota(jnp.int32, (passages, passages), 1)
    place = (docs_ref[...] == columns).astype(jnp.float32).astype(jnp.bfloat16)
    placed = matmul(codes, place, (((1,), (0,)), ((), ()))).astype(jnp.int32)
    for group in range(groups):
        held = jnp.bitwise_and(lax.shift_right_logical(placed, group), 1)
        mask_ref[group * SPAN : (group + 1) * SPAN, :] = held.astype(jnp.float32)


def pool_kernel(
    ids_ref, bounds_ref, own_ref, core_ref, far_ref, far_core_ref, table_ref, out_ref, rows_ref, logits_ref
):
    rows = (own_ref, core_ref, far_ref, far_core_ref)
    length = own_ref.shape[0]

    @pl.when(pl.program_id(0) == 0)
    def _():
        for r, row in enumerate(rows):
            rows_ref[r * length : (r + 1) * length, :] = row[...]

    logits_ref[...] = matmul(rows_ref[...], table_ref[...], NT)
    tile = 8
    sublane = lax.broadcasted_iota(jnp.int32, (tile, logits_ref.shape[1]), 0)
    maxima = []
    for r in range(len(rows)):
        for passage in range(PASS_DEV):
            first = bounds_ref[ids_ref[r], passage]
            end = bounds_ref[ids_ref[r], passage + 1]
            first_tile = lax.shift_right_logical(first, 3)
            last_tile = lax.shift_right_logical(end - 1, 3)

            def load(t):
                return logits_ref[pl.ds(pl.multiple_of(r * length + t * tile, tile), tile), :]

            def inside(t):
                token = sublane + t * tile
                return jnp.where((token >= first) & (token < end), load(t), LOWEST)

            held = jnp.maximum(inside(first_tile), inside(last_tile))
            held = lax.fori_loop(
                first_tile + 1, last_tile, lambda t, m: jnp.maximum(m, load(t)), held
            )
            maxima.append(jnp.max(held, axis=0, keepdims=True))
    half = len(maxima) // 2
    low = jnp.concatenate(maxima[:half], axis=0)
    high = jnp.concatenate(maxima[half:], axis=0)
    own_terms = out_ref.shape[2] // 2
    for slot in range(out_ref.shape[0]):
        at = slice(slot * own_terms, (slot + 1) * own_terms)
        to = slot - slot % NEAR + jnp.bitwise_xor(ids_ref[NEAR_AT], slot % NEAR)
        out_ref[to] = jnp.concatenate([low[:, at], high[:, at]], axis=1)


def place_kernel(maxima_ref, bias_ref, mask_ref, docs_ref, out_ref):
    raw = maxima_ref[...] + bias_ref[...]
    weighted = jnp.log1p(jnp.maximum(raw, 0.0))
    own_terms, passages = out_ref.shape
    columns = lax.broadcasted_iota(jnp.int32, (weighted.shape[0], passages), 1)
    terms = []
    rest = weighted
    for _ in range(3):
        terms.append(rest.astype(jnp.bfloat16))
        rest = rest - terms[-1].astype(jnp.float32)
    placed = jnp.zeros((own_terms, passages), jnp.float32)
    for half in range(2):
        place = (docs_ref[half] == columns).astype(jnp.float32).astype(jnp.bfloat16)
        at = slice(half * own_terms, (half + 1) * own_terms)
        sums = [matmul(term, place, TN)[at] for term in terms]
        placed = placed + (sums[0] + sums[1] + sums[2])
    out_ref[...] = placed * mask_ref[...]


def vmem():
    return pl.BlockSpec(memory_space=pltpu.VMEM)


def smem():
    return pl.BlockSpec(memory_space=pltpu.SMEM)


def grant(mib):
    return pltpu.CompilerParams(vmem_limit_bytes=mib << 20)


def cost(flops, nbytes):
    return pl.CostEstimate(flops=flops, bytes_accessed=nbytes, transcendentals=0)


def exchange(copies, axis):
    return lax.all_to_all(copies, axis, split_axis=0, concat_axis=0, tiled=True)


def swap(block, axis, d=1):
    return lax.ppermute(block, axis, [(i, i ^ d) for i in range(lax.axis_size(axis))])


def others(block, axis):
    return [swap(block, axis, d) for d in range(1, lax.axis_size(axis))]


def on_device(
    hidden,
    segment_ids,
    block_lists,
    doc_ids,
    attn_gain,
    qkv_weight,
    attn_out,
    mlp_gain,
    ffn_in,
    ffn_out,
    final_gain,
    head_dense,
    head_gain,
    decoder,
    decoder_bias,
):
    near = ("y", "zh")
    slices = lax.axis_size(near)
    slice_index = lax.axis_index(near)
    near_row = lax.axis_index(("zl", "core"))
    rows_here = lax.axis_size(("zl", "core"))
    row_index = slice_index * rows_here + near_row
    tensor = lax.axis_size("term")
    tokens = hidden[0]
    length, width = tokens.shape
    groups, span = decoder.shape[1], decoder.shape[3]
    own_terms = groups * span
    head_width = qkv_weight.shape[2]
    hidden_units = ffn_in.shape[2]
    passages = block_lists.shape[0]
    near_rows = jnp.stack([jnp.bitwise_xor(near_row, d) for d in range(rows_here)])
    row_ids = slice_index * rows_here + near_rows

    dp_count = slices * rows_here
    first_block = (lax.axis_index("term") * groups * dp_count * span + row_index * span) // BLOCK
    scalars = [
        lax.axis_index("zh"),
        lax.axis_index("term"),
        first_block,
        jnp.int32(dp_count * span // BLOCK),
    ]
    ids = jnp.concatenate([row_ids, jnp.stack(scalars)])

    merged = pl.pallas_call(
        attention_kernel,
        out_shape=jax.ShapeDtypeStruct((tensor, head_width, length + width), jnp.bfloat16),
        in_specs=[smem()] + [vmem()] * 6,
        out_specs=vmem(),
        compiler_params=grant(20),
        cost_estimate=cost(1200000000, 2000000),
        name="attention",
    )(
        ids,
        tokens,
        segment_ids,
        attn_gain[None],
        jnp.swapaxes(qkv_weight, 1, 2),
        jnp.asarray(rotary_table(length)),
        attn_out,
    )
    own_slice = decoder.reshape(own_terms, width)
    own_slice, merged = lax.optimization_barrier((own_slice, merged))
    part = jnp.concatenate([own_slice] + others(own_slice, "zh"), axis=0)
    merged = exchange(merged, "term").reshape(-1, length + width)
    merged, ffn_out = lax.optimization_barrier((merged, ffn_out))
    table = lax.all_gather(part, "y", axis=0, tiled=True)
    after_attn, inner = pl.pallas_call(
        inner_kernel,
        out_shape=(
            jax.ShapeDtypeStruct((length, width), jnp.float32),
            jax.ShapeDtypeStruct((tensor, hidden_units, length), jnp.bfloat16),
        ),
        in_specs=[vmem()] * 4,
        out_specs=(vmem(), vmem()),
        compiler_params=grant(20),
        cost_estimate=cost(600000000, 4000000),
        name="inner",
    )(tokens, merged, mlp_gain[None], jnp.swapaxes(ffn_in, 1, 2))
    downs = [ffn_out] + others(ffn_out, "term")
    bounds, mask = pl.pallas_call(
        prep_kernel,
        out_shape=(
            jax.ShapeDtypeStruct((segment_ids.shape[0], 2 * PASS_DEV), jnp.int32),
            jax.ShapeDtypeStruct((own_terms, passages), jnp.float32),
        ),
        in_specs=[smem()] + [vmem()] * 3,
        out_specs=(vmem(), vmem()),
        compiler_params=grant(20),
        cost_estimate=cost(1000000, 1000000),
        name="prep",
    )(ids, segment_ids, block_lists, doc_ids[:, None])
    all_inner = exchange(inner, "term")
    all_inner, bounds, mask = lax.optimization_barrier((all_inner, bounds, mask))
    headed = pl.pallas_call(
        head_kernel,
        out_shape=jax.ShapeDtypeStruct((length, width), jnp.bfloat16),
        in_specs=[smem()] + [vmem()] * (5 + tensor),
        out_specs=vmem(),
        compiler_params=grant(20),
        cost_estimate=cost(800000000, 5000000),
        name="head",
    )(ids, after_attn, all_inner, *downs, final_gain[None], head_dense, head_gain[None])

    far = swap(headed, "zl")
    core = swap(headed, "core")
    far_core = swap(far, "core")
    terms_here = slices * own_terms
    step = terms_here // 2
    pooled = pl.pallas_call(
        pool_kernel,
        out_shape=jax.ShapeDtypeStruct((slices, 2 * PASS_DEV, 2 * own_terms), jnp.float32),
        grid=(terms_here // step,),
        in_specs=[smem(), smem()]
        + [pl.BlockSpec((length, width), lambda j: (0, 0))] * rows_here
        + [pl.BlockSpec((step, width), lambda j: (j, 0))],
        out_specs=pl.BlockSpec(
            (step // own_terms, 2 * PASS_DEV, 2 * own_terms), lambda j: (j, 0, 0)
        ),
        scratch_shapes=[
            pltpu.VMEM((rows_here * length, width), jnp.bfloat16),
            pltpu.VMEM((rows_here * length, step), jnp.float32),
        ],
        compiler_params=grant(56),
        cost_estimate=cost(3300000000, 6000000),
        name="pool",
    )(ids, bounds, headed, core, far, far_core, table)
    received = exchange(pooled, near)

    bias = decoder_bias.reshape(1, own_terms).astype(jnp.float32)
    docs = doc_ids.reshape(slices, rows_here, PASS_DEV)
    docs = jnp.stack([docs[:, near_rows[d]] for d in range(rows_here)], axis=1)
    docs = jnp.transpose(docs.reshape(slices, 2, 2 * PASS_DEV), (1, 0, 2)).reshape(2, -1, 1)
    placed = pl.pallas_call(
        place_kernel,
        out_shape=jax.ShapeDtypeStruct((own_terms, passages), jnp.float32),
        in_specs=[vmem()] * 4,
        out_specs=vmem(),
        cost_estimate=cost(200000000, 1000000),
        compiler_params=grant(16),
        name="place",
    )(
        received.reshape(-1, 2 * own_terms),
        jnp.concatenate([bias, bias], axis=1),
        mask,
        docs,
    )
    return placed.reshape(1, groups, 1, span, passages)


def solution(mesh):
    shape = (8, 4, 2, 2, mesh.devices.shape[1])
    fine = Mesh(mesh.devices.reshape(shape), ("y", "zh", "zl", "core", "term"))
    dp = ("y", "zh", "zl", "core")
    in_specs = (
        P(dp, None, None),
        P(),
        P(),
        P(),
        P(),
        P(None, None, "term"),
        P("term", None),
        P(),
        P(None, None, "term"),
        P("term", None),
        P(),
        P(),
        P(),
        P("term", None, dp, None, None),
        P("term", None, dp, None),
    )
    out_specs = P("term", None, dp, None, None)
    return jax.shard_map(
        on_device, mesh=fine, in_specs=in_specs, out_specs=out_specs, check_vma=False
    )
```

```python
import functools

import jax
import jax.numpy as jnp
import numpy as np
from jax import lax
from jax.experimental import pallas as pl
from jax.experimental.pallas import tpu as pltpu
from jax.sharding import Mesh
from jax.sharding import PartitionSpec as P

BLOCK = 128
HALF_WIN = 64
PASS_DEV = 4
HEAD_DIM = 64
HALF_HEAD = 32
SPAN = 8
NEAR = 4
LOWEST = -3.0e38
NEAR_AT, TERM_AT, BLOCK_AT, STRIDE_AT = 4, 5, 6, 7

NT = (((1,), (1,)), ((), ()))
TN = (((0,), (0,)), ((), ()))


def rotary_table(length):
    frequency = 10000.0 ** (-2.0 * np.arange(HALF_HEAD, dtype=np.float64) / HEAD_DIM)
    angles = frequency[:, None] * np.arange(length, dtype=np.float64)[None, :]
    terms = []
    for whole in (np.cos(angles), np.sin(angles)):
        rest = whole.astype(np.float32)
        for _ in range(3):
            term = rest.astype(jnp.bfloat16)
            terms.append(term)
            rest = rest - term.astype(np.float32)
    return np.concatenate(terms, axis=0)


def layer_norm(values, gain_row):
    average = jnp.mean(values, axis=-1, keepdims=True)
    centered = values - average
    spread = jnp.mean(centered * centered, axis=-1, keepdims=True)
    return centered * lax.rsqrt(spread + 1e-05) * gain_row


def gelu(values):
    return 0.5 * values * (1.0 + lax.erf(values * np.float32(0.5**0.5)))


def matmul(left, right, dims):
    return lax.dot_general(left, right, dims, preferred_element_type=jnp.float32)


def attention_kernel(
    row_ref, hidden_ref, segment_ref, gain_ref, weight_ref, table_ref, out_weight_ref, out_ref
):
    out_weight = out_weight_ref[...]
    length = hidden_ref.shape[0]
    head_width = weight_ref.shape[1]
    segments = segment_ref[pl.ds(row_ref[0], 1), :]
    starts = jnp.zeros_like(segments)
    for passage in range(PASS_DEV - 1):
        held = jnp.sum((segments == passage).astype(jnp.int32), axis=1, keepdims=True)
        starts = starts + jnp.where(segments > passage, held, 0)
    lane = lax.broadcasted_iota(jnp.int32, (1, length), 1)
    positions = lane - starts
    sublane = lax.broadcasted_iota(jnp.int32, (length, length), 0)
    chosen = (sublane == positions).astype(jnp.float32).astype(jnp.bfloat16)
    parts = matmul(table_ref[...], chosen, (((1,), (0,)), ((), ())))
    part = [parts[i * HALF_HEAD : (i + 1) * HALF_HEAD] for i in range(6)]
    cosine = part[0] + part[1] + part[2]
    sine = part[3] + part[4] + part[5]
    lengths = jnp.zeros_like(segments)
    for passage in range(PASS_DEV):
        held = jnp.sum((segments == passage).astype(jnp.int32), axis=1, keepdims=True)
        lengths = jnp.where(segments == passage, held, lengths)
    low = jnp.maximum(starts, lane - HALF_WIN)
    high = jnp.minimum(starts + lengths - 1, lane + HALF_WIN)
    allowed = (sublane >= low) & (sublane <= high)

    normed = layer_norm(hidden_ref[...].astype(jnp.float32), gain_ref[...]).astype(jnp.bfloat16)
    queries = matmul(weight_ref[0], normed, NT)
    key_cols = matmul(weight_ref[1], normed, NT)
    values = matmul(weight_ref[2], normed, NT).astype(jnp.bfloat16)

    def rotate(block):
        first, second = block[:HALF_HEAD], block[HALF_HEAD:]
        turned = jnp.concatenate(
            [first * cosine - second * sine, second * cosine + first * sine], axis=0
        )
        return turned.astype(jnp.bfloat16)

    for head in range(head_width // HEAD_DIM):
        at = slice(head * HEAD_DIM, (head + 1) * HEAD_DIM)
        scores = matmul(rotate(key_cols[at]), rotate(queries[at]), TN) * np.float32(HEAD_DIM**-0.5)
        raised = jnp.where(allowed, jnp.exp(scores), 0.0)
        probabilities = (raised / jnp.sum(raised, axis=0, keepdims=True)).astype(jnp.bfloat16)
        context = matmul(values[at], probabilities, (((1,), (0,)), ((), ()))).astype(jnp.bfloat16)
        for copy in range(out_ref.shape[0]):
            out_ref[copy, at, :length] = context
    for copy in range(out_ref.shape[0]):
        out_ref[copy, :, length:] = out_weight


def ffn_kernel(hidden_ref, merged_ref, gain_ref, in_ref, down_ref, after_ref, out_ref):
    length = hidden_ref.shape[0]
    attended = matmul(merged_ref[:, :length], merged_ref[:, length:], TN)
    after_attn = hidden_ref[...].astype(jnp.float32) + attended
    after_ref[...] = after_attn
    mixed = layer_norm(after_attn, gain_ref[...]).astype(jnp.bfloat16)
    inner_up = matmul(in_ref[0], mixed, NT)
    gate_part = matmul(in_ref[1], mixed, NT)
    activated = (gelu(inner_up) * gate_part).astype(jnp.bfloat16)
    partial = matmul(activated, down_ref[...], TN).astype(jnp.bfloat16)
    for copy in range(out_ref.shape[0]):
        out_ref[copy] = partial


def head_kernel(after_ref, partial_ref, final_ref, dense_ref, head_ref, out_ref):
    after_ffn = after_ref[...]
    for shard in range(partial_ref.shape[0]):
        after_ffn = after_ffn + partial_ref[shard].astype(jnp.float32)
    normed = layer_norm(after_ffn, final_ref[...]).astype(jnp.bfloat16)
    dense = matmul(normed, dense_ref[...], (((1,), (0,)), ((), ())))
    out_ref[...] = layer_norm(gelu(dense), head_ref[...]).astype(jnp.bfloat16)


def prep_kernel(ids_ref, segment_ref, list_ref, docs_ref, bounds_ref, mask_ref):
    segments = segment_ref[...]
    slot = lax.broadcasted_iota(jnp.int32, bounds_ref.shape, 1)
    bounds = jnp.zeros(bounds_ref.shape, jnp.int32)
    for passage in range(1, PASS_DEV + 1):
        before = jnp.sum((segments < passage).astype(jnp.int32), axis=1, keepdims=True)
        bounds = jnp.where(slot == passage, before, bounds)
    bounds_ref[...] = bounds
    own_terms, passages = mask_ref.shape
    groups = own_terms // SPAN
    stride = ids_ref[STRIDE_AT]
    blocks = list_ref[...] - ids_ref[BLOCK_AT]
    bits = jnp.zeros(blocks.shape, jnp.float32)
    for group in range(groups):
        bits = jnp.where(blocks == group * stride, np.float32(2**group), bits)
    ones = jnp.ones((SPAN, bits.shape[1]), jnp.bfloat16)
    codes = matmul(ones, bits.astype(jnp.bfloat16), NT).astype(jnp.bfloat16)
    columns = lax.broadcasted_iota(jnp.int32, (passages, passages), 1)
    place = (docs_ref[...] == columns).astype(jnp.float32).astype(jnp.bfloat16)
    placed = matmul(codes, place, (((1,), (0,)), ((), ()))).astype(jnp.int32)
    for group in range(groups):
        held = jnp.bitwise_and(lax.shift_right_logical(placed, group), 1)
        mask_ref[group * SPAN : (group + 1) * SPAN, :] = held.astype(jnp.float32)


def pool_kernel(
    ids_ref, bounds_ref, own_ref, core_ref, far_ref, far_core_ref, table_ref, out_ref, rows_ref, logits_ref
):
    rows = (own_ref, core_ref, far_ref, far_core_ref)
    length = own_ref.shape[0]

    @pl.when(pl.program_id(0) == 0)
    def _():
        for r, row in enumerate(rows):
            rows_ref[r * length : (r + 1) * length, :] = row[...]

    logits_ref[...] = matmul(rows_ref[...], table_ref[...], NT)
    tile = 8
    sublane = lax.broadcasted_iota(jnp.int32, (tile, logits_ref.shape[1]), 0)
    maxima = []
    for r in range(len(rows)):
        for passage in range(PASS_DEV):
            first = bounds_ref[ids_ref[r], passage]
            end = bounds_ref[ids_ref[r], passage + 1]
            first_tile = lax.shift_right_logical(first, 3)
            last_tile = lax.shift_right_logical(end - 1, 3)

            def load(t):
                return logits_ref[pl.ds(pl.multiple_of(r * length + t * tile, tile), tile), :]

            def inside(t):
                token = sublane + t * tile
                return jnp.where((token >= first) & (token < end), load(t), LOWEST)

            held = jnp.maximum(inside(first_tile), inside(last_tile))
            held = lax.fori_loop(
                first_tile + 1, last_tile, lambda t, m: jnp.maximum(m, load(t)), held
            )
            maxima.append(jnp.max(held, axis=0, keepdims=True))
    half = len(maxima) // 2
    low = jnp.concatenate(maxima[:half], axis=0)
    high = jnp.concatenate(maxima[half:], axis=0)
    own_terms = out_ref.shape[2] // 2
    for slot in range(out_ref.shape[0]):
        at = slice(slot * own_terms, (slot + 1) * own_terms)
        to = slot - slot % NEAR + jnp.bitwise_xor(ids_ref[NEAR_AT], slot % NEAR)
        out_ref[to] = jnp.concatenate([low[:, at], high[:, at]], axis=1)


def place_kernel(maxima_ref, bias_ref, mask_ref, docs_ref, out_ref):
    raw = maxima_ref[...] + bias_ref[...]
    weighted = jnp.log1p(jnp.maximum(raw, 0.0))
    own_terms, passages = out_ref.shape
    columns = lax.broadcasted_iota(jnp.int32, (weighted.shape[0], passages), 1)
    terms = []
    rest = weighted
    for _ in range(3):
        terms.append(rest.astype(jnp.bfloat16))
        rest = rest - terms[-1].astype(jnp.float32)
    placed = jnp.zeros((own_terms, passages), jnp.float32)
    for half in range(2):
        place = (docs_ref[half] == columns).astype(jnp.float32).astype(jnp.bfloat16)
        at = slice(half * own_terms, (half + 1) * own_terms)
        sums = [matmul(term, place, TN)[at] for term in terms]
        placed = placed + (sums[0] + sums[1] + sums[2])
    out_ref[...] = placed * mask_ref[...]


def vmem():
    return pl.BlockSpec(memory_space=pltpu.VMEM)


def smem():
    return pl.BlockSpec(memory_space=pltpu.SMEM)


def grant(mib):
    return pltpu.CompilerParams(vmem_limit_bytes=mib << 20)


def cost(flops, nbytes):
    return pl.CostEstimate(flops=flops, bytes_accessed=nbytes, transcendentals=0)


def exchange(copies, axis):
    return lax.all_to_all(copies, axis, split_axis=0, concat_axis=0, tiled=True)


def swap(block, axis, d=1):
    return lax.ppermute(block, axis, [(i, i ^ d) for i in range(lax.axis_size(axis))])


def others(block, axis):
    return [swap(block, axis, d) for d in range(1, lax.axis_size(axis))]


def on_device(
    hidden,
    segment_ids,
    block_lists,
    doc_ids,
    attn_gain,
    qkv_weight,
    attn_out,
    mlp_gain,
    ffn_in,
    ffn_out,
    final_gain,
    head_dense,
    head_gain,
    decoder,
    decoder_bias,
):
    near = ("y", "zh")
    slices = lax.axis_size(near)
    slice_index = lax.axis_index(near)
    near_row = lax.axis_index(("zl", "core"))
    rows_here = lax.axis_size(("zl", "core"))
    row_index = slice_index * rows_here + near_row
    tensor = lax.axis_size("term")
    tokens = hidden[0]
    length, width = tokens.shape
    groups, span = decoder.shape[1], decoder.shape[3]
    own_terms = groups * span
    head_width = qkv_weight.shape[2]
    passages = block_lists.shape[0]
    near_rows = jnp.stack([jnp.bitwise_xor(near_row, d) for d in range(rows_here)])
    row_ids = slice_index * rows_here + near_rows

    dp_count = slices * rows_here
    first_block = (lax.axis_index("term") * groups * dp_count * span + row_index * span) // BLOCK
    scalars = [
        lax.axis_index("zh"),
        lax.axis_index("term"),
        first_block,
        jnp.int32(dp_count * span // BLOCK),
    ]
    ids = jnp.concatenate([row_ids, jnp.stack(scalars)])

    merged = pl.pallas_call(
        attention_kernel,
        out_shape=jax.ShapeDtypeStruct((tensor, head_width, length + width), jnp.bfloat16),
        in_specs=[smem()] + [vmem()] * 6,
        out_specs=vmem(),
        compiler_params=grant(20),
        cost_estimate=cost(1200000000, 2000000),
        name="attention",
    )(
        ids,
        tokens,
        segment_ids,
        attn_gain[None],
        jnp.swapaxes(qkv_weight, 1, 2),
        jnp.asarray(rotary_table(length)),
        attn_out,
    )
    own_slice = decoder.reshape(own_terms, width)
    pieces = others(own_slice, "zh")
    pieces, merged = lax.optimization_barrier((pieces, merged))
    part = jnp.concatenate([own_slice] + pieces, axis=0)
    merged = exchange(merged, "term").reshape(-1, length + width)
    table = lax.all_gather(part, "y", axis=0, tiled=True)
    after_attn, partial = pl.pallas_call(
        ffn_kernel,
        out_shape=(
            jax.ShapeDtypeStruct((length, width), jnp.float32),
            jax.ShapeDtypeStruct((tensor, length, width), jnp.bfloat16),
        ),
        in_specs=[vmem()] * 5,
        out_specs=(vmem(), vmem()),
        compiler_params=grant(20),
        cost_estimate=cost(700000000, 4000000),
        name="ffn",
    )(tokens, merged, mlp_gain[None], jnp.swapaxes(ffn_in, 1, 2), ffn_out)
    bounds, mask = pl.pallas_call(
        prep_kernel,
        out_shape=(
            jax.ShapeDtypeStruct((segment_ids.shape[0], 2 * PASS_DEV), jnp.int32),
            jax.ShapeDtypeStruct((own_terms, passages), jnp.float32),
        ),
        in_specs=[smem()] + [vmem()] * 3,
        out_specs=(vmem(), vmem()),
        compiler_params=grant(20),
        cost_estimate=cost(1000000, 1000000),
        name="prep",
    )(ids, segment_ids, block_lists, doc_ids[:, None])
    partials = exchange(partial, "term")
    partials, bounds, mask = lax.optimization_barrier((partials, bounds, mask))
    headed = pl.pallas_call(
        head_kernel,
        out_shape=jax.ShapeDtypeStruct((length, width), jnp.bfloat16),
        in_specs=[vmem()] * 5,
        out_specs=vmem(),
        compiler_params=grant(20),
        cost_estimate=cost(800000000, 5000000),
        name="head",
    )(after_attn, partials, final_gain[None], head_dense, head_gain[None])

    far = swap(headed, "zl")
    core = swap(headed, "core")
    far_core = swap(far, "core")
    terms_here = slices * own_terms
    step = terms_here // 2
    pooled = pl.pallas_call(
        pool_kernel,
        out_shape=jax.ShapeDtypeStruct((slices, 2 * PASS_DEV, 2 * own_terms), jnp.float32),
        grid=(terms_here // step,),
        in_specs=[smem(), smem()]
        + [pl.BlockSpec((length, width), lambda j: (0, 0))] * rows_here
        + [pl.BlockSpec((step, width), lambda j: (j, 0))],
        out_specs=pl.BlockSpec(
            (step // own_terms, 2 * PASS_DEV, 2 * own_terms), lambda j: (j, 0, 0)
        ),
        scratch_shapes=[
            pltpu.VMEM((rows_here * length, width), jnp.bfloat16),
            pltpu.VMEM((rows_here * length, step), jnp.float32),
        ],
        compiler_params=grant(56),
        cost_estimate=cost(3300000000, 6000000),
        name="pool",
    )(ids, bounds, headed, core, far, far_core, table)
    received = exchange(pooled, near)

    bias = decoder_bias.reshape(1, own_terms).astype(jnp.float32)
    docs = doc_ids.reshape(slices, rows_here, PASS_DEV)
    docs = jnp.stack([docs[:, near_rows[d]] for d in range(rows_here)], axis=1)
    docs = jnp.transpose(docs.reshape(slices, 2, 2 * PASS_DEV), (1, 0, 2)).reshape(2, -1, 1)
    placed = pl.pallas_call(
        place_kernel,
        out_shape=jax.ShapeDtypeStruct((own_terms, passages), jnp.float32),
        in_specs=[vmem()] * 4,
        out_specs=vmem(),
        cost_estimate=cost(200000000, 1000000),
        compiler_params=grant(16),
        name="place",
    )(
        received.reshape(-1, 2 * own_terms),
        jnp.concatenate([bias, bias], axis=1),
        mask,
        docs,
    )
    return placed.reshape(1, groups, 1, span, passages)


def solution(mesh):
    shape = (8, 4, 2, 2, mesh.devices.shape[1])
    fine = Mesh(mesh.devices.reshape(shape), ("y", "zh", "zl", "core", "term"))
    dp = ("y", "zh", "zl", "core")
    in_specs = (
        P(dp, None, None),
        P(),
        P(),
        P(),
        P(),
        P(None, None, "term"),
        P("term", None),
        P(),
        P(None, None, "term"),
        P("term", None),
        P(),
        P(),
        P(),
        P("term", None, dp, None, None),
        P("term", None, dp, None),
    )
    out_specs = P("term", None, dp, None, None)
    return jax.shard_map(
        on_device, mesh=fine, in_specs=in_specs, out_specs=out_specs, check_vma=False
    )
```

```python
import functools

import jax
import jax.numpy as jnp
import numpy as np
from jax import lax
from jax.experimental import pallas as pl
from jax.experimental.pallas import tpu as pltpu
from jax.sharding import Mesh
from jax.sharding import PartitionSpec as P

BLOCK = 128
HALF_WIN = 64
PASS_DEV = 4
HEAD_DIM = 64
HALF_HEAD = 32
SPAN = 8
LOWEST = -3.0e38
TERM_AT, BLOCK_AT, STRIDE_AT, CORE_AT = 4, 5, 6, 7

NT = (((1,), (1,)), ((), ()))
TN = (((0,), (0,)), ((), ()))


def rotary_table(length):
    frequency = 10000.0 ** (-2.0 * np.arange(HALF_HEAD, dtype=np.float64) / HEAD_DIM)
    angles = frequency[:, None] * np.arange(length, dtype=np.float64)[None, :]
    terms = []
    for whole in (np.cos(angles), np.sin(angles)):
        rest = whole.astype(np.float32)
        for _ in range(3):
            term = rest.astype(jnp.bfloat16)
            terms.append(term)
            rest = rest - term.astype(np.float32)
    return np.concatenate(terms, axis=0)


def layer_norm(values, gain_row):
    average = jnp.mean(values, axis=-1, keepdims=True)
    centered = values - average
    spread = jnp.mean(centered * centered, axis=-1, keepdims=True)
    return centered * lax.rsqrt(spread + 1e-05) * gain_row


def gelu(values):
    return 0.5 * values * (1.0 + lax.erf(values * np.float32(0.5**0.5)))


def matmul(left, right, dims):
    return lax.dot_general(left, right, dims, preferred_element_type=jnp.float32)


def attention_kernel(
    ids_ref,
    gain_ref,
    hidden_hbm,
    segment_hbm,
    weight_hbm,
    table_hbm,
    out_ref,
    hidden_ref,
    segment_ref,
    weight_ref,
    table_ref,
    sems,
):
    length = hidden_ref.shape[0]
    row = ids_ref[0]
    tile = pl.multiple_of(lax.shift_left(lax.shift_right_logical(row, 3), 3), 8)
    copies = [
        pltpu.make_async_copy(hidden_hbm, hidden_ref, sems.at[0]),
        pltpu.make_async_copy(segment_hbm.at[pl.ds(tile, 8), :], segment_ref, sems.at[1]),
        pltpu.make_async_copy(table_hbm, table_ref, sems.at[2]),
    ] + [
        pltpu.make_async_copy(weight_hbm.at[slot], weight_ref.at[slot], sems.at[3 + slot])
        for slot in range(3)
    ]
    for copy in copies:
        copy.start()
    copies[1].wait()
    head_width = weight_ref.shape[1]
    segments = segment_ref[pl.ds(row - tile, 1), :]
    starts = jnp.zeros_like(segments)
    for passage in range(PASS_DEV - 1):
        held = jnp.sum((segments == passage).astype(jnp.int32), axis=1, keepdims=True)
        starts = starts + jnp.where(segments > passage, held, 0)
    lane = lax.broadcasted_iota(jnp.int32, (1, length), 1)
    positions = lane - starts
    sublane = lax.broadcasted_iota(jnp.int32, (length, length), 0)
    copies[2].wait()
    chosen = (sublane == positions).astype(jnp.float32).astype(jnp.bfloat16)
    parts = matmul(table_ref[...], chosen, (((1,), (0,)), ((), ())))
    part = [parts[i * HALF_HEAD : (i + 1) * HALF_HEAD] for i in range(6)]
    cosine = part[0] + part[1] + part[2]
    sine = part[3] + part[4] + part[5]
    lengths = jnp.zeros_like(segments)
    for passage in range(PASS_DEV):
        held = jnp.sum((segments == passage).astype(jnp.int32), axis=1, keepdims=True)
        lengths = jnp.where(segments == passage, held, lengths)
    low = jnp.maximum(starts, lane - HALF_WIN)
    high = jnp.minimum(starts + lengths - 1, lane + HALF_WIN)
    allowed = (sublane >= low) & (sublane <= high)

    copies[0].wait()
    normed = layer_norm(hidden_ref[...].astype(jnp.float32), gain_ref[...]).astype(jnp.bfloat16)
    for copy in copies[3:]:
        copy.wait()
    queries = matmul(weight_ref[0], normed, NT)
    key_cols = matmul(weight_ref[1], normed, NT)
    values = matmul(weight_ref[2], normed, NT).astype(jnp.bfloat16)

    def rotate(block):
        first, second = block[:HALF_HEAD], block[HALF_HEAD:]
        turned = jnp.concatenate(
            [first * cosine - second * sine, second * cosine + first * sine], axis=0
        )
        return turned.astype(jnp.bfloat16)

    for head in range(head_width // HEAD_DIM):
        at = slice(head * HEAD_DIM, (head + 1) * HEAD_DIM)
        scores = matmul(rotate(key_cols[at]), rotate(queries[at]), TN) * np.float32(HEAD_DIM**-0.5)
        raised = jnp.where(allowed, jnp.exp(scores), 0.0)
        probabilities = (raised / jnp.sum(raised, axis=0, keepdims=True)).astype(jnp.bfloat16)
        context = matmul(values[at], probabilities, (((1,), (0,)), ((), ()))).astype(jnp.bfloat16)
        for copy in range(out_ref.shape[0]):
            out_ref[copy, at, :] = context


def ffn_kernel(
    ids_ref,
    hidden_ref,
    context_ref,
    gain_ref,
    in_ref,
    down_ref,
    own_weight_ref,
    mine_ref,
    other_ref,
    after_ref,
    out_ref,
):
    own = ids_ref[TERM_AT]
    after_attn = hidden_ref[...].astype(jnp.float32)
    after_attn = after_attn + matmul(context_ref[own], own_weight_ref[...], TN)
    half = own_weight_ref.shape[0] // 2
    for d in range(1, context_ref.shape[0]):
        shard = jnp.bitwise_xor(own, d)
        at = slice((d - 1) * half, d * half)
        for core, ref in ((ids_ref[CORE_AT], mine_ref), (1 - ids_ref[CORE_AT], other_ref)):
            first = pl.multiple_of(core * half, half)
            context = context_ref[shard, pl.ds(first, half), :]
            after_attn = after_attn + matmul(context, ref[at, :], TN)
    after_ref[...] = after_attn
    mixed = layer_norm(after_attn, gain_ref[...]).astype(jnp.bfloat16)
    inner_up = matmul(in_ref[0], mixed, NT)
    gate_part = matmul(in_ref[1], mixed, NT)
    activated = (gelu(inner_up) * gate_part).astype(jnp.bfloat16)
    partial = matmul(activated, down_ref[...], TN).astype(jnp.bfloat16)
    for copy in range(out_ref.shape[0]):
        out_ref[copy] = partial


def head_kernel(after_ref, partial_ref, final_ref, dense_ref, head_ref, out_ref):
    after_ffn = after_ref[...]
    for shard in range(partial_ref.shape[0]):
        after_ffn = after_ffn + partial_ref[shard].astype(jnp.float32)
    normed = layer_norm(after_ffn, final_ref[...]).astype(jnp.bfloat16)
    dense = matmul(normed, dense_ref[...], (((1,), (0,)), ((), ())))
    out_ref[...] = layer_norm(gelu(dense), head_ref[...]).astype(jnp.bfloat16)


def prep_kernel(ids_ref, segment_ref, list_ref, docs_ref, bounds_ref, mask_ref):
    segments = segment_ref[...]
    slot = lax.broadcasted_iota(jnp.int32, bounds_ref.shape, 1)
    bounds = jnp.zeros(bounds_ref.shape, jnp.int32)
    for passage in range(1, PASS_DEV + 1):
        before = jnp.sum((segments < passage).astype(jnp.int32), axis=1, keepdims=True)
        bounds = jnp.where(slot == passage, before, bounds)
    bounds_ref[...] = bounds
    own_terms, passages = mask_ref.shape
    groups = own_terms // SPAN
    stride = ids_ref[STRIDE_AT]
    blocks = list_ref[...] - ids_ref[BLOCK_AT]
    bits = jnp.zeros(blocks.shape, jnp.float32)
    for group in range(groups):
        bits = jnp.where(blocks == group * stride, np.float32(2**group), bits)
    ones = jnp.ones((SPAN, bits.shape[1]), jnp.bfloat16)
    codes = matmul(ones, bits.astype(jnp.bfloat16), NT).astype(jnp.bfloat16)
    columns = lax.broadcasted_iota(jnp.int32, (passages, passages), 1)
    place = (docs_ref[...] == columns).astype(jnp.float32).astype(jnp.bfloat16)
    placed = matmul(codes, place, (((1,), (0,)), ((), ()))).astype(jnp.int32)
    for group in range(groups):
        held = jnp.bitwise_and(lax.shift_right_logical(placed, group), 1)
        mask_ref[group * SPAN : (group + 1) * SPAN, :] = held.astype(jnp.float32)


def passage_maxima(ids_ref, bounds_ref, first_row, rows, table_ref, logits_ref):
    length = rows[0].shape[0]
    stacked = jnp.concatenate([row[...] for row in rows], axis=0)
    logits_ref[...] = matmul(stacked, table_ref[...], NT)
    tile = 8
    sublane = lax.broadcasted_iota(jnp.int32, (tile, logits_ref.shape[1]), 0)
    maxima = []
    for r in range(len(rows)):
        row = ids_ref[first_row + r]
        for passage in range(PASS_DEV):
            first = bounds_ref[row, passage]
            end = bounds_ref[row, passage + 1]
            first_tile = lax.shift_right_logical(first, 3)
            last_tile = lax.shift_right_logical(end - 1, 3)

            def load(t):
                return logits_ref[pl.ds(pl.multiple_of(r * length + t * tile, tile), tile), :]

            def inside(t):
                token = sublane + t * tile
                return jnp.where((token >= first) & (token < end), load(t), LOWEST)

            held = jnp.maximum(inside(first_tile), inside(last_tile))
            held = lax.fori_loop(
                first_tile + 1, last_tile, lambda t, m: jnp.maximum(m, load(t)), held
            )
            maxima.append(jnp.max(held, axis=0, keepdims=True))
    return jnp.concatenate(maxima, axis=0)


def near_pool_kernel(ids_ref, bounds_ref, own_ref, core_ref, table_ref, low_ref, logits_ref):
    rows = (own_ref, core_ref)
    low_ref[...] = passage_maxima(ids_ref, bounds_ref, 0, rows, table_ref, logits_ref)


def far_pool_kernel(
    ids_ref, bounds_ref, far_ref, far_core_ref, table_ref, low_ref, out_ref, logits_ref
):
    rows = (far_ref, far_core_ref)
    high = passage_maxima(ids_ref, bounds_ref, len(rows), rows, table_ref, logits_ref)
    low = low_ref[...]
    own_terms = out_ref.shape[2] // 2
    for slot in range(out_ref.shape[0]):
        at = slice(slot * own_terms, (slot + 1) * own_terms)
        out_ref[slot] = jnp.concatenate([low[:, at], high[:, at]], axis=1)


def place_kernel(maxima_ref, bias_ref, mask_ref, docs_ref, out_ref):
    raw = maxima_ref[...] + bias_ref[...]
    weighted = jnp.log1p(jnp.maximum(raw, 0.0))
    own_terms, passages = out_ref.shape
    columns = lax.broadcasted_iota(jnp.int32, (weighted.shape[0], passages), 1)
    terms = []
    rest = weighted
    for _ in range(3):
        terms.append(rest.astype(jnp.bfloat16))
        rest = rest - terms[-1].astype(jnp.float32)
    placed = jnp.zeros((own_terms, passages), jnp.float32)
    for half in range(2):
        place = (docs_ref[half] == columns).astype(jnp.float32).astype(jnp.bfloat16)
        at = slice(half * own_terms, (half + 1) * own_terms)
        sums = [matmul(term, place, TN)[at] for term in terms]
        placed = placed + (sums[0] + sums[1] + sums[2])
    out_ref[...] = placed * mask_ref[...]


def vmem():
    return pl.BlockSpec(memory_space=pltpu.VMEM)


def hbm():
    return pl.BlockSpec(memory_space=pltpu.HBM)


def smem():
    return pl.BlockSpec(memory_space=pltpu.SMEM)


def grant(mib):
    return pltpu.CompilerParams(vmem_limit_bytes=mib << 20)


def cost(flops, nbytes):
    return pl.CostEstimate(flops=flops, bytes_accessed=nbytes, transcendentals=0)


def exchange(copies, axis):
    return lax.all_to_all(copies, axis, split_axis=0, concat_axis=0, tiled=True)


def gather_by_exchange(block, axis):
    return exchange(jnp.broadcast_to(block[None], (lax.axis_size(axis),) + block.shape), axis)


def swap(block, axis, d=1):
    return lax.ppermute(block, axis, [(i, i ^ d) for i in range(lax.axis_size(axis))])


def others(block, axis):
    return [swap(block, axis, d) for d in range(1, lax.axis_size(axis))]


def on_device(
    hidden,
    segment_ids,
    block_lists,
    doc_ids,
    attn_gain,
    qkv_weight,
    attn_out,
    mlp_gain,
    ffn_in,
    ffn_out,
    final_gain,
    head_dense,
    head_gain,
    decoder,
    decoder_bias,
):
    near = ("y", "zh")
    slices = lax.axis_size(near)
    slice_index = lax.axis_index(near)
    near_row = lax.axis_index(("zl", "core"))
    rows_here = lax.axis_size(("zl", "core"))
    row_index = slice_index * rows_here + near_row
    tensor = lax.axis_size("term")
    tokens = hidden[0]
    length, width = tokens.shape
    groups, span = decoder.shape[1], decoder.shape[3]
    own_terms = groups * span
    head_width = qkv_weight.shape[2]
    passages = block_lists.shape[0]
    near_rows = jnp.stack([jnp.bitwise_xor(near_row, d) for d in range(rows_here)])
    row_ids = slice_index * rows_here + near_rows

    dp_count = slices * rows_here
    first_block = (lax.axis_index("term") * groups * dp_count * span + row_index * span) // BLOCK
    scalars = [
        lax.axis_index("term"),
        first_block,
        jnp.int32(dp_count * span // BLOCK),
        lax.axis_index("core"),
    ]
    ids = jnp.concatenate([row_ids, jnp.stack(scalars)])

    own_slice = decoder.reshape(own_terms, width)
    part = gather_by_exchange(own_slice, "zh").reshape(-1, width)
    half = head_width // 2
    own_half = lax.dynamic_slice_in_dim(attn_out, lax.axis_index("core") * half, half, 0)
    pieces = others(own_half, "term")
    rotary = jnp.asarray(rotary_table(length))
    context = pl.pallas_call(
        attention_kernel,
        out_shape=jax.ShapeDtypeStruct((tensor, head_width, length), jnp.bfloat16),
        in_specs=[smem(), vmem()] + [hbm()] * 4,
        out_specs=vmem(),
        scratch_shapes=[
            pltpu.VMEM((length, width), jnp.bfloat16),
            pltpu.VMEM((8, length), jnp.int32),
            pltpu.VMEM((3, head_width, width), jnp.bfloat16),
            pltpu.VMEM(rotary.shape, jnp.bfloat16),
            pltpu.SemaphoreType.DMA((6,)),
        ],
        compiler_params=grant(60),
        cost_estimate=cost(1200000000, 2000000),
        name="attention",
    )(ids, attn_gain[None], tokens, segment_ids, jnp.swapaxes(qkv_weight, 1, 2), rotary)
    part, pieces, context = lax.optimization_barrier((part, pieces, context))
    mine = jnp.concatenate(pieces, axis=0)
    other = swap(mine, "core")
    table = lax.all_gather(part, "y", axis=0, tiled=True)
    all_context = exchange(context, "term")
    after_attn, partial = pl.pallas_call(
        ffn_kernel,
        out_shape=(
            jax.ShapeDtypeStruct((length, width), jnp.float32),
            jax.ShapeDtypeStruct((tensor, length, width), jnp.bfloat16),
        ),
        in_specs=[smem()] + [vmem()] * 8,
        out_specs=(vmem(), vmem()),
        compiler_params=grant(20),
        cost_estimate=cost(700000000, 4000000),
        name="ffn",
    )(
        ids,
        tokens,
        all_context,
        mlp_gain[None],
        jnp.swapaxes(ffn_in, 1, 2),
        ffn_out,
        attn_out,
        mine,
        other,
    )
    bounds, mask = pl.pallas_call(
        prep_kernel,
        out_shape=(
            jax.ShapeDtypeStruct((segment_ids.shape[0], 2 * PASS_DEV), jnp.int32),
            jax.ShapeDtypeStruct((own_terms, passages), jnp.float32),
        ),
        in_specs=[smem()] + [vmem()] * 3,
        out_specs=(vmem(), vmem()),
        compiler_params=grant(20),
        cost_estimate=cost(1000000, 1000000),
        name="prep",
    )(ids, segment_ids, block_lists, doc_ids[:, None])
    partials = exchange(partial, "term")
    partials, bounds, mask = lax.optimization_barrier((partials, bounds, mask))
    headed = pl.pallas_call(
        head_kernel,
        out_shape=jax.ShapeDtypeStruct((length, width), jnp.bfloat16),
        in_specs=[vmem()] * 5,
        out_specs=vmem(),
        compiler_params=grant(20),
        cost_estimate=cost(800000000, 5000000),
        name="head",
    )(after_attn, partials, final_gain[None], head_dense, head_gain[None])

    far = swap(headed, "zl")
    core = swap(headed, "core")
    far_core = swap(far, "core")
    terms_here = slices * own_terms
    logits = pltpu.VMEM((2 * length, terms_here), jnp.float32)
    low = pl.pallas_call(
        near_pool_kernel,
        out_shape=jax.ShapeDtypeStruct((2 * PASS_DEV, terms_here), jnp.float32),
        in_specs=[smem(), smem()] + [vmem()] * 3,
        out_specs=vmem(),
        scratch_shapes=[logits],
        compiler_params=grant(20),
        cost_estimate=cost(1600000000, 4000000),
        name="near_pool",
    )(ids, bounds, headed, core, table)
    pooled = pl.pallas_call(
        far_pool_kernel,
        out_shape=jax.ShapeDtypeStruct((slices, 2 * PASS_DEV, 2 * own_terms), jnp.float32),
        in_specs=[smem(), smem()] + [vmem()] * 4,
        out_specs=vmem(),
        scratch_shapes=[logits],
        compiler_params=grant(20),
        cost_estimate=cost(1600000000, 4000000),
        name="far_pool",
    )(ids, bounds, far, far_core, table, low)
    received = exchange(pooled, near)

    bias = decoder_bias.reshape(1, own_terms).astype(jnp.float32)
    docs = doc_ids.reshape(slices, rows_here, PASS_DEV)
    docs = jnp.stack([docs[:, near_rows[d]] for d in range(rows_here)], axis=1)
    docs = jnp.transpose(docs.reshape(slices, 2, 2 * PASS_DEV), (1, 0, 2)).reshape(2, -1, 1)
    placed = pl.pallas_call(
        place_kernel,
        out_shape=jax.ShapeDtypeStruct((own_terms, passages), jnp.float32),
        in_specs=[vmem()] * 4,
        out_specs=vmem(),
        cost_estimate=cost(200000000, 1000000),
        compiler_params=grant(16),
        name="place",
    )(
        received.reshape(-1, 2 * own_terms),
        jnp.concatenate([bias, bias], axis=1),
        mask,
        docs,
    )
    return placed.reshape(1, groups, 1, span, passages)


def solution(mesh):
    shape = (8, 4, 2, 2, mesh.devices.shape[1])
    fine = Mesh(mesh.devices.reshape(shape), ("y", "zh", "zl", "core", "term"))
    dp = ("y", "zh", "zl", "core")
    in_specs = (
        P(dp, None, None),
        P(),
        P(),
        P(),
        P(),
        P(None, None, "term"),
        P("term", None),
        P(),
        P(None, None, "term"),
        P("term", None),
        P(),
        P(),
        P(),
        P("term", None, dp, None, None),
        P("term", None, dp, None),
    )
    out_specs = P("term", None, dp, None, None)
    return jax.shard_map(
        on_device, mesh=fine, in_specs=in_specs, out_specs=out_specs, check_vma=False
    )
```

```python
import functools

import jax
import jax.numpy as jnp
import numpy as np
from jax import lax
from jax.experimental import pallas as pl
from jax.experimental.pallas import tpu as pltpu
from jax.sharding import Mesh
from jax.sharding import PartitionSpec as P

BLOCK = 128
HALF_WIN = 64
PASS_DEV = 4
HEAD_DIM = 64
HALF_HEAD = 32
SPAN = 8
LOWEST = -3.0e38
TERM_AT, BLOCK_AT, STRIDE_AT, CORE_AT = 4, 5, 6, 7

NT = (((1,), (1,)), ((), ()))
TN = (((0,), (0,)), ((), ()))


def rotary_table(length):
    frequency = 10000.0 ** (-2.0 * np.arange(HALF_HEAD, dtype=np.float64) / HEAD_DIM)
    angles = frequency[:, None] * np.arange(length, dtype=np.float64)[None, :]
    terms = []
    for whole in (np.cos(angles), np.sin(angles)):
        rest = whole.astype(np.float32)
        for _ in range(3):
            term = rest.astype(jnp.bfloat16)
            terms.append(term)
            rest = rest - term.astype(np.float32)
    return np.concatenate(terms, axis=0)


def layer_norm(values, gain_row):
    average = jnp.mean(values, axis=-1, keepdims=True)
    centered = values - average
    spread = jnp.mean(centered * centered, axis=-1, keepdims=True)
    return centered * lax.rsqrt(spread + 1e-05) * gain_row


def gelu(values):
    return 0.5 * values * (1.0 + lax.erf(values * np.float32(0.5**0.5)))


def matmul(left, right, dims):
    return lax.dot_general(left, right, dims, preferred_element_type=jnp.float32)


def attention_kernel(
    ids_ref,
    gain_ref,
    hidden_hbm,
    segment_hbm,
    weight_hbm,
    table_hbm,
    out_weight_hbm,
    out_ref,
    hidden_ref,
    segment_ref,
    weight_ref,
    table_ref,
    half_ref,
    sems,
):
    length = hidden_ref.shape[0]
    row = ids_ref[0]
    tile = pl.multiple_of(lax.shift_left(lax.shift_right_logical(row, 3), 3), 8)
    copies = [
        pltpu.make_async_copy(hidden_hbm, hidden_ref, sems.at[0]),
        pltpu.make_async_copy(segment_hbm.at[pl.ds(tile, 8), :], segment_ref, sems.at[1]),
        pltpu.make_async_copy(table_hbm, table_ref, sems.at[2]),
    ] + [
        pltpu.make_async_copy(weight_hbm.at[slot], weight_ref.at[slot], sems.at[3 + slot])
        for slot in range(3)
    ]
    half = half_ref.shape[0]
    own_rows = pl.ds(pl.multiple_of(ids_ref[CORE_AT] * half, half), half)
    copies.append(pltpu.make_async_copy(out_weight_hbm.at[own_rows, :], half_ref, sems.at[6]))
    for copy in copies:
        copy.start()
    copies[1].wait()
    head_width = weight_ref.shape[1]
    segments = segment_ref[pl.ds(row - tile, 1), :]
    starts = jnp.zeros_like(segments)
    for passage in range(PASS_DEV - 1):
        held = jnp.sum((segments == passage).astype(jnp.int32), axis=1, keepdims=True)
        starts = starts + jnp.where(segments > passage, held, 0)
    lane = lax.broadcasted_iota(jnp.int32, (1, length), 1)
    positions = lane - starts
    sublane = lax.broadcasted_iota(jnp.int32, (length, length), 0)
    copies[2].wait()
    chosen = (sublane == positions).astype(jnp.float32).astype(jnp.bfloat16)
    parts = matmul(table_ref[...], chosen, (((1,), (0,)), ((), ())))
    part = [parts[i * HALF_HEAD : (i + 1) * HALF_HEAD] for i in range(6)]
    cosine = part[0] + part[1] + part[2]
    sine = part[3] + part[4] + part[5]
    lengths = jnp.zeros_like(segments)
    for passage in range(PASS_DEV):
        held = jnp.sum((segments == passage).astype(jnp.int32), axis=1, keepdims=True)
        lengths = jnp.where(segments == passage, held, lengths)
    low = jnp.maximum(starts, lane - HALF_WIN)
    high = jnp.minimum(starts + lengths - 1, lane + HALF_WIN)
    allowed = (sublane >= low) & (sublane <= high)

    copies[0].wait()
    normed = layer_norm(hidden_ref[...].astype(jnp.float32), gain_ref[...]).astype(jnp.bfloat16)
    for copy in copies[3:6]:
        copy.wait()
    queries = matmul(weight_ref[0], normed, NT)
    key_cols = matmul(weight_ref[1], normed, NT)
    values = matmul(weight_ref[2], normed, NT).astype(jnp.bfloat16)

    def rotate(block):
        first, second = block[:HALF_HEAD], block[HALF_HEAD:]
        turned = jnp.concatenate(
            [first * cosine - second * sine, second * cosine + first * sine], axis=0
        )
        return turned.astype(jnp.bfloat16)

    for head in range(head_width // HEAD_DIM):
        at = slice(head * HEAD_DIM, (head + 1) * HEAD_DIM)
        scores = matmul(rotate(key_cols[at]), rotate(queries[at]), TN) * np.float32(HEAD_DIM**-0.5)
        raised = jnp.where(allowed, jnp.exp(scores), 0.0)
        probabilities = (raised / jnp.sum(raised, axis=0, keepdims=True)).astype(jnp.bfloat16)
        context = matmul(values[at], probabilities, (((1,), (0,)), ((), ()))).astype(jnp.bfloat16)
        for copy in range(out_ref.shape[0]):
            out_ref[copy, at, :] = context
    copies[6].wait()
    for column in range(half_ref.shape[1] // length):
        block = half_ref[:, column * length : (column + 1) * length]
        at = slice(head_width + column * half, head_width + (column + 1) * half)
        for copy in range(out_ref.shape[0]):
            out_ref[copy, at, :] = block


def ffn_kernel(
    ids_ref, hidden_ref, merged_ref, other_ref, gain_ref, in_ref, down_ref, after_ref, out_ref, weight_ref, all_ref
):
    length, width = hidden_ref.shape
    shards = merged_ref.shape[0]
    head_width = width // shards
    half = head_width // 2
    for shard in range(shards):
        for column in range(width // length):
            to = slice(column * length, (column + 1) * length)
            at = slice(column * half, (column + 1) * half)
            mine = merged_ref[shard, head_width + column * half : head_width + (column + 1) * half]
            for core, block in (
                (ids_ref[CORE_AT], mine),
                (1 - ids_ref[CORE_AT], other_ref[shard, at, :]),
            ):
                first = pl.multiple_of(shard * head_width + core * half, half)
                weight_ref[pl.ds(first, half), to] = block
    context = jnp.concatenate([merged_ref[shard, :head_width] for shard in range(shards)], axis=0)
    after_attn = hidden_ref[...].astype(jnp.float32) + matmul(context, weight_ref[...], TN)
    all_ref[...] = after_attn
    share = after_ref.shape[0]
    after_ref[...] = all_ref[pl.ds(pl.multiple_of(ids_ref[TERM_AT] * share, share), share), :]
    mixed = layer_norm(after_attn, gain_ref[...]).astype(jnp.bfloat16)
    inner_up = matmul(in_ref[0], mixed, NT)
    gate_part = matmul(in_ref[1], mixed, NT)
    activated = (gelu(inner_up) * gate_part).astype(jnp.bfloat16)
    out_ref[...] = matmul(activated, down_ref[...], TN).astype(jnp.bfloat16)


def head_kernel(after_ref, partial_ref, final_ref, dense_ref, head_ref, out_ref):
    after_ffn = after_ref[...]
    for shard in range(partial_ref.shape[0]):
        after_ffn = after_ffn + partial_ref[shard].astype(jnp.float32)
    normed = layer_norm(after_ffn, final_ref[...]).astype(jnp.bfloat16)
    dense = matmul(normed, dense_ref[...], (((1,), (0,)), ((), ())))
    headed = layer_norm(gelu(dense), head_ref[...]).astype(jnp.bfloat16)
    for copy in range(out_ref.shape[0]):
        out_ref[copy] = headed


def prep_kernel(ids_ref, segment_ref, list_ref, docs_ref, bounds_ref, mask_ref):
    segments = segment_ref[...]
    slot = lax.broadcasted_iota(jnp.int32, bounds_ref.shape, 1)
    bounds = jnp.zeros(bounds_ref.shape, jnp.int32)
    for passage in range(1, PASS_DEV + 1):
        before = jnp.sum((segments < passage).astype(jnp.int32), axis=1, keepdims=True)
        bounds = jnp.where(slot == passage, before, bounds)
    bounds_ref[...] = bounds
    own_terms, passages = mask_ref.shape
    groups = own_terms // SPAN
    stride = ids_ref[STRIDE_AT]
    blocks = list_ref[...] - ids_ref[BLOCK_AT]
    bits = jnp.zeros(blocks.shape, jnp.float32)
    for group in range(groups):
        bits = jnp.where(blocks == group * stride, np.float32(2**group), bits)
    ones = jnp.ones((SPAN, bits.shape[1]), jnp.bfloat16)
    codes = matmul(ones, bits.astype(jnp.bfloat16), NT).astype(jnp.bfloat16)
    columns = lax.broadcasted_iota(jnp.int32, (passages, passages), 1)
    place = (docs_ref[...] == columns).astype(jnp.float32).astype(jnp.bfloat16)
    placed = matmul(codes, place, (((1,), (0,)), ((), ()))).astype(jnp.int32)
    for group in range(groups):
        held = jnp.bitwise_and(lax.shift_right_logical(placed, group), 1)
        mask_ref[group * SPAN : (group + 1) * SPAN, :] = held.astype(jnp.float32)


def passage_maxima(ids_ref, bounds_ref, first_row, rows, table_ref, logits_ref):
    length = rows[0].shape[0]
    stacked = jnp.concatenate([row[...] for row in rows], axis=0)
    logits_ref[...] = matmul(stacked, table_ref[...], NT)
    tile = 8
    sublane = lax.broadcasted_iota(jnp.int32, (tile, logits_ref.shape[1]), 0)
    maxima = []
    for r in range(len(rows)):
        row = ids_ref[first_row + r]
        for passage in range(PASS_DEV):
            first = bounds_ref[row, passage]
            end = bounds_ref[row, passage + 1]
            first_tile = lax.shift_right_logical(first, 3)
            last_tile = lax.shift_right_logical(end - 1, 3)

            def load(t):
                return logits_ref[pl.ds(pl.multiple_of(r * length + t * tile, tile), tile), :]

            def inside(t):
                token = sublane + t * tile
                return jnp.where((token >= first) & (token < end), load(t), LOWEST)

            held = jnp.maximum(inside(first_tile), inside(last_tile))
            held = lax.fori_loop(
                first_tile + 1, last_tile, lambda t, m: jnp.maximum(m, load(t)), held
            )
            maxima.append(jnp.max(held, axis=0, keepdims=True))
    return jnp.concatenate(maxima, axis=0)


def near_pool_kernel(ids_ref, bounds_ref, own_ref, core_ref, table_ref, low_ref, logits_ref):
    rows = (own_ref, core_ref)
    low_ref[...] = passage_maxima(ids_ref, bounds_ref, 0, rows, table_ref, logits_ref)


def far_pool_kernel(
    ids_ref, bounds_ref, far_ref, far_core_ref, table_ref, low_ref, out_ref, logits_ref
):
    rows = (far_ref, far_core_ref)
    high = passage_maxima(ids_ref, bounds_ref, len(rows), rows, table_ref, logits_ref)
    low = low_ref[...]
    own_terms = out_ref.shape[2] // 2
    for slot in range(out_ref.shape[0]):
        at = slice(slot * own_terms, (slot + 1) * own_terms)
        out_ref[slot] = jnp.concatenate([low[:, at], high[:, at]], axis=1)


def place_kernel(maxima_ref, bias_ref, mask_ref, docs_ref, out_ref):
    raw = maxima_ref[...] + bias_ref[...]
    weighted = jnp.log1p(jnp.maximum(raw, 0.0))
    own_terms, passages = out_ref.shape
    columns = lax.broadcasted_iota(jnp.int32, (weighted.shape[0], passages), 1)
    terms = []
    rest = weighted
    for _ in range(3):
        terms.append(rest.astype(jnp.bfloat16))
        rest = rest - terms[-1].astype(jnp.float32)
    placed = jnp.zeros((own_terms, passages), jnp.float32)
    for half in range(2):
        place = (docs_ref[half] == columns).astype(jnp.float32).astype(jnp.bfloat16)
        at = slice(half * own_terms, (half + 1) * own_terms)
        sums = [matmul(term, place, TN)[at] for term in terms]
        placed = placed + (sums[0] + sums[1] + sums[2])
    out_ref[...] = placed * mask_ref[...]


def vmem():
    return pl.BlockSpec(memory_space=pltpu.VMEM)


def hbm():
    return pl.BlockSpec(memory_space=pltpu.HBM)


def smem():
    return pl.BlockSpec(memory_space=pltpu.SMEM)


def grant(mib):
    return pltpu.CompilerParams(vmem_limit_bytes=mib << 20)


def cost(flops, nbytes):
    return pl.CostEstimate(flops=flops, bytes_accessed=nbytes, transcendentals=0)


def exchange(copies, axis):
    return lax.all_to_all(copies, axis, split_axis=0, concat_axis=0, tiled=True)


def gather_by_exchange(block, axis):
    return exchange(jnp.broadcast_to(block[None], (lax.axis_size(axis),) + block.shape), axis)


def swap(block, axis, d=1):
    return lax.ppermute(block, axis, [(i, i ^ d) for i in range(lax.axis_size(axis))])


def others(block, axis):
    return [swap(block, axis, d) for d in range(1, lax.axis_size(axis))]


def on_device(
    hidden,
    segment_ids,
    block_lists,
    doc_ids,
    attn_gain,
    qkv_weight,
    attn_out,
    mlp_gain,
    ffn_in,
    ffn_out,
    final_gain,
    head_dense,
    head_gain,
    decoder,
    decoder_bias,
):
    near = ("y", "zh")
    slices = lax.axis_size(near)
    slice_index = lax.axis_index(near)
    near_row = lax.axis_index(("zl", "core"))
    rows_here = lax.axis_size(("zl", "core"))
    row_index = slice_index * rows_here + near_row
    tensor = lax.axis_size("term")
    tokens = hidden[0]
    length, width = tokens.shape
    groups, span = decoder.shape[1], decoder.shape[3]
    own_terms = groups * span
    head_width = qkv_weight.shape[2]
    passages = block_lists.shape[0]
    near_rows = jnp.stack([jnp.bitwise_xor(near_row, d) for d in range(rows_here)])
    row_ids = slice_index * rows_here + near_rows

    dp_count = slices * rows_here
    first_block = (lax.axis_index("term") * groups * dp_count * span + row_index * span) // BLOCK
    scalars = [
        lax.axis_index("term"),
        first_block,
        jnp.int32(dp_count * span // BLOCK),
        lax.axis_index("core"),
    ]
    ids = jnp.concatenate([row_ids, jnp.stack(scalars)])

    own_slice = decoder.reshape(own_terms, width)
    part = gather_by_exchange(own_slice, "zh").reshape(-1, width)
    rotary = jnp.asarray(rotary_table(length))
    half = head_width // 2
    chunk = head_width + half * width // length
    merged = pl.pallas_call(
        attention_kernel,
        out_shape=jax.ShapeDtypeStruct((tensor, chunk, length), jnp.bfloat16),
        in_specs=[smem(), vmem()] + [hbm()] * 5,
        out_specs=vmem(),
        scratch_shapes=[
            pltpu.VMEM((length, width), jnp.bfloat16),
            pltpu.VMEM((8, length), jnp.int32),
            pltpu.VMEM((3, head_width, width), jnp.bfloat16),
            pltpu.VMEM(rotary.shape, jnp.bfloat16),
            pltpu.VMEM((half, width), jnp.bfloat16),
            pltpu.SemaphoreType.DMA((7,)),
        ],
        compiler_params=grant(60),
        cost_estimate=cost(1200000000, 2000000),
        name="attention",
    )(
        ids, attn_gain[None], tokens, segment_ids, jnp.swapaxes(qkv_weight, 1, 2), rotary, attn_out
    )
    part, merged = lax.optimization_barrier((part, merged))
    table = lax.all_gather(part, "y", axis=0, tiled=True)
    merged = exchange(merged, "term")
    other = swap(merged[:, head_width:], "core")
    after_attn, partial = pl.pallas_call(
        ffn_kernel,
        out_shape=(
            jax.ShapeDtypeStruct((length // tensor, width), jnp.float32),
            jax.ShapeDtypeStruct((length, width), jnp.bfloat16),
        ),
        in_specs=[smem()] + [vmem()] * 6,
        out_specs=(vmem(), vmem()),
        scratch_shapes=[
            pltpu.VMEM((width, width), jnp.bfloat16),
            pltpu.VMEM((length, width), jnp.float32),
        ],
        compiler_params=grant(20),
        cost_estimate=cost(700000000, 4000000),
        name="ffn",
    )(ids, tokens, merged, other, mlp_gain[None], jnp.swapaxes(ffn_in, 1, 2), ffn_out)
    bounds, mask = pl.pallas_call(
        prep_kernel,
        out_shape=(
            jax.ShapeDtypeStruct((segment_ids.shape[0], 2 * PASS_DEV), jnp.int32),
            jax.ShapeDtypeStruct((own_terms, passages), jnp.float32),
        ),
        in_specs=[smem()] + [vmem()] * 3,
        out_specs=(vmem(), vmem()),
        compiler_params=grant(20),
        cost_estimate=cost(1000000, 1000000),
        name="prep",
    )(ids, segment_ids, block_lists, doc_ids[:, None])
    partials = exchange(partial.reshape(tensor, -1, width), "term")
    partials, bounds, mask = lax.optimization_barrier((partials, bounds, mask))
    headed = pl.pallas_call(
        head_kernel,
        out_shape=jax.ShapeDtypeStruct((tensor, length // tensor, width), jnp.bfloat16),
        in_specs=[vmem()] * 5,
        out_specs=vmem(),
        compiler_params=grant(20),
        cost_estimate=cost(800000000, 5000000),
        name="head",
    )(after_attn, partials, final_gain[None], head_dense, head_gain[None])

    headed = exchange(headed, "term").reshape(length, width)

    far = swap(headed, "zl")
    core = swap(headed, "core")
    far_core = swap(far, "core")
    terms_here = slices * own_terms
    logits = pltpu.VMEM((2 * length, terms_here), jnp.float32)
    low = pl.pallas_call(
        near_pool_kernel,
        out_shape=jax.ShapeDtypeStruct((2 * PASS_DEV, terms_here), jnp.float32),
        in_specs=[smem(), smem()] + [vmem()] * 3,
        out_specs=vmem(),
        scratch_shapes=[logits],
        compiler_params=grant(20),
        cost_estimate=cost(1600000000, 4000000),
        name="near_pool",
    )(ids, bounds, headed, core, table)
    pooled = pl.pallas_call(
        far_pool_kernel,
        out_shape=jax.ShapeDtypeStruct((slices, 2 * PASS_DEV, 2 * own_terms), jnp.float32),
        in_specs=[smem(), smem()] + [vmem()] * 4,
        out_specs=vmem(),
        scratch_shapes=[logits],
        compiler_params=grant(20),
        cost_estimate=cost(1600000000, 4000000),
        name="far_pool",
    )(ids, bounds, far, far_core, table, low)
    received = exchange(pooled, near)

    bias = decoder_bias.reshape(1, own_terms).astype(jnp.float32)
    docs = doc_ids.reshape(slices, rows_here, PASS_DEV)
    docs = jnp.stack([docs[:, near_rows[d]] for d in range(rows_here)], axis=1)
    docs = jnp.transpose(docs.reshape(slices, 2, 2 * PASS_DEV), (1, 0, 2)).reshape(2, -1, 1)
    placed = pl.pallas_call(
        place_kernel,
        out_shape=jax.ShapeDtypeStruct((own_terms, passages), jnp.float32),
        in_specs=[vmem()] * 4,
        out_specs=vmem(),
        cost_estimate=cost(200000000, 1000000),
        compiler_params=grant(16),
        name="place",
    )(
        received.reshape(-1, 2 * own_terms),
        jnp.concatenate([bias, bias], axis=1),
        mask,
        docs,
    )
    return placed.reshape(1, groups, 1, span, passages)


def solution(mesh):
    shape = (8, 4, 2, 2, mesh.devices.shape[1])
    fine = Mesh(mesh.devices.reshape(shape), ("y", "zh", "zl", "core", "term"))
    dp = ("y", "zh", "zl", "core")
    in_specs = (
        P(dp, None, None),
        P(),
        P(),
        P(),
        P(),
        P(None, None, "term"),
        P("term", None),
        P(),
        P(None, None, "term"),
        P("term", None),
        P(),
        P(),
        P(),
        P("term", None, dp, None, None),
        P("term", None, dp, None),
    )
    out_specs = P("term", None, dp, None, None)
    return jax.shard_map(
        on_device, mesh=fine, in_specs=in_specs, out_specs=out_specs, check_vma=False
    )
```

```python
import functools

import jax
import jax.numpy as jnp
import numpy as np
from jax import lax
from jax.experimental import pallas as pl
from jax.experimental.pallas import tpu as pltpu
from jax.sharding import Mesh
from jax.sharding import PartitionSpec as P

BLOCK = 128
HALF_WIN = 64
PASS_DEV = 4
HEAD_DIM = 64
HALF_HEAD = 32
SPAN = 8
NEAR = 4
LOWEST = -3.0e38
TERM_AT, BLOCK_AT, STRIDE_AT, CORE_AT, NEAR_AT = 4, 5, 6, 7, 8

NT = (((1,), (1,)), ((), ()))
TN = (((0,), (0,)), ((), ()))


def rotary_table(length):
    frequency = 10000.0 ** (-2.0 * np.arange(HALF_HEAD, dtype=np.float64) / HEAD_DIM)
    angles = frequency[:, None] * np.arange(length, dtype=np.float64)[None, :]
    terms = []
    for whole in (np.cos(angles), np.sin(angles)):
        rest = whole.astype(np.float32)
        for _ in range(3):
            term = rest.astype(jnp.bfloat16)
            terms.append(term)
            rest = rest - term.astype(np.float32)
    return np.concatenate(terms, axis=0)


def layer_norm(values, gain_row):
    average = jnp.mean(values, axis=-1, keepdims=True)
    centered = values - average
    spread = jnp.mean(centered * centered, axis=-1, keepdims=True)
    return centered * lax.rsqrt(spread + 1e-05) * gain_row


def gelu(values):
    return 0.5 * values * (1.0 + lax.erf(values * np.float32(0.5**0.5)))


def matmul(left, right, dims):
    return lax.dot_general(left, right, dims, preferred_element_type=jnp.float32)


def attention_kernel(
    gain_hbm,
    hidden_hbm,
    segment_hbm,
    weight_hbm,
    table_hbm,
    out_weight_hbm,
    out_ref,
    gain_ref,
    hidden_ref,
    segment_ref,
    weight_ref,
    table_ref,
    half_ref,
    sems,
):
    length = hidden_ref.shape[0]
    row = lax.axis_index("y")
    for axis in ("zh", "zl", "core"):
        row = row * lax.axis_size(axis) + lax.axis_index(axis)
    tile = pl.multiple_of(lax.shift_left(lax.shift_right_logical(row, 3), 3), 8)
    copies = [
        pltpu.make_async_copy(hidden_hbm, hidden_ref, sems.at[0]),
        pltpu.make_async_copy(segment_hbm.at[pl.ds(tile, 8), :], segment_ref, sems.at[1]),
        pltpu.make_async_copy(table_hbm, table_ref, sems.at[2]),
    ] + [
        pltpu.make_async_copy(weight_hbm.at[slot], weight_ref.at[slot], sems.at[3 + slot])
        for slot in range(3)
    ]
    half = half_ref.shape[0]
    own_rows = pl.ds(pl.multiple_of(lax.axis_index("core") * half, half), half)
    copies.append(pltpu.make_async_copy(out_weight_hbm.at[own_rows, :], half_ref, sems.at[6]))
    copies.append(pltpu.make_async_copy(gain_hbm, gain_ref, sems.at[7]))
    for copy in copies:
        copy.start()
    copies[1].wait()
    head_width = weight_ref.shape[1]
    segments = segment_ref[pl.ds(row - tile, 1), :]
    starts = jnp.zeros_like(segments)
    for passage in range(PASS_DEV - 1):
        held = jnp.sum((segments == passage).astype(jnp.int32), axis=1, keepdims=True)
        starts = starts + jnp.where(segments > passage, held, 0)
    lane = lax.broadcasted_iota(jnp.int32, (1, length), 1)
    positions = lane - starts
    sublane = lax.broadcasted_iota(jnp.int32, (length, length), 0)
    copies[2].wait()
    chosen = (sublane == positions).astype(jnp.float32).astype(jnp.bfloat16)
    parts = matmul(table_ref[...], chosen, (((1,), (0,)), ((), ())))
    part = [parts[i * HALF_HEAD : (i + 1) * HALF_HEAD] for i in range(6)]
    cosine = part[0] + part[1] + part[2]
    sine = part[3] + part[4] + part[5]
    lengths = jnp.zeros_like(segments)
    for passage in range(PASS_DEV):
        held = jnp.sum((segments == passage).astype(jnp.int32), axis=1, keepdims=True)
        lengths = jnp.where(segments == passage, held, lengths)
    low = jnp.maximum(starts, lane - HALF_WIN)
    high = jnp.minimum(starts + lengths - 1, lane + HALF_WIN)
    allowed = (sublane >= low) & (sublane <= high)

    copies[0].wait()
    copies[7].wait()
    gain = gain_ref[...].reshape(1, -1)
    normed = layer_norm(hidden_ref[...].astype(jnp.float32), gain).astype(jnp.bfloat16)
    for copy in copies[3:6]:
        copy.wait()
    queries = matmul(weight_ref[0], normed, NT)
    key_cols = matmul(weight_ref[1], normed, NT)
    values = matmul(weight_ref[2], normed, NT).astype(jnp.bfloat16)

    def rotate(block):
        first, second = block[:HALF_HEAD], block[HALF_HEAD:]
        turned = jnp.concatenate(
            [first * cosine - second * sine, second * cosine + first * sine], axis=0
        )
        return turned.astype(jnp.bfloat16)

    for head in range(head_width // HEAD_DIM):
        at = slice(head * HEAD_DIM, (head + 1) * HEAD_DIM)
        scores = matmul(rotate(key_cols[at]), rotate(queries[at]), TN) * np.float32(HEAD_DIM**-0.5)
        raised = jnp.where(allowed, jnp.exp(scores), 0.0)
        probabilities = (raised / jnp.sum(raised, axis=0, keepdims=True)).astype(jnp.bfloat16)
        context = matmul(values[at], probabilities, (((1,), (0,)), ((), ()))).astype(jnp.bfloat16)
        for copy in range(out_ref.shape[0]):
            out_ref[copy, at, :] = context
    copies[6].wait()
    for column in range(half_ref.shape[1] // length):
        block = half_ref[:, column * length : (column + 1) * length]
        at = slice(head_width + column * half, head_width + (column + 1) * half)
        for copy in range(out_ref.shape[0]):
            out_ref[copy, at, :] = block


def ffn_kernel(
    ids_ref, hidden_ref, merged_ref, other_ref, gain_ref, in_ref, down_ref, after_ref, out_ref, weight_ref, all_ref
):
    length, width = hidden_ref.shape
    shards = merged_ref.shape[0]
    head_width = width // shards
    half = head_width // 2
    for shard in range(shards):
        for column in range(width // length):
            to = slice(column * length, (column + 1) * length)
            at = slice(column * half, (column + 1) * half)
            mine = merged_ref[shard, head_width + column * half : head_width + (column + 1) * half]
            for core, block in (
                (ids_ref[CORE_AT], mine),
                (1 - ids_ref[CORE_AT], other_ref[shard, at, :]),
            ):
                first = pl.multiple_of(shard * head_width + core * half, half)
                weight_ref[pl.ds(first, half), to] = block
    context = jnp.concatenate([merged_ref[shard, :head_width] for shard in range(shards)], axis=0)
    after_attn = hidden_ref[...].astype(jnp.float32) + matmul(context, weight_ref[...], TN)
    all_ref[...] = after_attn
    share = after_ref.shape[0]
    after_ref[...] = all_ref[pl.ds(pl.multiple_of(ids_ref[TERM_AT] * share, share), share), :]
    mixed = layer_norm(after_attn, gain_ref[...]).astype(jnp.bfloat16)
    inner_up = matmul(in_ref[0], mixed, NT)
    gate_part = matmul(in_ref[1], mixed, NT)
    activated = (gelu(inner_up) * gate_part).astype(jnp.bfloat16)
    out_ref[...] = matmul(activated, down_ref[...], TN).astype(jnp.bfloat16)


def head_kernel(after_ref, partial_ref, final_ref, dense_ref, head_ref, out_ref):
    after_ffn = after_ref[...]
    for shard in range(partial_ref.shape[0]):
        after_ffn = after_ffn + partial_ref[shard].astype(jnp.float32)
    normed = layer_norm(after_ffn, final_ref[...]).astype(jnp.bfloat16)
    dense = matmul(normed, dense_ref[...], (((1,), (0,)), ((), ())))
    headed = layer_norm(gelu(dense), head_ref[...]).astype(jnp.bfloat16)
    for copy in range(out_ref.shape[0]):
        out_ref[copy] = headed


def prep_kernel(ids_ref, segment_ref, list_ref, docs_ref, bounds_ref, mask_ref):
    segments = segment_ref[...]
    slot = lax.broadcasted_iota(jnp.int32, bounds_ref.shape, 1)
    bounds = jnp.zeros(bounds_ref.shape, jnp.int32)
    for passage in range(1, PASS_DEV + 1):
        before = jnp.sum((segments < passage).astype(jnp.int32), axis=1, keepdims=True)
        bounds = jnp.where(slot == passage, before, bounds)
    bounds_ref[...] = bounds
    own_terms, passages = mask_ref.shape
    groups = own_terms // SPAN
    stride = ids_ref[STRIDE_AT]
    blocks = list_ref[...] - ids_ref[BLOCK_AT]
    bits = jnp.zeros(blocks.shape, jnp.float32)
    for group in range(groups):
        bits = jnp.where(blocks == group * stride, np.float32(2**group), bits)
    ones = jnp.ones((SPAN, bits.shape[1]), jnp.bfloat16)
    codes = matmul(ones, bits.astype(jnp.bfloat16), NT).astype(jnp.bfloat16)
    columns = lax.broadcasted_iota(jnp.int32, (passages, passages), 1)
    place = (docs_ref[...] == columns).astype(jnp.float32).astype(jnp.bfloat16)
    placed = matmul(codes, place, (((1,), (0,)), ((), ()))).astype(jnp.int32)
    for group in range(groups):
        held = jnp.bitwise_and(lax.shift_right_logical(placed, group), 1)
        mask_ref[group * SPAN : (group + 1) * SPAN, :] = held.astype(jnp.float32)


def passage_maxima(ids_ref, bounds_ref, first_row, rows, table_ref, logits_ref):
    length = rows[0].shape[0]
    stacked = jnp.concatenate([row[...] for row in rows], axis=0)
    logits_ref[...] = matmul(stacked, table_ref[...], NT)
    tile = 8
    sublane = lax.broadcasted_iota(jnp.int32, (tile, logits_ref.shape[1]), 0)
    maxima = []
    for r in range(len(rows)):
        row = ids_ref[first_row + r]
        for passage in range(PASS_DEV):
            first = bounds_ref[row, passage]
            end = bounds_ref[row, passage + 1]
            first_tile = lax.shift_right_logical(first, 3)
            last_tile = lax.shift_right_logical(end - 1, 3)

            def load(t):
                return logits_ref[pl.ds(pl.multiple_of(r * length + t * tile, tile), tile), :]

            def inside(t):
                token = sublane + t * tile
                return jnp.where((token >= first) & (token < end), load(t), LOWEST)

            held = jnp.maximum(inside(first_tile), inside(last_tile))
            held = lax.fori_loop(
                first_tile + 1, last_tile, lambda t, m: jnp.maximum(m, load(t)), held
            )
            maxima.append(jnp.max(held, axis=0, keepdims=True))
    return jnp.concatenate(maxima, axis=0)


def near_pool_kernel(ids_ref, bounds_ref, own_ref, core_ref, table_ref, low_ref, logits_ref):
    rows = (own_ref, core_ref)
    low_ref[...] = passage_maxima(ids_ref, bounds_ref, 0, rows, table_ref, logits_ref)


def far_pool_kernel(
    ids_ref, bounds_ref, far_ref, far_core_ref, table_ref, low_ref, out_ref, logits_ref
):
    rows = (far_ref, far_core_ref)
    high = passage_maxima(ids_ref, bounds_ref, len(rows), rows, table_ref, logits_ref)
    low = low_ref[...]
    own_terms = out_ref.shape[2] // 2
    for slot in range(out_ref.shape[0]):
        at = slice(slot * own_terms, (slot + 1) * own_terms)
        to = slot - slot % NEAR + jnp.bitwise_xor(ids_ref[NEAR_AT], slot % NEAR)
        out_ref[to] = jnp.concatenate([low[:, at], high[:, at]], axis=1)


def place_kernel(maxima_ref, bias_ref, mask_ref, docs_ref, out_ref):
    raw = maxima_ref[...] + bias_ref[...]
    weighted = jnp.log1p(jnp.maximum(raw, 0.0))
    own_terms, passages = out_ref.shape
    columns = lax.broadcasted_iota(jnp.int32, (weighted.shape[0], passages), 1)
    terms = []
    rest = weighted
    for _ in range(3):
        terms.append(rest.astype(jnp.bfloat16))
        rest = rest - terms[-1].astype(jnp.float32)
    placed = jnp.zeros((own_terms, passages), jnp.float32)
    for half in range(2):
        place = (docs_ref[half] == columns).astype(jnp.float32).astype(jnp.bfloat16)
        at = slice(half * own_terms, (half + 1) * own_terms)
        sums = [matmul(term, place, TN)[at] for term in terms]
        placed = placed + (sums[0] + sums[1] + sums[2])
    out_ref[...] = placed * mask_ref[...]


def vmem():
    return pl.BlockSpec(memory_space=pltpu.VMEM)


def hbm():
    return pl.BlockSpec(memory_space=pltpu.HBM)


def smem():
    return pl.BlockSpec(memory_space=pltpu.SMEM)


def grant(mib):
    return pltpu.CompilerParams(vmem_limit_bytes=mib << 20)


def cost(flops, nbytes):
    return pl.CostEstimate(flops=flops, bytes_accessed=nbytes, transcendentals=0)


def exchange(copies, axis):
    return lax.all_to_all(copies, axis, split_axis=0, concat_axis=0, tiled=True)


def swap(block, axis, d=1):
    return lax.ppermute(block, axis, [(i, i ^ d) for i in range(lax.axis_size(axis))])


def others(block, axis):
    return [swap(block, axis, d) for d in range(1, lax.axis_size(axis))]


def on_device(
    hidden,
    segment_ids,
    block_lists,
    doc_ids,
    attn_gain,
    qkv_weight,
    attn_out,
    mlp_gain,
    ffn_in,
    ffn_out,
    final_gain,
    head_dense,
    head_gain,
    decoder,
    decoder_bias,
):
    near = ("y", "zh")
    slices = lax.axis_size(near)
    slice_index = lax.axis_index(near)
    near_row = lax.axis_index(("zl", "core"))
    rows_here = lax.axis_size(("zl", "core"))
    row_index = slice_index * rows_here + near_row
    tensor = lax.axis_size("term")
    tokens = hidden[0]
    length, width = tokens.shape
    groups, span = decoder.shape[1], decoder.shape[3]
    own_terms = groups * span
    head_width = qkv_weight.shape[2]
    passages = block_lists.shape[0]
    near_rows = jnp.stack([jnp.bitwise_xor(near_row, d) for d in range(rows_here)])
    row_ids = slice_index * rows_here + near_rows

    dp_count = slices * rows_here
    first_block = (lax.axis_index("term") * groups * dp_count * span + row_index * span) // BLOCK
    scalars = [
        lax.axis_index("term"),
        first_block,
        jnp.int32(dp_count * span // BLOCK),
        lax.axis_index("core"),
        lax.axis_index("zh"),
    ]
    ids = jnp.concatenate([row_ids, jnp.stack(scalars)])

    own_slice = decoder.reshape(own_terms, width)
    pieces = others(own_slice, "zh")
    rotary = jnp.asarray(rotary_table(length))
    half = head_width // 2
    chunk = head_width + half * width // length
    merged = pl.pallas_call(
        attention_kernel,
        out_shape=jax.ShapeDtypeStruct((tensor, chunk, length), jnp.bfloat16),
        in_specs=[hbm()] * 6,
        out_specs=vmem(),
        scratch_shapes=[
            pltpu.VMEM((width,), jnp.float32),
            pltpu.VMEM((length, width), jnp.bfloat16),
            pltpu.VMEM((8, length), jnp.int32),
            pltpu.VMEM((3, head_width, width), jnp.bfloat16),
            pltpu.VMEM(rotary.shape, jnp.bfloat16),
            pltpu.VMEM((half, width), jnp.bfloat16),
            pltpu.SemaphoreType.DMA((8,)),
        ],
        compiler_params=grant(60),
        cost_estimate=cost(1200000000, 2000000),
        name="attention",
    )(attn_gain, tokens, segment_ids, jnp.swapaxes(qkv_weight, 1, 2), rotary, attn_out)
    pieces, merged = lax.optimization_barrier((pieces, merged))
    part = jnp.concatenate([own_slice] + pieces, axis=0)
    table = lax.all_gather(part, "y", axis=0, tiled=True)
    merged = exchange(merged, "term")
    other = swap(merged[:, head_width:], "core")
    after_attn, partial = pl.pallas_call(
        ffn_kernel,
        out_shape=(
            jax.ShapeDtypeStruct((length // tensor, width), jnp.float32),
            jax.ShapeDtypeStruct((length, width), jnp.bfloat16),
        ),
        in_specs=[smem()] + [vmem()] * 6,
        out_specs=(vmem(), vmem()),
        scratch_shapes=[
            pltpu.VMEM((width, width), jnp.bfloat16),
            pltpu.VMEM((length, width), jnp.float32),
        ],
        compiler_params=grant(20),
        cost_estimate=cost(700000000, 4000000),
        name="ffn",
    )(ids, tokens, merged, other, mlp_gain[None], jnp.swapaxes(ffn_in, 1, 2), ffn_out)
    bounds, mask = pl.pallas_call(
        prep_kernel,
        out_shape=(
            jax.ShapeDtypeStruct((segment_ids.shape[0], 2 * PASS_DEV), jnp.int32),
            jax.ShapeDtypeStruct((own_terms, passages), jnp.float32),
        ),
        in_specs=[smem()] + [vmem()] * 3,
        out_specs=(vmem(), vmem()),
        compiler_params=grant(20),
        cost_estimate=cost(1000000, 1000000),
        name="prep",
    )(ids, segment_ids, block_lists, doc_ids[:, None])
    partials = exchange(partial.reshape(tensor, -1, width), "term")
    partials, bounds, mask = lax.optimization_barrier((partials, bounds, mask))
    headed = pl.pallas_call(
        head_kernel,
        out_shape=jax.ShapeDtypeStruct((tensor, length // tensor, width), jnp.bfloat16),
        in_specs=[vmem()] * 5,
        out_specs=vmem(),
        compiler_params=grant(20),
        cost_estimate=cost(800000000, 5000000),
        name="head",
    )(after_attn, partials, final_gain[None], head_dense, head_gain[None])

    headed = exchange(headed, "term").reshape(length, width)

    far = swap(headed, "zl")
    core = swap(headed, "core")
    terms_here = slices * own_terms
    logits = pltpu.VMEM((2 * length, terms_here), jnp.float32)
    low = pl.pallas_call(
        near_pool_kernel,
        out_shape=jax.ShapeDtypeStruct((2 * PASS_DEV, terms_here), jnp.float32),
        in_specs=[smem(), smem()] + [vmem()] * 3,
        out_specs=vmem(),
        scratch_shapes=[logits],
        compiler_params=grant(20),
        cost_estimate=cost(1600000000, 4000000),
        name="near_pool",
    )(ids, bounds, headed, core, table)
    far, low = lax.optimization_barrier((far, low))
    far_core = swap(far, "core")
    pooled = pl.pallas_call(
        far_pool_kernel,
        out_shape=jax.ShapeDtypeStruct((slices, 2 * PASS_DEV, 2 * own_terms), jnp.float32),
        in_specs=[smem(), smem()] + [vmem()] * 4,
        out_specs=vmem(),
        scratch_shapes=[logits],
        compiler_params=grant(20),
        cost_estimate=cost(1600000000, 4000000),
        name="far_pool",
    )(ids, bounds, far, far_core, table, low)
    received = exchange(pooled, near)

    bias = decoder_bias.reshape(1, own_terms).astype(jnp.float32)
    docs = doc_ids.reshape(slices, rows_here, PASS_DEV)
    docs = jnp.stack([docs[:, near_rows[d]] for d in range(rows_here)], axis=1)
    docs = jnp.transpose(docs.reshape(slices, 2, 2 * PASS_DEV), (1, 0, 2)).reshape(2, -1, 1)
    placed = pl.pallas_call(
        place_kernel,
        out_shape=jax.ShapeDtypeStruct((own_terms, passages), jnp.float32),
        in_specs=[vmem()] * 4,
        out_specs=vmem(),
        cost_estimate=cost(200000000, 1000000),
        compiler_params=grant(16),
        name="place",
    )(
        received.reshape(-1, 2 * own_terms),
        jnp.concatenate([bias, bias], axis=1),
        mask,
        docs,
    )
    return placed.reshape(1, groups, 1, span, passages)


def solution(mesh):
    shape = (8, 4, 2, 2, mesh.devices.shape[1])
    fine = Mesh(mesh.devices.reshape(shape), ("y", "zh", "zl", "core", "term"))
    dp = ("y", "zh", "zl", "core")
    in_specs = (
        P(dp, None, None),
        P(),
        P(),
        P(),
        P(),
        P(None, None, "term"),
        P("term", None),
        P(),
        P(None, None, "term"),
        P("term", None),
        P(),
        P(),
        P(),
        P("term", None, dp, None, None),
        P("term", None, dp, None),
    )
    out_specs = P("term", None, dp, None, None)
    return jax.shard_map(
        on_device, mesh=fine, in_specs=in_specs, out_specs=out_specs, check_vma=False
    )
```

```python
import functools

import jax
import jax.numpy as jnp
import numpy as np
from jax import lax
from jax.experimental import pallas as pl
from jax.experimental.pallas import tpu as pltpu
from jax.sharding import Mesh
from jax.sharding import PartitionSpec as P

BLOCK = 128
HALF_WIN = 64
PASS_DEV = 4
HEAD_DIM = 64
HALF_HEAD = 32
SPAN = 8
NEAR = 4
LOWEST = -3.0e38

NT = (((1,), (1,)), ((), ()))
TN = (((0,), (0,)), ((), ()))


def rotary_table(length):
    frequency = 10000.0 ** (-2.0 * np.arange(HALF_HEAD, dtype=np.float64) / HEAD_DIM)
    angles = frequency[:, None] * np.arange(length, dtype=np.float64)[None, :]
    terms = []
    for whole in (np.cos(angles), np.sin(angles)):
        rest = whole.astype(np.float32)
        for _ in range(3):
            term = rest.astype(jnp.bfloat16)
            terms.append(term)
            rest = rest - term.astype(np.float32)
    return np.concatenate(terms, axis=0)


def layer_norm(values, gain_row):
    average = jnp.mean(values, axis=-1, keepdims=True)
    centered = values - average
    spread = jnp.mean(centered * centered, axis=-1, keepdims=True)
    return centered * lax.rsqrt(spread + 1e-05) * gain_row


def gelu(values):
    return 0.5 * values * (1.0 + lax.erf(values * np.float32(0.5**0.5)))


def matmul(left, right, dims):
    return lax.dot_general(left, right, dims, preferred_element_type=jnp.float32)


def row_index(d=0):
    near = lax.axis_index("zl") * lax.axis_size("core") + lax.axis_index("core")
    own = lax.axis_index("y") * lax.axis_size("zh") + lax.axis_index("zh")
    return own * lax.axis_size("zl") * lax.axis_size("core") + jnp.bitwise_xor(near, d)


def attention_kernel(
    gain_hbm,
    hidden_hbm,
    segment_hbm,
    weight_hbm,
    table_hbm,
    out_weight_hbm,
    out_ref,
    gain_ref,
    hidden_ref,
    segment_ref,
    weight_ref,
    table_ref,
    half_ref,
    sems,
):
    length = hidden_ref.shape[0]
    row = row_index()
    tile = pl.multiple_of(lax.shift_left(lax.shift_right_logical(row, 3), 3), 8)
    copies = [
        pltpu.make_async_copy(hidden_hbm, hidden_ref, sems.at[0]),
        pltpu.make_async_copy(segment_hbm.at[pl.ds(tile, 8), :], segment_ref, sems.at[1]),
        pltpu.make_async_copy(table_hbm, table_ref, sems.at[2]),
    ] + [
        pltpu.make_async_copy(weight_hbm.at[slot], weight_ref.at[slot], sems.at[3 + slot])
        for slot in range(3)
    ]
    half = half_ref.shape[0]
    own_rows = pl.ds(pl.multiple_of(lax.axis_index("core") * half, half), half)
    copies.append(pltpu.make_async_copy(out_weight_hbm.at[own_rows, :], half_ref, sems.at[6]))
    copies.append(pltpu.make_async_copy(gain_hbm, gain_ref, sems.at[7]))
    for copy in copies:
        copy.start()
    copies[1].wait()
    head_width = weight_ref.shape[1]
    segments = segment_ref[pl.ds(row - tile, 1), :]
    starts = jnp.zeros_like(segments)
    for passage in range(PASS_DEV - 1):
        held = jnp.sum((segments == passage).astype(jnp.int32), axis=1, keepdims=True)
        starts = starts + jnp.where(segments > passage, held, 0)
    lane = lax.broadcasted_iota(jnp.int32, (1, length), 1)
    positions = lane - starts
    sublane = lax.broadcasted_iota(jnp.int32, (length, length), 0)
    copies[2].wait()
    chosen = (sublane == positions).astype(jnp.float32).astype(jnp.bfloat16)
    parts = matmul(table_ref[...], chosen, (((1,), (0,)), ((), ())))
    part = [parts[i * HALF_HEAD : (i + 1) * HALF_HEAD] for i in range(6)]
    cosine = part[0] + part[1] + part[2]
    sine = part[3] + part[4] + part[5]
    lengths = jnp.zeros_like(segments)
    for passage in range(PASS_DEV):
        held = jnp.sum((segments == passage).astype(jnp.int32), axis=1, keepdims=True)
        lengths = jnp.where(segments == passage, held, lengths)
    low = jnp.maximum(starts, lane - HALF_WIN)
    high = jnp.minimum(starts + lengths - 1, lane + HALF_WIN)
    allowed = (sublane >= low) & (sublane <= high)

    copies[0].wait()
    copies[7].wait()
    gain = gain_ref[...].reshape(1, -1)
    normed = layer_norm(hidden_ref[...].astype(jnp.float32), gain).astype(jnp.bfloat16)
    for copy in copies[3:6]:
        copy.wait()
    queries = matmul(weight_ref[0], normed, NT)
    key_cols = matmul(weight_ref[1], normed, NT)
    values = matmul(weight_ref[2], normed, NT).astype(jnp.bfloat16)

    def rotate(block):
        first, second = block[:HALF_HEAD], block[HALF_HEAD:]
        turned = jnp.concatenate(
            [first * cosine - second * sine, second * cosine + first * sine], axis=0
        )
        return turned.astype(jnp.bfloat16)

    for head in range(head_width // HEAD_DIM):
        at = slice(head * HEAD_DIM, (head + 1) * HEAD_DIM)
        scores = matmul(rotate(key_cols[at]), rotate(queries[at]), TN) * np.float32(HEAD_DIM**-0.5)
        raised = jnp.where(allowed, jnp.exp(scores), 0.0)
        probabilities = (raised / jnp.sum(raised, axis=0, keepdims=True)).astype(jnp.bfloat16)
        context = matmul(values[at], probabilities, (((1,), (0,)), ((), ()))).astype(jnp.bfloat16)
        for copy in range(out_ref.shape[0]):
            out_ref[copy, at, :] = context
    copies[6].wait()
    for column in range(half_ref.shape[1] // length):
        block = half_ref[:, column * length : (column + 1) * length]
        at = slice(head_width + column * half, head_width + (column + 1) * half)
        for copy in range(out_ref.shape[0]):
            out_ref[copy, at, :] = block


def ffn_kernel(
    hidden_ref, merged_ref, other_ref, gain_ref, in_ref, down_ref, after_ref, out_ref, weight_ref, all_ref
):
    length, width = hidden_ref.shape
    shards = merged_ref.shape[0]
    head_width = width // shards
    half = head_width // 2
    for shard in range(shards):
        for column in range(width // length):
            to = slice(column * length, (column + 1) * length)
            at = slice(column * half, (column + 1) * half)
            mine = merged_ref[shard, head_width + column * half : head_width + (column + 1) * half]
            for core, block in (
                (lax.axis_index("core"), mine),
                (1 - lax.axis_index("core"), other_ref[shard, at, :]),
            ):
                first = pl.multiple_of(shard * head_width + core * half, half)
                weight_ref[pl.ds(first, half), to] = block
    context = jnp.concatenate([merged_ref[shard, :head_width] for shard in range(shards)], axis=0)
    after_attn = hidden_ref[...].astype(jnp.float32) + matmul(context, weight_ref[...], TN)
    all_ref[...] = after_attn
    share = after_ref.shape[0]
    after_ref[...] = all_ref[pl.ds(pl.multiple_of(lax.axis_index("term") * share, share), share), :]
    mixed = layer_norm(after_attn, gain_ref[...].reshape(1, -1)).astype(jnp.bfloat16)
    inner_up = matmul(in_ref[0], mixed, NT)
    gate_part = matmul(in_ref[1], mixed, NT)
    activated = (gelu(inner_up) * gate_part).astype(jnp.bfloat16)
    out_ref[...] = matmul(activated, down_ref[...], TN).astype(jnp.bfloat16)


def head_kernel(after_ref, partial_ref, final_ref, dense_ref, head_ref, out_ref):
    after_ffn = after_ref[...]
    for shard in range(partial_ref.shape[0]):
        after_ffn = after_ffn + partial_ref[shard].astype(jnp.float32)
    normed = layer_norm(after_ffn, final_ref[...].reshape(1, -1)).astype(jnp.bfloat16)
    dense = matmul(normed, dense_ref[...], (((1,), (0,)), ((), ())))
    headed = layer_norm(gelu(dense), head_ref[...].reshape(1, -1)).astype(jnp.bfloat16)
    for copy in range(out_ref.shape[0]):
        out_ref[copy] = headed


def prep_kernel(segment_ref, list_ref, docs_ref, bounds_ref, mask_ref):
    segments = segment_ref[...]
    slot = lax.broadcasted_iota(jnp.int32, bounds_ref.shape, 1)
    bounds = jnp.zeros(bounds_ref.shape, jnp.int32)
    for passage in range(1, PASS_DEV + 1):
        before = jnp.sum((segments < passage).astype(jnp.int32), axis=1, keepdims=True)
        bounds = jnp.where(slot == passage, before, bounds)
    bounds_ref[...] = bounds
    own_terms, passages = mask_ref.shape
    groups = own_terms // SPAN
    stride = segment_ref.shape[0] * SPAN // BLOCK
    first_block = lax.axis_index("term") * groups * stride + row_index() * SPAN // BLOCK
    blocks = list_ref[...] - first_block
    bits = jnp.zeros(blocks.shape, jnp.float32)
    for group in range(groups):
        bits = jnp.where(blocks == group * stride, np.float32(2**group), bits)
    ones = jnp.ones((SPAN, bits.shape[1]), jnp.bfloat16)
    codes = matmul(ones, bits.astype(jnp.bfloat16), NT).astype(jnp.bfloat16)
    columns = lax.broadcasted_iota(jnp.int32, (passages, passages), 1)
    place = (docs_ref[...] == columns).astype(jnp.float32).astype(jnp.bfloat16)
    placed = matmul(codes, place, (((1,), (0,)), ((), ()))).astype(jnp.int32)
    for group in range(groups):
        held = jnp.bitwise_and(lax.shift_right_logical(placed, group), 1)
        mask_ref[group * SPAN : (group + 1) * SPAN, :] = held.astype(jnp.float32)


def passage_maxima(bounds_ref, first_row, rows, table_ref, logits_ref):
    length = rows[0].shape[0]
    stacked = jnp.concatenate([row[...] for row in rows], axis=0)
    logits_ref[...] = matmul(stacked, table_ref[...], NT)
    tile = 8
    sublane = lax.broadcasted_iota(jnp.int32, (tile, logits_ref.shape[1]), 0)
    maxima = []
    for r in range(len(rows)):
        row = row_index(first_row + r)
        for passage in range(PASS_DEV):
            first = bounds_ref[row, passage]
            end = bounds_ref[row, passage + 1]
            first_tile = lax.shift_right_logical(first, 3)
            last_tile = lax.shift_right_logical(end - 1, 3)

            def load(t):
                return logits_ref[pl.ds(pl.multiple_of(r * length + t * tile, tile), tile), :]

            def inside(t):
                token = sublane + t * tile
                return jnp.where((token >= first) & (token < end), load(t), LOWEST)

            held = jnp.maximum(inside(first_tile), inside(last_tile))
            held = lax.fori_loop(
                first_tile + 1, last_tile, lambda t, m: jnp.maximum(m, load(t)), held
            )
            maxima.append(jnp.max(held, axis=0, keepdims=True))
    return jnp.concatenate(maxima, axis=0)


def near_pool_kernel(bounds_ref, own_ref, core_ref, table_ref, low_ref, logits_ref):
    rows = (own_ref, core_ref)
    low_ref[...] = passage_maxima(bounds_ref, 0, rows, table_ref, logits_ref)


def far_pool_kernel(
    bounds_ref, far_ref, far_core_ref, table_ref, low_ref, out_ref, logits_ref
):
    rows = (far_ref, far_core_ref)
    high = passage_maxima(bounds_ref, len(rows), rows, table_ref, logits_ref)
    low = low_ref[...]
    own_terms = out_ref.shape[2] // 2
    for slot in range(out_ref.shape[0]):
        at = slice(slot * own_terms, (slot + 1) * own_terms)
        to = slot - slot % NEAR + jnp.bitwise_xor(lax.axis_index("zh"), slot % NEAR)
        out_ref[to] = jnp.concatenate([low[:, at], high[:, at]], axis=1)


def place_kernel(maxima_ref, bias_ref, mask_ref, docs_ref, out_ref):
    raw = maxima_ref[...] + bias_ref[...]
    weighted = jnp.log1p(jnp.maximum(raw, 0.0))
    own_terms, passages = out_ref.shape
    columns = lax.broadcasted_iota(jnp.int32, (weighted.shape[0], passages), 1)
    terms = []
    rest = weighted
    for _ in range(3):
        terms.append(rest.astype(jnp.bfloat16))
        rest = rest - terms[-1].astype(jnp.float32)
    placed = jnp.zeros((own_terms, passages), jnp.float32)
    for half in range(2):
        place = (docs_ref[half] == columns).astype(jnp.float32).astype(jnp.bfloat16)
        at = slice(half * own_terms, (half + 1) * own_terms)
        sums = [matmul(term, place, TN)[at] for term in terms]
        placed = placed + (sums[0] + sums[1] + sums[2])
    out_ref[...] = placed * mask_ref[...]


def vmem():
    return pl.BlockSpec(memory_space=pltpu.VMEM)


def hbm():
    return pl.BlockSpec(memory_space=pltpu.HBM)


def smem():
    return pl.BlockSpec(memory_space=pltpu.SMEM)


def grant(mib):
    return pltpu.CompilerParams(vmem_limit_bytes=mib << 20)


def cost(flops, nbytes):
    return pl.CostEstimate(flops=flops, bytes_accessed=nbytes, transcendentals=0)


def exchange(copies, axis):
    return lax.all_to_all(copies, axis, split_axis=0, concat_axis=0, tiled=True)


def swap(block, axis, d=1):
    return lax.ppermute(block, axis, [(i, i ^ d) for i in range(lax.axis_size(axis))])


def others(block, axis):
    return [swap(block, axis, d) for d in range(1, lax.axis_size(axis))]


def on_device(
    hidden,
    segment_ids,
    block_lists,
    doc_ids,
    attn_gain,
    qkv_weight,
    attn_out,
    mlp_gain,
    ffn_in,
    ffn_out,
    final_gain,
    head_dense,
    head_gain,
    decoder,
    decoder_bias,
):
    near = ("y", "zh")
    slices = lax.axis_size(near)
    near_row = lax.axis_index(("zl", "core"))
    rows_here = lax.axis_size(("zl", "core"))
    tensor = lax.axis_size("term")
    tokens = hidden[0]
    length, width = tokens.shape
    groups, span = decoder.shape[1], decoder.shape[3]
    own_terms = groups * span
    head_width = qkv_weight.shape[2]
    passages = block_lists.shape[0]
    near_rows = jnp.stack([jnp.bitwise_xor(near_row, d) for d in range(rows_here)])

    own_slice = decoder.reshape(own_terms, width)
    rotary = jnp.asarray(rotary_table(length))
    half = head_width // 2
    chunk = head_width + half * width // length
    merged = pl.pallas_call(
        attention_kernel,
        out_shape=jax.ShapeDtypeStruct((tensor, chunk, length), jnp.bfloat16),
        in_specs=[hbm()] * 6,
        out_specs=vmem(),
        scratch_shapes=[
            pltpu.VMEM((width,), jnp.float32),
            pltpu.VMEM((length, width), jnp.bfloat16),
            pltpu.VMEM((8, length), jnp.int32),
            pltpu.VMEM((3, head_width, width), jnp.bfloat16),
            pltpu.VMEM(rotary.shape, jnp.bfloat16),
            pltpu.VMEM((half, width), jnp.bfloat16),
            pltpu.SemaphoreType.DMA((8,)),
        ],
        compiler_params=grant(60),
        cost_estimate=cost(1200000000, 2000000),
        name="attention",
    )(attn_gain, tokens, segment_ids, jnp.swapaxes(qkv_weight, 1, 2), rotary, attn_out)
    own_slice, merged = lax.optimization_barrier((own_slice, merged))
    part = jnp.concatenate([own_slice] + others(own_slice, "zh"), axis=0)
    merged, part = lax.optimization_barrier((exchange(merged, "term"), part))
    table = lax.all_gather(part, "y", axis=0, tiled=True)
    other = swap(merged[:, head_width:], "core")
    after_attn, partial = pl.pallas_call(
        ffn_kernel,
        out_shape=(
            jax.ShapeDtypeStruct((length // tensor, width), jnp.float32),
            jax.ShapeDtypeStruct((length, width), jnp.bfloat16),
        ),
        in_specs=[vmem()] * 6,
        out_specs=(vmem(), vmem()),
        scratch_shapes=[
            pltpu.VMEM((width, width), jnp.bfloat16),
            pltpu.VMEM((length, width), jnp.float32),
        ],
        compiler_params=grant(20),
        cost_estimate=cost(700000000, 4000000),
        name="ffn",
    )(tokens, merged, other, mlp_gain, jnp.swapaxes(ffn_in, 1, 2), ffn_out)
    bounds, mask = pl.pallas_call(
        prep_kernel,
        out_shape=(
            jax.ShapeDtypeStruct((segment_ids.shape[0], 2 * PASS_DEV), jnp.int32),
            jax.ShapeDtypeStruct((own_terms, passages), jnp.float32),
        ),
        in_specs=[vmem()] * 3,
        out_specs=(vmem(), vmem()),
        compiler_params=grant(20),
        cost_estimate=cost(1000000, 1000000),
        name="prep",
    )(segment_ids, block_lists, doc_ids[:, None])
    partials = exchange(partial.reshape(tensor, -1, width), "term")
    partials, bounds, mask = lax.optimization_barrier((partials, bounds, mask))
    headed = pl.pallas_call(
        head_kernel,
        out_shape=jax.ShapeDtypeStruct((tensor, length // tensor, width), jnp.bfloat16),
        in_specs=[vmem()] * 5,
        out_specs=vmem(),
        compiler_params=grant(20),
        cost_estimate=cost(800000000, 5000000),
        name="head",
    )(after_attn, partials, final_gain, head_dense, head_gain)

    headed = exchange(headed, "term").reshape(length, width)

    far = swap(headed, "zl")
    core = swap(headed, "core")
    terms_here = slices * own_terms
    logits = pltpu.VMEM((2 * length, terms_here), jnp.float32)
    low = pl.pallas_call(
        near_pool_kernel,
        out_shape=jax.ShapeDtypeStruct((2 * PASS_DEV, terms_here), jnp.float32),
        in_specs=[smem()] + [vmem()] * 3,
        out_specs=vmem(),
        scratch_shapes=[logits],
        compiler_params=grant(20),
        cost_estimate=cost(1600000000, 4000000),
        name="near_pool",
    )(bounds, headed, core, table)
    far_core = swap(far, "core")
    pooled = pl.pallas_call(
        far_pool_kernel,
        out_shape=jax.ShapeDtypeStruct((slices, 2 * PASS_DEV, 2 * own_terms), jnp.float32),
        in_specs=[smem()] + [vmem()] * 4,
        out_specs=vmem(),
        scratch_shapes=[logits],
        compiler_params=grant(20),
        cost_estimate=cost(1600000000, 4000000),
        name="far_pool",
    )(bounds, far, far_core, table, low)
    received = exchange(pooled, near)

    bias = decoder_bias.reshape(1, own_terms).astype(jnp.float32)
    docs = doc_ids.reshape(slices, rows_here, PASS_DEV)
    docs = jnp.stack([docs[:, near_rows[d]] for d in range(rows_here)], axis=1)
    docs = jnp.transpose(docs.reshape(slices, 2, 2 * PASS_DEV), (1, 0, 2)).reshape(2, -1, 1)
    placed = pl.pallas_call(
        place_kernel,
        out_shape=jax.ShapeDtypeStruct((own_terms, passages), jnp.float32),
        in_specs=[vmem()] * 4,
        out_specs=vmem(),
        cost_estimate=cost(200000000, 1000000),
        compiler_params=grant(16),
        name="place",
    )(
        received.reshape(-1, 2 * own_terms),
        jnp.concatenate([bias, bias], axis=1),
        mask,
        docs,
    )
    return placed.reshape(1, groups, 1, span, passages)


def solution(mesh):
    shape = (8, 4, 2, 2, mesh.devices.shape[1])
    fine = Mesh(mesh.devices.reshape(shape), ("y", "zh", "zl", "core", "term"))
    dp = ("y", "zh", "zl", "core")
    in_specs = (
        P(dp, None, None),
        P(),
        P(),
        P(),
        P(),
        P(None, None, "term"),
        P("term", None),
        P(),
        P(None, None, "term"),
        P("term", None),
        P(),
        P(),
        P(),
        P("term", None, dp, None, None),
        P("term", None, dp, None),
    )
    out_specs = P("term", None, dp, None, None)
    return jax.shard_map(
        on_device, mesh=fine, in_specs=in_specs, out_specs=out_specs, check_vma=False
    )
```

```python
import functools

import jax
import jax.numpy as jnp
import numpy as np
from jax import lax
from jax.experimental import pallas as pl
from jax.experimental.pallas import tpu as pltpu
from jax.sharding import Mesh
from jax.sharding import PartitionSpec as P

BLOCK = 128
HALF_WIN = 64
PASS_DEV = 4
HEAD_DIM = 64
HALF_HEAD = 32
SPAN = 8
NEAR = 4
LOWEST = -3.0e38

NT = (((1,), (1,)), ((), ()))
TN = (((0,), (0,)), ((), ()))


def rotary_table(length):
    frequency = 10000.0 ** (-2.0 * np.arange(HALF_HEAD, dtype=np.float64) / HEAD_DIM)
    angles = frequency[:, None] * np.arange(length, dtype=np.float64)[None, :]
    terms = []
    for whole in (np.cos(angles), np.sin(angles)):
        rest = whole.astype(np.float32)
        for _ in range(3):
            term = rest.astype(jnp.bfloat16)
            terms.append(term)
            rest = rest - term.astype(np.float32)
    return np.concatenate(terms, axis=0)


def layer_norm(values, gain_row):
    average = jnp.mean(values, axis=-1, keepdims=True)
    centered = values - average
    spread = jnp.mean(centered * centered, axis=-1, keepdims=True)
    return centered * lax.rsqrt(spread + 1e-05) * gain_row


def gelu(values):
    return 0.5 * values * (1.0 + lax.erf(values * np.float32(0.5**0.5)))


def matmul(left, right, dims):
    return lax.dot_general(left, right, dims, preferred_element_type=jnp.float32)


def row_index(d=0):
    near = lax.axis_index("zl") * lax.axis_size("core") + lax.axis_index("core")
    own = lax.axis_index("y") * lax.axis_size("zh") + lax.axis_index("zh")
    return own * lax.axis_size("zl") * lax.axis_size("core") + jnp.bitwise_xor(near, d)


def attention_kernel(
    gain_hbm,
    hidden_hbm,
    segment_hbm,
    weight_hbm,
    table_hbm,
    out_weight_hbm,
    in_hbm,
    down_hbm,
    out_ref,
    shard_ref,
    gain_ref,
    hidden_ref,
    segment_ref,
    weight_ref,
    table_ref,
    half_ref,
    sems,
):
    length = hidden_ref.shape[0]
    row = row_index()
    tile = pl.multiple_of(lax.shift_left(lax.shift_right_logical(row, 3), 3), 8)
    copies = [
        pltpu.make_async_copy(hidden_hbm, hidden_ref, sems.at[0]),
        pltpu.make_async_copy(segment_hbm.at[pl.ds(tile, 8), :], segment_ref, sems.at[1]),
        pltpu.make_async_copy(table_hbm, table_ref, sems.at[2]),
    ] + [
        pltpu.make_async_copy(weight_hbm.at[slot], weight_ref.at[slot], sems.at[3 + slot])
        for slot in range(3)
    ]
    half = half_ref.shape[0]
    own_rows = pl.ds(pl.multiple_of(lax.axis_index("core") * half, half), half)
    copies.append(pltpu.make_async_copy(out_weight_hbm.at[own_rows, :], half_ref, sems.at[6]))
    copies.append(pltpu.make_async_copy(gain_hbm, gain_ref, sems.at[7]))
    units = shard_ref.shape[0] // 3
    own_units = pl.ds(pl.multiple_of(lax.axis_index("core") * units, units), units)
    for slot, source in enumerate((in_hbm.at[0], in_hbm.at[1], down_hbm)):
        to = shard_ref.at[slot * units : (slot + 1) * units, :]
        copies.append(pltpu.make_async_copy(source.at[own_units, :], to, sems.at[8 + slot]))
    for copy in copies:
        copy.start()
    copies[1].wait()
    head_width = weight_ref.shape[1]
    segments = segment_ref[pl.ds(row - tile, 1), :]
    starts = jnp.zeros_like(segments)
    for passage in range(PASS_DEV - 1):
        held = jnp.sum((segments == passage).astype(jnp.int32), axis=1, keepdims=True)
        starts = starts + jnp.where(segments > passage, held, 0)
    lane = lax.broadcasted_iota(jnp.int32, (1, length), 1)
    positions = lane - starts
    sublane = lax.broadcasted_iota(jnp.int32, (length, length), 0)
    copies[2].wait()
    chosen = (sublane == positions).astype(jnp.float32).astype(jnp.bfloat16)
    parts = matmul(table_ref[...], chosen, (((1,), (0,)), ((), ())))
    part = [parts[i * HALF_HEAD : (i + 1) * HALF_HEAD] for i in range(6)]
    cosine = part[0] + part[1] + part[2]
    sine = part[3] + part[4] + part[5]
    lengths = jnp.zeros_like(segments)
    for passage in range(PASS_DEV):
        held = jnp.sum((segments == passage).astype(jnp.int32), axis=1, keepdims=True)
        lengths = jnp.where(segments == passage, held, lengths)
    low = jnp.maximum(starts, lane - HALF_WIN)
    high = jnp.minimum(starts + lengths - 1, lane + HALF_WIN)
    allowed = (sublane >= low) & (sublane <= high)

    copies[0].wait()
    copies[7].wait()
    gain = gain_ref[...].reshape(1, -1)
    normed = layer_norm(hidden_ref[...].astype(jnp.float32), gain).astype(jnp.bfloat16)
    for copy in copies[3:6]:
        copy.wait()
    queries = matmul(weight_ref[0], normed, NT)
    key_cols = matmul(weight_ref[1], normed, NT)
    values = matmul(weight_ref[2], normed, NT).astype(jnp.bfloat16)

    def rotate(block):
        first, second = block[:HALF_HEAD], block[HALF_HEAD:]
        turned = jnp.concatenate(
            [first * cosine - second * sine, second * cosine + first * sine], axis=0
        )
        return turned.astype(jnp.bfloat16)

    for head in range(head_width // HEAD_DIM):
        at = slice(head * HEAD_DIM, (head + 1) * HEAD_DIM)
        scores = matmul(rotate(key_cols[at]), rotate(queries[at]), TN) * np.float32(HEAD_DIM**-0.5)
        raised = jnp.where(allowed, jnp.exp(scores), 0.0)
        probabilities = (raised / jnp.sum(raised, axis=0, keepdims=True)).astype(jnp.bfloat16)
        context = matmul(values[at], probabilities, (((1,), (0,)), ((), ()))).astype(jnp.bfloat16)
        for copy in range(out_ref.shape[0]):
            out_ref[copy, at, :] = context
    copies[6].wait()
    for column in range(half_ref.shape[1] // length):
        block = half_ref[:, column * length : (column + 1) * length]
        at = slice(head_width + column * half, head_width + (column + 1) * half)
        for copy in range(out_ref.shape[0]):
            out_ref[copy, at, :] = block
    for copy in copies[8:]:
        copy.wait()


def ffn_kernel(
    hidden_ref,
    merged_ref,
    other_ref,
    gain_ref,
    in_ref,
    down_ref,
    near_half_ref,
    far_half_ref,
    after_ref,
    out_ref,
    weight_ref,
    shards_ref,
):
    length, width = hidden_ref.shape
    shards = merged_ref.shape[0]
    head_width = width // shards
    half = head_width // 2
    for shard in range(shards):
        for column in range(width // length):
            to = slice(column * length, (column + 1) * length)
            at = slice(column * half, (column + 1) * half)
            mine = merged_ref[shard, head_width + column * half : head_width + (column + 1) * half]
            for core, block in (
                (lax.axis_index("core"), mine),
                (1 - lax.axis_index("core"), other_ref[shard, at, :]),
            ):
                first = pl.multiple_of(shard * head_width + core * half, half)
                weight_ref[pl.ds(first, half), to] = block
    context = jnp.concatenate([merged_ref[shard, :head_width] for shard in range(shards)], axis=0)
    after_attn = hidden_ref[...].astype(jnp.float32) + matmul(context, weight_ref[...], TN)
    units = near_half_ref.shape[0] // 3
    for slot in range(3):
        at = slice(slot * units, (slot + 1) * units)
        own = down_ref[...] if slot == 2 else in_ref[slot]
        parts = [own, near_half_ref[at, :], far_half_ref[at, :]]
        shards_ref[slot] = jnp.concatenate(parts, axis=0)
    mixed = layer_norm(after_attn, gain_ref[...].reshape(1, -1)).astype(jnp.bfloat16)
    inner_up = matmul(shards_ref[0], mixed, NT)
    gate_part = matmul(shards_ref[1], mixed, NT)
    activated = (gelu(inner_up) * gate_part).astype(jnp.bfloat16)
    partial = matmul(activated, shards_ref[2], TN)
    after_ref[...] = after_attn + partial
    out_ref[...] = partial.astype(jnp.bfloat16)


def head_kernel(after_ref, partial_ref, final_ref, dense_ref, head_ref, out_ref):
    after_ffn = after_ref[...] + partial_ref[...].astype(jnp.float32)
    normed = layer_norm(after_ffn, final_ref[...].reshape(1, -1)).astype(jnp.bfloat16)
    dense = matmul(normed, dense_ref[...], (((1,), (0,)), ((), ())))
    headed = layer_norm(gelu(dense), head_ref[...].reshape(1, -1))
    out_ref[...] = headed.astype(jnp.bfloat16)


def prep_kernel(segment_ref, list_ref, docs_ref, bounds_ref, mask_ref):
    segments = segment_ref[...]
    slot = lax.broadcasted_iota(jnp.int32, bounds_ref.shape, 1)
    bounds = jnp.zeros(bounds_ref.shape, jnp.int32)
    for passage in range(1, PASS_DEV + 1):
        before = jnp.sum((segments < passage).astype(jnp.int32), axis=1, keepdims=True)
        bounds = jnp.where(slot == passage, before, bounds)
    bounds_ref[...] = bounds
    own_terms, passages = mask_ref.shape
    groups = own_terms // SPAN
    stride = segment_ref.shape[0] * SPAN // BLOCK
    first_block = lax.axis_index("term") * groups * stride + row_index() * SPAN // BLOCK
    blocks = list_ref[...] - first_block
    bits = jnp.zeros(blocks.shape, jnp.float32)
    for group in range(groups):
        bits = jnp.where(blocks == group * stride, np.float32(2**group), bits)
    ones = jnp.ones((SPAN, bits.shape[1]), jnp.bfloat16)
    codes = matmul(ones, bits.astype(jnp.bfloat16), NT).astype(jnp.bfloat16)
    columns = lax.broadcasted_iota(jnp.int32, (passages, passages), 1)
    place = (docs_ref[...] == columns).astype(jnp.float32).astype(jnp.bfloat16)
    placed = matmul(codes, place, (((1,), (0,)), ((), ()))).astype(jnp.int32)
    for group in range(groups):
        held = jnp.bitwise_and(lax.shift_right_logical(placed, group), 1)
        mask_ref[group * SPAN : (group + 1) * SPAN, :] = held.astype(jnp.float32)


def passage_maxima(bounds_ref, first_row, rows, table_ref, logits_ref):
    length = rows[0].shape[0]
    stacked = jnp.concatenate([row[...] for row in rows], axis=0)
    logits_ref[...] = matmul(stacked, table_ref[...], NT)
    tile = 8
    sublane = lax.broadcasted_iota(jnp.int32, (tile, logits_ref.shape[1]), 0)
    maxima = []
    for r in range(len(rows)):
        row = row_index(first_row + r)
        for passage in range(PASS_DEV):
            first = bounds_ref[row, passage]
            end = bounds_ref[row, passage + 1]
            first_tile = lax.shift_right_logical(first, 3)
            last_tile = lax.shift_right_logical(end - 1, 3)

            def load(t):
                return logits_ref[pl.ds(pl.multiple_of(r * length + t * tile, tile), tile), :]

            def inside(t):
                token = sublane + t * tile
                return jnp.where((token >= first) & (token < end), load(t), LOWEST)

            held = jnp.maximum(inside(first_tile), inside(last_tile))
            held = lax.fori_loop(
                first_tile + 1, last_tile, lambda t, m: jnp.maximum(m, load(t)), held
            )
            maxima.append(jnp.max(held, axis=0, keepdims=True))
    return jnp.concatenate(maxima, axis=0)


def near_pool_kernel(bounds_ref, own_ref, core_ref, table_ref, low_ref, logits_ref):
    rows = (own_ref, core_ref)
    low_ref[...] = passage_maxima(bounds_ref, 0, rows, table_ref, logits_ref)


def far_pool_kernel(
    bounds_ref, far_ref, far_core_ref, table_ref, low_ref, out_ref, logits_ref
):
    rows = (far_ref, far_core_ref)
    high = passage_maxima(bounds_ref, len(rows), rows, table_ref, logits_ref)
    low = low_ref[...]
    own_terms = out_ref.shape[2] // 2
    for slot in range(out_ref.shape[0]):
        at = slice(slot * own_terms, (slot + 1) * own_terms)
        to = slot - slot % NEAR + jnp.bitwise_xor(lax.axis_index("zh"), slot % NEAR)
        out_ref[to] = jnp.concatenate([low[:, at], high[:, at]], axis=1)


def place_kernel(maxima_ref, bias_ref, mask_ref, docs_ref, out_ref):
    raw = maxima_ref[...] + bias_ref[...]
    weighted = jnp.log1p(jnp.maximum(raw, 0.0))
    own_terms, passages = out_ref.shape
    columns = lax.broadcasted_iota(jnp.int32, (weighted.shape[0], passages), 1)
    terms = []
    rest = weighted
    for _ in range(3):
        terms.append(rest.astype(jnp.bfloat16))
        rest = rest - terms[-1].astype(jnp.float32)
    placed = jnp.zeros((own_terms, passages), jnp.float32)
    for half in range(2):
        place = (docs_ref[half] == columns).astype(jnp.float32).astype(jnp.bfloat16)
        at = slice(half * own_terms, (half + 1) * own_terms)
        sums = [matmul(term, place, TN)[at] for term in terms]
        placed = placed + (sums[0] + sums[1] + sums[2])
    out_ref[...] = placed * mask_ref[...]


def vmem():
    return pl.BlockSpec(memory_space=pltpu.VMEM)


def hbm():
    return pl.BlockSpec(memory_space=pltpu.HBM)


def smem():
    return pl.BlockSpec(memory_space=pltpu.SMEM)


def grant(mib):
    return pltpu.CompilerParams(vmem_limit_bytes=mib << 20)


def cost(flops, nbytes):
    return pl.CostEstimate(flops=flops, bytes_accessed=nbytes, transcendentals=0)


def exchange(copies, axis):
    return lax.all_to_all(copies, axis, split_axis=0, concat_axis=0, tiled=True)


def swap(block, axis, d=1):
    return lax.ppermute(block, axis, [(i, i ^ d) for i in range(lax.axis_size(axis))])


def others(block, axis):
    return [swap(block, axis, d) for d in range(1, lax.axis_size(axis))]


def on_device(
    hidden,
    segment_ids,
    block_lists,
    doc_ids,
    attn_gain,
    qkv_weight,
    attn_out,
    mlp_gain,
    ffn_in,
    ffn_out,
    final_gain,
    head_dense,
    head_gain,
    decoder,
    decoder_bias,
):
    near = ("y", "zh")
    slices = lax.axis_size(near)
    near_row = lax.axis_index(("zl", "core"))
    rows_here = lax.axis_size(("zl", "core"))
    tensor = lax.axis_size("term")
    tokens = hidden[0]
    length, width = tokens.shape
    groups, span = decoder.shape[1], decoder.shape[3]
    own_terms = groups * span
    head_width = qkv_weight.shape[2]
    passages = block_lists.shape[0]
    near_rows = jnp.stack([jnp.bitwise_xor(near_row, d) for d in range(rows_here)])

    own_slice = decoder.reshape(own_terms, width)
    rotary = jnp.asarray(rotary_table(length))
    half = head_width // 2
    chunk = head_width + half * width // length
    pieces = others(own_slice, "zh")
    ffn_in_rows = jnp.swapaxes(ffn_in, 1, 2)
    units = ffn_out.shape[0] // 2
    merged, shard = pl.pallas_call(
        attention_kernel,
        out_shape=(
            jax.ShapeDtypeStruct((tensor, chunk, length), jnp.bfloat16),
            jax.ShapeDtypeStruct((3 * units, width), jnp.bfloat16),
        ),
        in_specs=[hbm()] * 8,
        out_specs=(vmem(), vmem()),
        scratch_shapes=[
            pltpu.VMEM((width,), jnp.float32),
            pltpu.VMEM((length, width), jnp.bfloat16),
            pltpu.VMEM((8, length), jnp.int32),
            pltpu.VMEM((3, head_width, width), jnp.bfloat16),
            pltpu.VMEM(rotary.shape, jnp.bfloat16),
            pltpu.VMEM((half, width), jnp.bfloat16),
            pltpu.SemaphoreType.DMA((11,)),
        ],
        compiler_params=grant(60),
        cost_estimate=cost(1200000000, 2000000),
        name="attention",
    )(
        attn_gain,
        tokens,
        segment_ids,
        jnp.swapaxes(qkv_weight, 1, 2),
        rotary,
        attn_out,
        ffn_in_rows,
        ffn_out,
    )
    pieces, merged, shard = lax.optimization_barrier((pieces, merged, shard))
    part = jnp.concatenate([own_slice] + pieces, axis=0)
    table = lax.all_gather(part, "y", axis=0, tiled=True)
    merged, near_half = lax.optimization_barrier(
        (exchange(merged, "term"), swap(shard, "term", 1))
    )
    other = swap(merged[:, head_width:], "core")
    far_half = swap(near_half, "core")
    after_ffn, partial = pl.pallas_call(
        ffn_kernel,
        out_shape=(
            jax.ShapeDtypeStruct((length, width), jnp.float32),
            jax.ShapeDtypeStruct((length, width), jnp.bfloat16),
        ),
        in_specs=[vmem()] * 8,
        out_specs=(vmem(), vmem()),
        scratch_shapes=[
            pltpu.VMEM((width, width), jnp.bfloat16),
            pltpu.VMEM((3, 4 * units, width), jnp.bfloat16),
        ],
        compiler_params=grant(20),
        cost_estimate=cost(1200000000, 4000000),
        name="ffn",
    )(tokens, merged, other, mlp_gain, ffn_in_rows, ffn_out, near_half, far_half)
    bounds, mask = pl.pallas_call(
        prep_kernel,
        out_shape=(
            jax.ShapeDtypeStruct((segment_ids.shape[0], 2 * PASS_DEV), jnp.int32),
            jax.ShapeDtypeStruct((own_terms, passages), jnp.float32),
        ),
        in_specs=[vmem()] * 3,
        out_specs=(vmem(), vmem()),
        compiler_params=grant(20),
        cost_estimate=cost(1000000, 1000000),
        name="prep",
    )(segment_ids, block_lists, doc_ids[:, None])
    rest = swap(partial, "term", 3)
    rest, bounds, mask = lax.optimization_barrier((rest, bounds, mask))
    headed = pl.pallas_call(
        head_kernel,
        out_shape=jax.ShapeDtypeStruct((length, width), jnp.bfloat16),
        in_specs=[vmem()] * 5,
        out_specs=vmem(),
        compiler_params=grant(20),
        cost_estimate=cost(800000000, 5000000),
        name="head",
    )(after_ffn, rest, final_gain, head_dense, head_gain)

    far = swap(headed, "zl")
    core = swap(headed, "core")
    terms_here = slices * own_terms
    logits = pltpu.VMEM((2 * length, terms_here), jnp.float32)
    low = pl.pallas_call(
        near_pool_kernel,
        out_shape=jax.ShapeDtypeStruct((2 * PASS_DEV, terms_here), jnp.float32),
        in_specs=[smem()] + [vmem()] * 3,
        out_specs=vmem(),
        scratch_shapes=[logits],
        compiler_params=grant(20),
        cost_estimate=cost(1600000000, 4000000),
        name="near_pool",
    )(bounds, headed, core, table)
    far_core = swap(far, "core")
    pooled = pl.pallas_call(
        far_pool_kernel,
        out_shape=jax.ShapeDtypeStruct((slices, 2 * PASS_DEV, 2 * own_terms), jnp.float32),
        in_specs=[smem()] + [vmem()] * 4,
        out_specs=vmem(),
        scratch_shapes=[logits],
        compiler_params=grant(20),
        cost_estimate=cost(1600000000, 4000000),
        name="far_pool",
    )(bounds, far, far_core, table, low)
    received = exchange(pooled, near)

    bias = decoder_bias.reshape(1, own_terms).astype(jnp.float32)
    docs = doc_ids.reshape(slices, rows_here, PASS_DEV)
    docs = jnp.stack([docs[:, near_rows[d]] for d in range(rows_here)], axis=1)
    docs = jnp.transpose(docs.reshape(slices, 2, 2 * PASS_DEV), (1, 0, 2)).reshape(2, -1, 1)
    placed = pl.pallas_call(
        place_kernel,
        out_shape=jax.ShapeDtypeStruct((own_terms, passages), jnp.float32),
        in_specs=[vmem()] * 4,
        out_specs=vmem(),
        cost_estimate=cost(200000000, 1000000),
        compiler_params=grant(16),
        name="place",
    )(
        received.reshape(-1, 2 * own_terms),
        jnp.concatenate([bias, bias], axis=1),
        mask,
        docs,
    )
    return placed.reshape(1, groups, 1, span, passages)


def solution(mesh):
    shape = (8, 4, 2, 2, mesh.devices.shape[1])
    fine = Mesh(mesh.devices.reshape(shape), ("y", "zh", "zl", "core", "term"))
    dp = ("y", "zh", "zl", "core")
    in_specs = (
        P(dp, None, None),
        P(),
        P(),
        P(),
        P(),
        P(None, None, "term"),
        P("term", None),
        P(),
        P(None, None, "term"),
        P("term", None),
        P(),
        P(),
        P(),
        P("term", None, dp, None, None),
        P("term", None, dp, None),
    )
    out_specs = P("term", None, dp, None, None)
    return jax.shard_map(
        on_device, mesh=fine, in_specs=in_specs, out_specs=out_specs, check_vma=False
    )
```

```python
import functools

import jax
import jax.numpy as jnp
import numpy as np
from jax import lax
from jax.experimental import pallas as pl
from jax.experimental.pallas import tpu as pltpu
from jax.sharding import Mesh
from jax.sharding import PartitionSpec as P

BLOCK = 128
HALF_WIN = 64
PASS_DEV = 4
HEAD_DIM = 64
HALF_HEAD = 32
SPAN = 8
NEAR = 4
LOWEST = -3.0e38

NT = (((1,), (1,)), ((), ()))
TN = (((0,), (0,)), ((), ()))


def rotary_table(length):
    frequency = 10000.0 ** (-2.0 * np.arange(HALF_HEAD, dtype=np.float64) / HEAD_DIM)
    angles = frequency[:, None] * np.arange(length, dtype=np.float64)[None, :]
    terms = []
    for whole in (np.cos(angles), np.sin(angles)):
        rest = whole.astype(np.float32)
        for _ in range(3):
            term = rest.astype(jnp.bfloat16)
            terms.append(term)
            rest = rest - term.astype(np.float32)
    return np.concatenate(terms, axis=0)


def layer_norm(values, gain_row):
    average = jnp.mean(values, axis=-1, keepdims=True)
    centered = values - average
    spread = jnp.mean(centered * centered, axis=-1, keepdims=True)
    return centered * lax.rsqrt(spread + 1e-05) * gain_row


def gelu(values):
    return 0.5 * values * (1.0 + lax.erf(values * np.float32(0.5**0.5)))


def matmul(left, right, dims):
    return lax.dot_general(left, right, dims, preferred_element_type=jnp.float32)


def row_index(d=0):
    near = lax.axis_index("zl") * lax.axis_size("core") + lax.axis_index("core")
    own = lax.axis_index("y") * lax.axis_size("zh") + lax.axis_index("zh")
    return own * lax.axis_size("zl") * lax.axis_size("core") + jnp.bitwise_xor(near, d)


def attention_kernel(
    gain_hbm,
    hidden_hbm,
    segment_hbm,
    weight_hbm,
    table_hbm,
    out_weight_hbm,
    out_ref,
    gain_ref,
    hidden_ref,
    segment_ref,
    weight_ref,
    table_ref,
    half_ref,
    sems,
):
    length = hidden_ref.shape[0]
    row = row_index()
    tile = pl.multiple_of(lax.shift_left(lax.shift_right_logical(row, 3), 3), 8)
    sem = iter(range(sems.shape[0]))

    def fetch(source, to):
        return pltpu.make_async_copy(source, to, sems.at[next(sem)])

    share = length // 4
    cuts = [slice(i * share, (i + 1) * share) for i in range(4)]
    hidden_copies = [fetch(hidden_hbm.at[cut, :], hidden_ref.at[cut, :]) for cut in cuts]
    hidden_copies.append(fetch(gain_hbm, gain_ref))
    segment_copy = fetch(segment_hbm.at[pl.ds(tile, 8), :], segment_ref)
    table_copy = fetch(table_hbm, table_ref)
    half = half_ref.shape[0]
    weight_copies = [
        fetch(weight_hbm.at[slot, cut, :], weight_ref.at[slot, cut, :])
        for slot in range(3)
        for cut in (slice(0, half), slice(half, 2 * half))
    ]
    own_rows = pl.ds(pl.multiple_of(lax.axis_index("core") * half, half), half)
    half_copy = fetch(out_weight_hbm.at[own_rows, :], half_ref)
    copies = hidden_copies + [segment_copy, table_copy] + weight_copies + [half_copy]
    for copy in copies:
        copy.start()
    segment_copy.wait()
    head_width = weight_ref.shape[1]
    segments = segment_ref[pl.ds(row - tile, 1), :]
    starts = jnp.zeros_like(segments)
    for passage in range(PASS_DEV - 1):
        held = jnp.sum((segments == passage).astype(jnp.int32), axis=1, keepdims=True)
        starts = starts + jnp.where(segments > passage, held, 0)
    lane = lax.broadcasted_iota(jnp.int32, (1, length), 1)
    positions = lane - starts
    sublane = lax.broadcasted_iota(jnp.int32, (length, length), 0)
    table_copy.wait()
    chosen = (sublane == positions).astype(jnp.float32).astype(jnp.bfloat16)
    parts = matmul(table_ref[...], chosen, (((1,), (0,)), ((), ())))
    part = [parts[i * HALF_HEAD : (i + 1) * HALF_HEAD] for i in range(6)]
    cosine = part[0] + part[1] + part[2]
    sine = part[3] + part[4] + part[5]
    lengths = jnp.zeros_like(segments)
    for passage in range(PASS_DEV):
        held = jnp.sum((segments == passage).astype(jnp.int32), axis=1, keepdims=True)
        lengths = jnp.where(segments == passage, held, lengths)
    low = jnp.maximum(starts, lane - HALF_WIN)
    high = jnp.minimum(starts + lengths - 1, lane + HALF_WIN)
    allowed = (sublane >= low) & (sublane <= high)

    for copy in hidden_copies:
        copy.wait()
    gain = gain_ref[...].reshape(1, -1)
    normed = layer_norm(hidden_ref[...].astype(jnp.float32), gain).astype(jnp.bfloat16)
    for copy in weight_copies:
        copy.wait()
    queries = matmul(weight_ref[0], normed, NT)
    key_cols = matmul(weight_ref[1], normed, NT)
    values = matmul(weight_ref[2], normed, NT).astype(jnp.bfloat16)

    def rotate(block):
        first, second = block[:HALF_HEAD], block[HALF_HEAD:]
        turned = jnp.concatenate(
            [first * cosine - second * sine, second * cosine + first * sine], axis=0
        )
        return turned.astype(jnp.bfloat16)

    for head in range(head_width // HEAD_DIM):
        at = slice(head * HEAD_DIM, (head + 1) * HEAD_DIM)
        scores = matmul(rotate(key_cols[at]), rotate(queries[at]), TN) * np.float32(HEAD_DIM**-0.5)
        raised = jnp.where(allowed, jnp.exp(scores), 0.0)
        probabilities = (raised / jnp.sum(raised, axis=0, keepdims=True)).astype(jnp.bfloat16)
        context = matmul(values[at], probabilities, (((1,), (0,)), ((), ()))).astype(jnp.bfloat16)
        for copy in range(out_ref.shape[0]):
            out_ref[copy, at, :] = context
    half_copy.wait()
    for column in range(half_ref.shape[1] // length):
        block = half_ref[:, column * length : (column + 1) * length]
        at = slice(head_width + column * half, head_width + (column + 1) * half)
        for copy in range(out_ref.shape[0]):
            out_ref[copy, at, :] = block


def ffn_kernel(
    hidden_ref, merged_ref, other_ref, gain_ref, in_ref, down_ref, after_ref, out_ref, weight_ref, all_ref
):
    length, width = hidden_ref.shape
    shards = merged_ref.shape[0]
    head_width = width // shards
    half = head_width // 2
    for shard in range(shards):
        for column in range(width // length):
            to = slice(column * length, (column + 1) * length)
            at = slice(column * half, (column + 1) * half)
            mine = merged_ref[shard, head_width + column * half : head_width + (column + 1) * half]
            for core, block in (
                (lax.axis_index("core"), mine),
                (1 - lax.axis_index("core"), other_ref[shard, at, :]),
            ):
                first = pl.multiple_of(shard * head_width + core * half, half)
                weight_ref[pl.ds(first, half), to] = block
    context = jnp.concatenate([merged_ref[shard, :head_width] for shard in range(shards)], axis=0)
    after_attn = hidden_ref[...].astype(jnp.float32) + matmul(context, weight_ref[...], TN)
    all_ref[...] = after_attn
    share = after_ref.shape[0]
    after_ref[...] = all_ref[pl.ds(pl.multiple_of(lax.axis_index("term") * share, share), share), :]
    mixed = layer_norm(after_attn, gain_ref[...].reshape(1, -1)).astype(jnp.bfloat16)
    inner_up = matmul(in_ref[0], mixed, NT)
    gate_part = matmul(in_ref[1], mixed, NT)
    activated = (gelu(inner_up) * gate_part).astype(jnp.bfloat16)
    out_ref[...] = matmul(activated, down_ref[...], TN).astype(jnp.bfloat16)


def head_kernel(after_ref, partial_ref, final_ref, dense_ref, head_ref, out_ref):
    after_ffn = after_ref[...]
    for shard in range(partial_ref.shape[0]):
        after_ffn = after_ffn + partial_ref[shard].astype(jnp.float32)
    normed = layer_norm(after_ffn, final_ref[...].reshape(1, -1)).astype(jnp.bfloat16)
    dense = matmul(normed, dense_ref[...], (((1,), (0,)), ((), ())))
    headed = layer_norm(gelu(dense), head_ref[...].reshape(1, -1)).astype(jnp.bfloat16)
    for copy in range(out_ref.shape[0]):
        out_ref[copy] = headed


def prep_kernel(segment_ref, list_ref, docs_ref, bounds_ref, mask_ref):
    segments = segment_ref[...]
    slot = lax.broadcasted_iota(jnp.int32, bounds_ref.shape, 1)
    bounds = jnp.zeros(bounds_ref.shape, jnp.int32)
    for passage in range(1, PASS_DEV + 1):
        before = jnp.sum((segments < passage).astype(jnp.int32), axis=1, keepdims=True)
        bounds = jnp.where(slot == passage, before, bounds)
    bounds_ref[...] = bounds
    own_terms, passages = mask_ref.shape
    groups = own_terms // SPAN
    stride = segment_ref.shape[0] * SPAN // BLOCK
    first_block = lax.axis_index("term") * groups * stride + row_index() * SPAN // BLOCK
    blocks = list_ref[...] - first_block
    bits = jnp.zeros(blocks.shape, jnp.float32)
    for group in range(groups):
        bits = jnp.where(blocks == group * stride, np.float32(2**group), bits)
    ones = jnp.ones((SPAN, bits.shape[1]), jnp.bfloat16)
    codes = matmul(ones, bits.astype(jnp.bfloat16), NT).astype(jnp.bfloat16)
    columns = lax.broadcasted_iota(jnp.int32, (passages, passages), 1)
    place = (docs_ref[...] == columns).astype(jnp.float32).astype(jnp.bfloat16)
    placed = matmul(codes, place, (((1,), (0,)), ((), ()))).astype(jnp.int32)
    for group in range(groups):
        held = jnp.bitwise_and(lax.shift_right_logical(placed, group), 1)
        mask_ref[group * SPAN : (group + 1) * SPAN, :] = held.astype(jnp.float32)


def passage_maxima(bounds_ref, rows, length, logits_ref):
    tile = 8
    sublane = lax.broadcasted_iota(jnp.int32, (tile, logits_ref.shape[1]), 0)
    maxima = []
    for r in range(rows):
        row = row_index(r)
        for passage in range(PASS_DEV):
            first = bounds_ref[row, passage]
            end = bounds_ref[row, passage + 1]
            first_tile = lax.shift_right_logical(first, 3)
            last_tile = lax.shift_right_logical(end - 1, 3)

            def load(t):
                return logits_ref[pl.ds(pl.multiple_of(r * length + t * tile, tile), tile), :]

            def inside(t):
                token = sublane + t * tile
                return jnp.where((token >= first) & (token < end), load(t), LOWEST)

            held = jnp.maximum(inside(first_tile), inside(last_tile))
            held = lax.fori_loop(
                first_tile + 1, last_tile, lambda t, m: jnp.maximum(m, load(t)), held
            )
            maxima.append(jnp.max(held, axis=0, keepdims=True))
    return jnp.concatenate(maxima, axis=0)


def pool_kernel(
    bounds_ref, own_ref, core_ref, far_ref, far_core_ref, table_ref, out_ref, rows_ref, logits_ref
):
    rows = (own_ref, core_ref, far_ref, far_core_ref)
    length = own_ref.shape[0]

    @pl.when(pl.program_id(0) == 0)
    def _():
        for r, row in enumerate(rows):
            rows_ref[r * length : (r + 1) * length, :] = row[...]

    logits_ref[...] = matmul(rows_ref[...], table_ref[...], NT)
    maxima = passage_maxima(bounds_ref, len(rows), length, logits_ref)
    half = maxima.shape[0] // 2
    own_terms = out_ref.shape[2] // 2
    for slot in range(out_ref.shape[0]):
        at = slice(slot * own_terms, (slot + 1) * own_terms)
        to = slot - slot % NEAR + jnp.bitwise_xor(lax.axis_index("zh"), slot % NEAR)
        out_ref[to] = jnp.concatenate([maxima[:half, at], maxima[half:, at]], axis=1)


def place_kernel(maxima_ref, bias_ref, mask_ref, docs_ref, out_ref):
    raw = maxima_ref[...] + bias_ref[...]
    weighted = jnp.log1p(jnp.maximum(raw, 0.0))
    own_terms, passages = out_ref.shape
    columns = lax.broadcasted_iota(jnp.int32, (weighted.shape[0], passages), 1)
    terms = []
    rest = weighted
    for _ in range(3):
        terms.append(rest.astype(jnp.bfloat16))
        rest = rest - terms[-1].astype(jnp.float32)
    placed = jnp.zeros((own_terms, passages), jnp.float32)
    for half in range(2):
        place = (docs_ref[half] == columns).astype(jnp.float32).astype(jnp.bfloat16)
        at = slice(half * own_terms, (half + 1) * own_terms)
        sums = [matmul(term, place, TN)[at] for term in terms]
        placed = placed + (sums[0] + sums[1] + sums[2])
    out_ref[...] = placed * mask_ref[...]


def vmem():
    return pl.BlockSpec(memory_space=pltpu.VMEM)


def hbm():
    return pl.BlockSpec(memory_space=pltpu.HBM)


def smem():
    return pl.BlockSpec(memory_space=pltpu.SMEM)


def grant(mib):
    return pltpu.CompilerParams(vmem_limit_bytes=mib << 20)


def cost(flops, nbytes):
    return pl.CostEstimate(flops=flops, bytes_accessed=nbytes, transcendentals=0)


def exchange(copies, axis):
    return lax.all_to_all(copies, axis, split_axis=0, concat_axis=0, tiled=True)


def swap(block, axis, d=1):
    return lax.ppermute(block, axis, [(i, i ^ d) for i in range(lax.axis_size(axis))])


def others(block, axis):
    return [swap(block, axis, d) for d in range(1, lax.axis_size(axis))]


def on_device(
    hidden,
    segment_ids,
    block_lists,
    doc_ids,
    attn_gain,
    qkv_weight,
    attn_out,
    mlp_gain,
    ffn_in,
    ffn_out,
    final_gain,
    head_dense,
    head_gain,
    decoder,
    decoder_bias,
):
    near = ("y", "zh")
    slices = lax.axis_size(near)
    near_row = lax.axis_index(("zl", "core"))
    rows_here = lax.axis_size(("zl", "core"))
    tensor = lax.axis_size("term")
    tokens = hidden[0]
    length, width = tokens.shape
    groups, span = decoder.shape[1], decoder.shape[3]
    own_terms = groups * span
    head_width = qkv_weight.shape[2]
    passages = block_lists.shape[0]
    near_rows = jnp.stack([jnp.bitwise_xor(near_row, d) for d in range(rows_here)])

    own_slice = decoder.reshape(own_terms, width)
    rotary = jnp.asarray(rotary_table(length))
    half = head_width // 2
    chunk = head_width + half * width // length
    merged = pl.pallas_call(
        attention_kernel,
        out_shape=jax.ShapeDtypeStruct((tensor, chunk, length), jnp.bfloat16),
        in_specs=[hbm()] * 6,
        out_specs=vmem(),
        scratch_shapes=[
            pltpu.VMEM((width,), jnp.float32),
            pltpu.VMEM((length, width), jnp.bfloat16),
            pltpu.VMEM((8, length), jnp.int32),
            pltpu.VMEM((3, head_width, width), jnp.bfloat16),
            pltpu.VMEM(rotary.shape, jnp.bfloat16),
            pltpu.VMEM((half, width), jnp.bfloat16),
            pltpu.SemaphoreType.DMA((14,)),
        ],
        compiler_params=grant(60),
        cost_estimate=cost(1200000000, 2000000),
        name="attention",
    )(attn_gain, tokens, segment_ids, jnp.swapaxes(qkv_weight, 1, 2), rotary, attn_out)
    own_slice, merged = lax.optimization_barrier((own_slice, merged))
    part = jnp.concatenate([own_slice] + others(own_slice, "zh"), axis=0)
    merged, part = lax.optimization_barrier((exchange(merged, "term"), part))
    table = lax.all_gather(part, "y", axis=0, tiled=True)
    other = swap(merged[:, head_width:], "core")
    after_attn, partial = pl.pallas_call(
        ffn_kernel,
        out_shape=(
            jax.ShapeDtypeStruct((length // tensor, width), jnp.float32),
            jax.ShapeDtypeStruct((length, width), jnp.bfloat16),
        ),
        in_specs=[vmem()] * 6,
        out_specs=(vmem(), vmem()),
        scratch_shapes=[
            pltpu.VMEM((width, width), jnp.bfloat16),
            pltpu.VMEM((length, width), jnp.float32),
        ],
        compiler_params=grant(20),
        cost_estimate=cost(700000000, 4000000),
        name="ffn",
    )(tokens, merged, other, mlp_gain, jnp.swapaxes(ffn_in, 1, 2), ffn_out)
    bounds, mask = pl.pallas_call(
        prep_kernel,
        out_shape=(
            jax.ShapeDtypeStruct((segment_ids.shape[0], 2 * PASS_DEV), jnp.int32),
            jax.ShapeDtypeStruct((own_terms, passages), jnp.float32),
        ),
        in_specs=[vmem()] * 3,
        out_specs=(vmem(), vmem()),
        compiler_params=grant(20),
        cost_estimate=cost(1000000, 1000000),
        name="prep",
    )(segment_ids, block_lists, doc_ids[:, None])
    partials = exchange(partial.reshape(tensor, -1, width), "term")
    partials, bounds, mask = lax.optimization_barrier((partials, bounds, mask))
    headed = pl.pallas_call(
        head_kernel,
        out_shape=jax.ShapeDtypeStruct((tensor, length // tensor, width), jnp.bfloat16),
        in_specs=[vmem()] * 5,
        out_specs=vmem(),
        compiler_params=grant(20),
        cost_estimate=cost(800000000, 5000000),
        name="head",
    )(after_attn, partials, final_gain, head_dense, head_gain)

    headed = exchange(headed, "term").reshape(length, width)

    far = swap(headed, "zl")
    core = swap(headed, "core")
    far_core = swap(far, "core")
    terms_here = slices * own_terms
    step = terms_here // 2
    pooled = pl.pallas_call(
        pool_kernel,
        out_shape=jax.ShapeDtypeStruct((slices, 2 * PASS_DEV, 2 * own_terms), jnp.float32),
        grid=(terms_here // step,),
        in_specs=[smem()]
        + [pl.BlockSpec((length, width), lambda j: (0, 0))] * rows_here
        + [pl.BlockSpec((step, width), lambda j: (j, 0))],
        out_specs=pl.BlockSpec(
            (step // own_terms, 2 * PASS_DEV, 2 * own_terms), lambda j: (j, 0, 0)
        ),
        scratch_shapes=[
            pltpu.VMEM((rows_here * length, width), jnp.bfloat16),
            pltpu.VMEM((rows_here * length, step), jnp.float32),
        ],
        compiler_params=grant(56),
        cost_estimate=cost(3300000000, 6000000),
        name="pool",
    )(bounds, headed, core, far, far_core, table)
    received = exchange(pooled, near)

    bias = decoder_bias.reshape(1, own_terms).astype(jnp.float32)
    docs = doc_ids.reshape(slices, rows_here, PASS_DEV)
    docs = jnp.stack([docs[:, near_rows[d]] for d in range(rows_here)], axis=1)
    docs = jnp.transpose(docs.reshape(slices, 2, 2 * PASS_DEV), (1, 0, 2)).reshape(2, -1, 1)
    placed = pl.pallas_call(
        place_kernel,
        out_shape=jax.ShapeDtypeStruct((own_terms, passages), jnp.float32),
        in_specs=[vmem()] * 4,
        out_specs=vmem(),
        cost_estimate=cost(200000000, 1000000),
        compiler_params=grant(16),
        name="place",
    )(
        received.reshape(-1, 2 * own_terms),
        jnp.concatenate([bias, bias], axis=1),
        mask,
        docs,
    )
    return placed.reshape(1, groups, 1, span, passages)


def solution(mesh):
    shape = (8, 4, 2, 2, mesh.devices.shape[1])
    fine = Mesh(mesh.devices.reshape(shape), ("y", "zh", "zl", "core", "term"))
    dp = ("y", "zh", "zl", "core")
    in_specs = (
        P(dp, None, None),
        P(),
        P(),
        P(),
        P(),
        P(None, None, "term"),
        P("term", None),
        P(),
        P(None, None, "term"),
        P("term", None),
        P(),
        P(),
        P(),
        P("term", None, dp, None, None),
        P("term", None, dp, None),
    )
    out_specs = P("term", None, dp, None, None)
    return jax.shard_map(
        on_device, mesh=fine, in_specs=in_specs, out_specs=out_specs, check_vma=False
    )
```

```python
import functools

import jax
import jax.numpy as jnp
import numpy as np
from jax import lax
from jax.experimental import pallas as pl
from jax.experimental.pallas import tpu as pltpu
from jax.sharding import Mesh
from jax.sharding import PartitionSpec as P

BLOCK = 128
HALF_WIN = 64
PASS_DEV = 4
HEAD_DIM = 64
HALF_HEAD = 32
SPAN = 8
NEAR = 4
LOWEST = -3.0e38

NT = (((1,), (1,)), ((), ()))
TN = (((0,), (0,)), ((), ()))


def rotary_table(length):
    frequency = 10000.0 ** (-2.0 * np.arange(HALF_HEAD, dtype=np.float64) / HEAD_DIM)
    angles = frequency[:, None] * np.arange(length, dtype=np.float64)[None, :]
    terms = []
    for whole in (np.cos(angles), np.sin(angles)):
        rest = whole.astype(np.float32)
        for _ in range(3):
            term = rest.astype(jnp.bfloat16)
            terms.append(term)
            rest = rest - term.astype(np.float32)
    return np.concatenate(terms, axis=0)


def layer_norm(values, gain_row):
    average = jnp.mean(values, axis=-1, keepdims=True)
    centered = values - average
    spread = jnp.mean(centered * centered, axis=-1, keepdims=True)
    return centered * lax.rsqrt(spread + 1e-05) * gain_row


def gelu(values):
    return 0.5 * values * (1.0 + lax.erf(values * np.float32(0.5**0.5)))


def matmul(left, right, dims):
    return lax.dot_general(left, right, dims, preferred_element_type=jnp.float32)


def row_index(d=0):
    near = lax.axis_index("zl") * lax.axis_size("core") + lax.axis_index("core")
    own = lax.axis_index("y") * lax.axis_size("zh") + lax.axis_index("zh")
    return own * lax.axis_size("zl") * lax.axis_size("core") + jnp.bitwise_xor(near, d)


def attention_kernel(
    gain_hbm,
    hidden_hbm,
    segment_hbm,
    weight_hbm,
    table_hbm,
    out_weight_hbm,
    out_ref,
    gain_ref,
    hidden_ref,
    segment_ref,
    weight_ref,
    table_ref,
    half_ref,
    sems,
):
    length = hidden_ref.shape[0]
    row = row_index()
    tile = pl.multiple_of(lax.shift_left(lax.shift_right_logical(row, 3), 3), 8)
    sem = iter(range(sems.shape[0]))

    def fetch(source, to):
        return pltpu.make_async_copy(source, to, sems.at[next(sem)])

    share = length // 4
    cuts = [slice(i * share, (i + 1) * share) for i in range(4)]
    hidden_copies = [fetch(hidden_hbm.at[cut, :], hidden_ref.at[cut, :]) for cut in cuts]
    hidden_copies.append(fetch(gain_hbm, gain_ref))
    segment_copy = fetch(segment_hbm.at[pl.ds(tile, 8), :], segment_ref)
    table_copy = fetch(table_hbm, table_ref)
    half = half_ref.shape[0]
    weight_copies = [
        fetch(weight_hbm.at[slot, cut, :], weight_ref.at[slot, cut, :])
        for slot in range(3)
        for cut in (slice(0, half), slice(half, 2 * half))
    ]
    own_rows = pl.ds(pl.multiple_of(lax.axis_index("core") * half, half), half)
    half_copy = fetch(out_weight_hbm.at[own_rows, :], half_ref)
    copies = hidden_copies + [segment_copy, table_copy] + weight_copies + [half_copy]
    for copy in copies:
        copy.start()
    segment_copy.wait()
    head_width = weight_ref.shape[1]
    segments = segment_ref[pl.ds(row - tile, 1), :]
    starts = jnp.zeros_like(segments)
    for passage in range(PASS_DEV - 1):
        held = jnp.sum((segments == passage).astype(jnp.int32), axis=1, keepdims=True)
        starts = starts + jnp.where(segments > passage, held, 0)
    lane = lax.broadcasted_iota(jnp.int32, (1, length), 1)
    positions = lane - starts
    sublane = lax.broadcasted_iota(jnp.int32, (length, length), 0)
    table_copy.wait()
    chosen = (sublane == positions).astype(jnp.float32).astype(jnp.bfloat16)
    parts = matmul(table_ref[...], chosen, (((1,), (0,)), ((), ())))
    part = [parts[i * HALF_HEAD : (i + 1) * HALF_HEAD] for i in range(6)]
    cosine = part[0] + part[1] + part[2]
    sine = part[3] + part[4] + part[5]
    lengths = jnp.zeros_like(segments)
    for passage in range(PASS_DEV):
        held = jnp.sum((segments == passage).astype(jnp.int32), axis=1, keepdims=True)
        lengths = jnp.where(segments == passage, held, lengths)
    low = jnp.maximum(starts, lane - HALF_WIN)
    high = jnp.minimum(starts + lengths - 1, lane + HALF_WIN)
    allowed = (sublane >= low) & (sublane <= high)

    for copy in hidden_copies:
        copy.wait()
    gain = gain_ref[...].reshape(1, -1)
    normed = layer_norm(hidden_ref[...].astype(jnp.float32), gain).astype(jnp.bfloat16)
    for copy in weight_copies:
        copy.wait()
    queries = matmul(weight_ref[0], normed, NT)
    key_cols = matmul(weight_ref[1], normed, NT)
    values = matmul(weight_ref[2], normed, NT).astype(jnp.bfloat16)

    def rotate(block):
        first, second = block[:HALF_HEAD], block[HALF_HEAD:]
        turned = jnp.concatenate(
            [first * cosine - second * sine, second * cosine + first * sine], axis=0
        )
        return turned.astype(jnp.bfloat16)

    for head in range(head_width // HEAD_DIM):
        at = slice(head * HEAD_DIM, (head + 1) * HEAD_DIM)
        scores = matmul(rotate(key_cols[at]), rotate(queries[at]), TN) * np.float32(HEAD_DIM**-0.5)
        raised = jnp.where(allowed, jnp.exp(scores), 0.0)
        probabilities = (raised / jnp.sum(raised, axis=0, keepdims=True)).astype(jnp.bfloat16)
        context = matmul(values[at], probabilities, (((1,), (0,)), ((), ()))).astype(jnp.bfloat16)
        for copy in range(out_ref.shape[0]):
            out_ref[copy, at, :] = context
    half_copy.wait()
    for column in range(half_ref.shape[1] // length):
        block = half_ref[:, column * length : (column + 1) * length]
        at = slice(head_width + column * half, head_width + (column + 1) * half)
        for copy in range(out_ref.shape[0]):
            out_ref[copy, at, :] = block


def ffn_kernel(
    hidden_ref, merged_ref, other_ref, gain_ref, in_ref, down_ref, after_ref, out_ref, weight_ref, all_ref
):
    length, width = hidden_ref.shape
    shards = merged_ref.shape[0]
    head_width = width // shards
    half = head_width // 2
    for shard in range(shards):
        for column in range(width // length):
            to = slice(column * length, (column + 1) * length)
            at = slice(column * half, (column + 1) * half)
            mine = merged_ref[shard, head_width + column * half : head_width + (column + 1) * half]
            for core, block in (
                (lax.axis_index("core"), mine),
                (1 - lax.axis_index("core"), other_ref[shard, at, :]),
            ):
                first = pl.multiple_of(shard * head_width + core * half, half)
                weight_ref[pl.ds(first, half), to] = block
    context = jnp.concatenate([merged_ref[shard, :head_width] for shard in range(shards)], axis=0)
    after_attn = hidden_ref[...].astype(jnp.float32) + matmul(context, weight_ref[...], TN)
    all_ref[...] = after_attn
    share = after_ref.shape[0]
    after_ref[...] = all_ref[pl.ds(pl.multiple_of(lax.axis_index("term") * share, share), share), :]
    mixed = layer_norm(after_attn, gain_ref[...].reshape(1, -1)).astype(jnp.bfloat16)
    inner_up = matmul(in_ref[0], mixed, NT)
    gate_part = matmul(in_ref[1], mixed, NT)
    activated = (gelu(inner_up) * gate_part).astype(jnp.bfloat16)
    out_ref[...] = matmul(activated, down_ref[...], TN).astype(jnp.bfloat16)


def head_kernel(after_ref, partial_ref, final_ref, dense_ref, head_ref, out_ref):
    after_ffn = after_ref[...]
    for shard in range(partial_ref.shape[0]):
        after_ffn = after_ffn + partial_ref[shard].astype(jnp.float32)
    normed = layer_norm(after_ffn, final_ref[...].reshape(1, -1)).astype(jnp.bfloat16)
    dense = matmul(normed, dense_ref[...], (((1,), (0,)), ((), ())))
    headed = layer_norm(gelu(dense), head_ref[...].reshape(1, -1)).astype(jnp.bfloat16)
    for copy in range(out_ref.shape[0]):
        out_ref[copy] = headed


def prep_kernel(segment_ref, list_ref, docs_ref, bounds_ref, mask_ref):
    segments = segment_ref[...]
    slot = lax.broadcasted_iota(jnp.int32, bounds_ref.shape, 1)
    bounds = jnp.zeros(bounds_ref.shape, jnp.int32)
    for passage in range(1, PASS_DEV + 1):
        before = jnp.sum((segments < passage).astype(jnp.int32), axis=1, keepdims=True)
        bounds = jnp.where(slot == passage, before, bounds)
    bounds_ref[...] = bounds
    own_terms, passages = mask_ref.shape
    groups = own_terms // SPAN
    stride = segment_ref.shape[0] * SPAN // BLOCK
    first_block = lax.axis_index("term") * groups * stride + row_index() * SPAN // BLOCK
    blocks = list_ref[...] - first_block
    bits = jnp.zeros(blocks.shape, jnp.float32)
    for group in range(groups):
        bits = jnp.where(blocks == group * stride, np.float32(2**group), bits)
    ones = jnp.ones((SPAN, bits.shape[1]), jnp.bfloat16)
    codes = matmul(ones, bits.astype(jnp.bfloat16), NT).astype(jnp.bfloat16)
    columns = lax.broadcasted_iota(jnp.int32, (passages, passages), 1)
    place = (docs_ref[...] == columns).astype(jnp.float32).astype(jnp.bfloat16)
    placed = matmul(codes, place, (((1,), (0,)), ((), ()))).astype(jnp.int32)
    for group in range(groups):
        held = jnp.bitwise_and(lax.shift_right_logical(placed, group), 1)
        mask_ref[group * SPAN : (group + 1) * SPAN, :] = held.astype(jnp.float32)


def passage_maxima(bounds_ref, rows, length, logits_ref):
    tile = 8
    sublane = lax.broadcasted_iota(jnp.int32, (tile, logits_ref.shape[1]), 0)
    maxima = []
    for r in range(rows):
        row = row_index(r)
        for passage in range(PASS_DEV):
            first = bounds_ref[row, passage]
            end = bounds_ref[row, passage + 1]
            first_tile = lax.shift_right_logical(first, 3)
            last_tile = lax.shift_right_logical(end - 1, 3)

            def load(t):
                return logits_ref[pl.ds(pl.multiple_of(r * length + t * tile, tile), tile), :]

            def inside(t):
                token = sublane + t * tile
                return jnp.where((token >= first) & (token < end), load(t), LOWEST)

            held = jnp.maximum(inside(first_tile), inside(last_tile))
            held = lax.fori_loop(
                first_tile + 1, last_tile, lambda t, m: jnp.maximum(m, load(t)), held
            )
            maxima.append(jnp.max(held, axis=0, keepdims=True))
    return jnp.concatenate(maxima, axis=0)


def pool_kernel(
    bounds_ref, own_ref, core_ref, far_ref, far_core_ref, table_ref, out_ref, rows_ref, logits_ref
):
    rows = (own_ref, core_ref, far_ref, far_core_ref)
    length = own_ref.shape[0]

    @pl.when(pl.program_id(0) == 0)
    def _():
        for r, row in enumerate(rows):
            rows_ref[r * length : (r + 1) * length, :] = row[...]

    logits_ref[...] = matmul(rows_ref[...], table_ref[...], NT)
    maxima = passage_maxima(bounds_ref, len(rows), length, logits_ref)
    half = maxima.shape[0] // 2
    own_terms = out_ref.shape[2] // 2
    for slot in range(out_ref.shape[0]):
        at = slice(slot * own_terms, (slot + 1) * own_terms)
        to = slot - slot % NEAR + jnp.bitwise_xor(lax.axis_index("zh"), slot % NEAR)
        out_ref[to] = jnp.concatenate([maxima[:half, at], maxima[half:, at]], axis=1)


def place_kernel(maxima_ref, bias_ref, mask_ref, docs_ref, out_ref):
    raw = maxima_ref[...] + bias_ref[...]
    weighted = jnp.log1p(jnp.maximum(raw, 0.0))
    own_terms, passages = out_ref.shape
    columns = lax.broadcasted_iota(jnp.int32, (weighted.shape[0], passages), 1)
    terms = []
    rest = weighted
    for _ in range(3):
        terms.append(rest.astype(jnp.bfloat16))
        rest = rest - terms[-1].astype(jnp.float32)
    placed = jnp.zeros((own_terms, passages), jnp.float32)
    for half in range(2):
        place = (docs_ref[half] == columns).astype(jnp.float32).astype(jnp.bfloat16)
        at = slice(half * own_terms, (half + 1) * own_terms)
        sums = [matmul(term, place, TN)[at] for term in terms]
        placed = placed + (sums[0] + sums[1] + sums[2])
    out_ref[...] = placed * mask_ref[...]


def vmem():
    return pl.BlockSpec(memory_space=pltpu.VMEM)


def hbm():
    return pl.BlockSpec(memory_space=pltpu.HBM)


def smem():
    return pl.BlockSpec(memory_space=pltpu.SMEM)


def grant(mib):
    return pltpu.CompilerParams(vmem_limit_bytes=mib << 20)


def cost(flops, nbytes):
    return pl.CostEstimate(flops=flops, bytes_accessed=nbytes, transcendentals=0)


def exchange(copies, axis):
    return lax.all_to_all(copies, axis, split_axis=0, concat_axis=0, tiled=True)


def swap(block, axis, d=1):
    return lax.ppermute(block, axis, [(i, i ^ d) for i in range(lax.axis_size(axis))])


def others(block, axis):
    return [swap(block, axis, d) for d in range(1, lax.axis_size(axis))]


def on_device(
    hidden,
    segment_ids,
    block_lists,
    doc_ids,
    attn_gain,
    qkv_weight,
    attn_out,
    mlp_gain,
    ffn_in,
    ffn_out,
    final_gain,
    head_dense,
    head_gain,
    decoder,
    decoder_bias,
):
    near = ("y", "zh")
    slices = lax.axis_size(near)
    near_row = lax.axis_index(("zl", "core"))
    rows_here = lax.axis_size(("zl", "core"))
    tensor = lax.axis_size("term")
    tokens = hidden[0]
    length, width = tokens.shape
    groups, span = decoder.shape[1], decoder.shape[3]
    own_terms = groups * span
    head_width = qkv_weight.shape[2]
    passages = block_lists.shape[0]
    near_rows = jnp.stack([jnp.bitwise_xor(near_row, d) for d in range(rows_here)])

    own_slice = decoder.reshape(own_terms, width)
    rotary = jnp.asarray(rotary_table(length))
    half = head_width // 2
    chunk = head_width + half * width // length
    merged = pl.pallas_call(
        attention_kernel,
        out_shape=jax.ShapeDtypeStruct((tensor, chunk, length), jnp.bfloat16),
        in_specs=[hbm()] * 6,
        out_specs=vmem(),
        scratch_shapes=[
            pltpu.VMEM((width,), jnp.float32),
            pltpu.VMEM((length, width), jnp.bfloat16),
            pltpu.VMEM((8, length), jnp.int32),
            pltpu.VMEM((3, head_width, width), jnp.bfloat16),
            pltpu.VMEM(rotary.shape, jnp.bfloat16),
            pltpu.VMEM((half, width), jnp.bfloat16),
            pltpu.SemaphoreType.DMA((14,)),
        ],
        compiler_params=grant(60),
        cost_estimate=cost(1200000000, 2000000),
        name="attention",
    )(attn_gain, tokens, segment_ids, jnp.swapaxes(qkv_weight, 1, 2), rotary, attn_out)
    across = swap(own_slice, "zh", 2)
    late_slice, merged = lax.optimization_barrier((own_slice, merged))
    pieces = [own_slice, swap(late_slice, "zh", 1), across, swap(late_slice, "zh", 3)]
    part = jnp.concatenate(pieces, axis=0)
    merged, part = lax.optimization_barrier((exchange(merged, "term"), part))
    table = lax.all_gather(part, "y", axis=0, tiled=True)
    other = swap(merged[:, head_width:], "core")
    after_attn, partial = pl.pallas_call(
        ffn_kernel,
        out_shape=(
            jax.ShapeDtypeStruct((length // tensor, width), jnp.float32),
            jax.ShapeDtypeStruct((length, width), jnp.bfloat16),
        ),
        in_specs=[vmem()] * 6,
        out_specs=(vmem(), vmem()),
        scratch_shapes=[
            pltpu.VMEM((width, width), jnp.bfloat16),
            pltpu.VMEM((length, width), jnp.float32),
        ],
        compiler_params=grant(20),
        cost_estimate=cost(700000000, 4000000),
        name="ffn",
    )(tokens, merged, other, mlp_gain, jnp.swapaxes(ffn_in, 1, 2), ffn_out)
    bounds, mask = pl.pallas_call(
        prep_kernel,
        out_shape=(
            jax.ShapeDtypeStruct((segment_ids.shape[0], 2 * PASS_DEV), jnp.int32),
            jax.ShapeDtypeStruct((own_terms, passages), jnp.float32),
        ),
        in_specs=[vmem()] * 3,
        out_specs=(vmem(), vmem()),
        compiler_params=grant(20),
        cost_estimate=cost(1000000, 1000000),
        name="prep",
    )(segment_ids, block_lists, doc_ids[:, None])
    partials = exchange(partial.reshape(tensor, -1, width), "term")
    partials, bounds, mask = lax.optimization_barrier((partials, bounds, mask))
    headed = pl.pallas_call(
        head_kernel,
        out_shape=jax.ShapeDtypeStruct((tensor, length // tensor, width), jnp.bfloat16),
        in_specs=[vmem()] * 5,
        out_specs=vmem(),
        compiler_params=grant(20),
        cost_estimate=cost(800000000, 5000000),
        name="head",
    )(after_attn, partials, final_gain, head_dense, head_gain)

    headed = exchange(headed, "term").reshape(length, width)

    far = swap(headed, "zl")
    core = swap(headed, "core")
    far_core = swap(far, "core")
    terms_here = slices * own_terms
    step = terms_here // 2
    pooled = pl.pallas_call(
        pool_kernel,
        out_shape=jax.ShapeDtypeStruct((slices, 2 * PASS_DEV, 2 * own_terms), jnp.float32),
        grid=(terms_here // step,),
        in_specs=[smem()]
        + [pl.BlockSpec((length, width), lambda j: (0, 0))] * rows_here
        + [pl.BlockSpec((step, width), lambda j: (j, 0))],
        out_specs=pl.BlockSpec(
            (step // own_terms, 2 * PASS_DEV, 2 * own_terms), lambda j: (j, 0, 0)
        ),
        scratch_shapes=[
            pltpu.VMEM((rows_here * length, width), jnp.bfloat16),
            pltpu.VMEM((rows_here * length, step), jnp.float32),
        ],
        compiler_params=grant(56),
        cost_estimate=cost(3300000000, 6000000),
        name="pool",
    )(bounds, headed, core, far, far_core, table)
    received = exchange(pooled, near)

    bias = decoder_bias.reshape(1, own_terms).astype(jnp.float32)
    docs = doc_ids.reshape(slices, rows_here, PASS_DEV)
    docs = jnp.stack([docs[:, near_rows[d]] for d in range(rows_here)], axis=1)
    docs = jnp.transpose(docs.reshape(slices, 2, 2 * PASS_DEV), (1, 0, 2)).reshape(2, -1, 1)
    placed = pl.pallas_call(
        place_kernel,
        out_shape=jax.ShapeDtypeStruct((own_terms, passages), jnp.float32),
        in_specs=[vmem()] * 4,
        out_specs=vmem(),
        cost_estimate=cost(200000000, 1000000),
        compiler_params=grant(16),
        name="place",
    )(
        received.reshape(-1, 2 * own_terms),
        jnp.concatenate([bias, bias], axis=1),
        mask,
        docs,
    )
    return placed.reshape(1, groups, 1, span, passages)


def solution(mesh):
    shape = (8, 4, 2, 2, mesh.devices.shape[1])
    fine = Mesh(mesh.devices.reshape(shape), ("y", "zh", "zl", "core", "term"))
    dp = ("y", "zh", "zl", "core")
    in_specs = (
        P(dp, None, None),
        P(),
        P(),
        P(),
        P(),
        P(None, None, "term"),
        P("term", None),
        P(),
        P(None, None, "term"),
        P("term", None),
        P(),
        P(),
        P(),
        P("term", None, dp, None, None),
        P("term", None, dp, None),
    )
    out_specs = P("term", None, dp, None, None)
    return jax.shard_map(
        on_device, mesh=fine, in_specs=in_specs, out_specs=out_specs, check_vma=False
    )
```

```python
import functools

import jax
import jax.numpy as jnp
import numpy as np
from jax import lax
from jax.experimental import pallas as pl
from jax.experimental.pallas import tpu as pltpu
from jax.sharding import Mesh
from jax.sharding import PartitionSpec as P

BLOCK = 128
HALF_WIN = 64
PASS_DEV = 4
HEAD_DIM = 64
HALF_HEAD = 32
SPAN = 8
NEAR = 4
LOWEST = -3.0e38

NT = (((1,), (1,)), ((), ()))
TN = (((0,), (0,)), ((), ()))


def rotary_table(length):
    frequency = 10000.0 ** (-2.0 * np.arange(HALF_HEAD, dtype=np.float64) / HEAD_DIM)
    angles = frequency[:, None] * np.arange(length, dtype=np.float64)[None, :]
    terms = []
    for whole in (np.cos(angles), np.sin(angles)):
        rest = whole.astype(np.float32)
        for _ in range(3):
            term = rest.astype(jnp.bfloat16)
            terms.append(term)
            rest = rest - term.astype(np.float32)
    return np.concatenate(terms, axis=0)


def layer_norm(values, gain_row):
    average = jnp.mean(values, axis=-1, keepdims=True)
    centered = values - average
    spread = jnp.mean(centered * centered, axis=-1, keepdims=True)
    return centered * lax.rsqrt(spread + 1e-05) * gain_row


def gelu(values):
    return 0.5 * values * (1.0 + lax.erf(values * np.float32(0.5**0.5)))


def matmul(left, right, dims):
    return lax.dot_general(left, right, dims, preferred_element_type=jnp.float32)


def row_index(d=0):
    near = lax.axis_index("zl") * lax.axis_size("core") + lax.axis_index("core")
    own = lax.axis_index("y") * lax.axis_size("zh") + lax.axis_index("zh")
    return own * lax.axis_size("zl") * lax.axis_size("core") + jnp.bitwise_xor(near, d)


def attention_kernel(
    gain_hbm,
    hidden_hbm,
    segment_hbm,
    weight_hbm,
    table_hbm,
    out_weight_hbm,
    out_hbm,
    gain_ref,
    hidden_ref,
    segment_ref,
    weight_ref,
    table_ref,
    context_ref,
    sems,
):
    length = hidden_ref.shape[0]
    row = row_index()
    tile = pl.multiple_of(lax.shift_left(lax.shift_right_logical(row, 3), 3), 8)
    sem = iter(range(sems.shape[0]))

    def fetch(source, to):
        return pltpu.make_async_copy(source, to, sems.at[next(sem)])

    share = length // 4
    cuts = [slice(i * share, (i + 1) * share) for i in range(4)]
    hidden_copies = [fetch(hidden_hbm.at[cut, :], hidden_ref.at[cut, :]) for cut in cuts]
    hidden_copies.append(fetch(gain_hbm, gain_ref))
    segment_copy = fetch(segment_hbm.at[pl.ds(tile, 8), :], segment_ref)
    table_copy = fetch(table_hbm, table_ref)
    head_width, length = context_ref.shape
    half = head_width // 2
    weight_copies = [
        fetch(weight_hbm.at[slot, cut, :], weight_ref.at[slot, cut, :])
        for slot in range(3)
        for cut in (slice(0, half), slice(half, 2 * half))
    ]
    own_rows = pl.ds(pl.multiple_of(lax.axis_index("core") * half, half), half)
    half_copies = [
        fetch(
            out_weight_hbm.at[own_rows, column * length : (column + 1) * length],
            out_hbm.at[place, head_width + column * half : head_width + (column + 1) * half, :],
        )
        for column in range(out_weight_hbm.shape[1] // length)
        for place in range(out_hbm.shape[0])
    ]
    copies = hidden_copies + [segment_copy, table_copy] + weight_copies + half_copies
    for copy in copies:
        copy.start()
    segment_copy.wait()
    segments = segment_ref[pl.ds(row - tile, 1), :]
    starts = jnp.zeros_like(segments)
    for passage in range(PASS_DEV - 1):
        held = jnp.sum((segments == passage).astype(jnp.int32), axis=1, keepdims=True)
        starts = starts + jnp.where(segments > passage, held, 0)
    lane = lax.broadcasted_iota(jnp.int32, (1, length), 1)
    positions = lane - starts
    sublane = lax.broadcasted_iota(jnp.int32, (length, length), 0)
    table_copy.wait()
    chosen = (sublane == positions).astype(jnp.float32).astype(jnp.bfloat16)
    parts = matmul(table_ref[...], chosen, (((1,), (0,)), ((), ())))
    part = [parts[i * HALF_HEAD : (i + 1) * HALF_HEAD] for i in range(6)]
    cosine = part[0] + part[1] + part[2]
    sine = part[3] + part[4] + part[5]
    lengths = jnp.zeros_like(segments)
    for passage in range(PASS_DEV):
        held = jnp.sum((segments == passage).astype(jnp.int32), axis=1, keepdims=True)
        lengths = jnp.where(segments == passage, held, lengths)
    low = jnp.maximum(starts, lane - HALF_WIN)
    high = jnp.minimum(starts + lengths - 1, lane + HALF_WIN)
    allowed = (sublane >= low) & (sublane <= high)

    for copy in hidden_copies:
        copy.wait()
    gain = gain_ref[...].reshape(1, -1)
    normed = layer_norm(hidden_ref[...].astype(jnp.float32), gain).astype(jnp.bfloat16)
    for copy in weight_copies:
        copy.wait()
    queries = matmul(weight_ref[0], normed, NT)
    key_cols = matmul(weight_ref[1], normed, NT)
    values = matmul(weight_ref[2], normed, NT).astype(jnp.bfloat16)

    def rotate(block):
        first, second = block[:HALF_HEAD], block[HALF_HEAD:]
        turned = jnp.concatenate(
            [first * cosine - second * sine, second * cosine + first * sine], axis=0
        )
        return turned.astype(jnp.bfloat16)

    for head in range(head_width // HEAD_DIM):
        at = slice(head * HEAD_DIM, (head + 1) * HEAD_DIM)
        scores = matmul(rotate(key_cols[at]), rotate(queries[at]), TN) * np.float32(HEAD_DIM**-0.5)
        raised = jnp.where(allowed, jnp.exp(scores), 0.0)
        probabilities = (raised / jnp.sum(raised, axis=0, keepdims=True)).astype(jnp.bfloat16)
        context = matmul(values[at], probabilities, (((1,), (0,)), ((), ()))).astype(jnp.bfloat16)
        context_ref[at, :] = context
        for place in range(out_hbm.shape[0]):
            sent = fetch(context_ref.at[at, :], out_hbm.at[place, at, :])
            sent.start()
            half_copies.append(sent)
    for copy in half_copies:
        copy.wait()


def ffn_kernel(
    hidden_ref, merged_ref, other_ref, gain_ref, in_ref, down_ref, after_ref, out_ref, weight_ref, all_ref
):
    length, width = hidden_ref.shape
    shards = merged_ref.shape[0]
    head_width = width // shards
    half = head_width // 2
    for shard in range(shards):
        for column in range(width // length):
            to = slice(column * length, (column + 1) * length)
            at = slice(column * half, (column + 1) * half)
            mine = merged_ref[shard, head_width + column * half : head_width + (column + 1) * half]
            for core, block in (
                (lax.axis_index("core"), mine),
                (1 - lax.axis_index("core"), other_ref[shard, at, :]),
            ):
                first = pl.multiple_of(shard * head_width + core * half, half)
                weight_ref[pl.ds(first, half), to] = block
    context = jnp.concatenate([merged_ref[shard, :head_width] for shard in range(shards)], axis=0)
    after_attn = hidden_ref[...].astype(jnp.float32) + matmul(context, weight_ref[...], TN)
    all_ref[...] = after_attn
    share = after_ref.shape[0]
    after_ref[...] = all_ref[pl.ds(pl.multiple_of(lax.axis_index("term") * share, share), share), :]
    mixed = layer_norm(after_attn, gain_ref[...].reshape(1, -1)).astype(jnp.bfloat16)
    inner_up = matmul(in_ref[0], mixed, NT)
    gate_part = matmul(in_ref[1], mixed, NT)
    activated = (gelu(inner_up) * gate_part).astype(jnp.bfloat16)
    out_ref[...] = matmul(activated, down_ref[...], TN).astype(jnp.bfloat16)


def head_kernel(after_ref, partial_ref, final_ref, dense_ref, head_ref, out_ref):
    after_ffn = after_ref[...]
    for shard in range(partial_ref.shape[0]):
        after_ffn = after_ffn + partial_ref[shard].astype(jnp.float32)
    normed = layer_norm(after_ffn, final_ref[...].reshape(1, -1)).astype(jnp.bfloat16)
    dense = matmul(normed, dense_ref[...], (((1,), (0,)), ((), ())))
    headed = layer_norm(gelu(dense), head_ref[...].reshape(1, -1)).astype(jnp.bfloat16)
    for copy in range(out_ref.shape[0]):
        out_ref[copy] = headed


def prep_kernel(segment_ref, list_ref, docs_ref, bounds_ref, mask_ref):
    segments = segment_ref[...]
    slot = lax.broadcasted_iota(jnp.int32, bounds_ref.shape, 1)
    bounds = jnp.zeros(bounds_ref.shape, jnp.int32)
    for passage in range(1, PASS_DEV + 1):
        before = jnp.sum((segments < passage).astype(jnp.int32), axis=1, keepdims=True)
        bounds = jnp.where(slot == passage, before, bounds)
    bounds_ref[...] = bounds
    own_terms, passages = mask_ref.shape
    groups = own_terms // SPAN
    stride = segment_ref.shape[0] * SPAN // BLOCK
    first_block = lax.axis_index("term") * groups * stride + row_index() * SPAN // BLOCK
    blocks = list_ref[...] - first_block
    bits = jnp.zeros(blocks.shape, jnp.float32)
    for group in range(groups):
        bits = jnp.where(blocks == group * stride, np.float32(2**group), bits)
    ones = jnp.ones((SPAN, bits.shape[1]), jnp.bfloat16)
    codes = matmul(ones, bits.astype(jnp.bfloat16), NT).astype(jnp.bfloat16)
    columns = lax.broadcasted_iota(jnp.int32, (passages, passages), 1)
    place = (docs_ref[...] == columns).astype(jnp.float32).astype(jnp.bfloat16)
    placed = matmul(codes, place, (((1,), (0,)), ((), ()))).astype(jnp.int32)
    for group in range(groups):
        held = jnp.bitwise_and(lax.shift_right_logical(placed, group), 1)
        mask_ref[group * SPAN : (group + 1) * SPAN, :] = held.astype(jnp.float32)


def passage_maxima(bounds_ref, rows, length, logits_ref):
    tile = 8
    sublane = lax.broadcasted_iota(jnp.int32, (tile, logits_ref.shape[1]), 0)
    maxima = []
    for r in range(rows):
        row = row_index(r)
        for passage in range(PASS_DEV):
            first = bounds_ref[row, passage]
            end = bounds_ref[row, passage + 1]
            first_tile = lax.shift_right_logical(first, 3)
            last_tile = lax.shift_right_logical(end - 1, 3)

            def load(t):
                return logits_ref[pl.ds(pl.multiple_of(r * length + t * tile, tile), tile), :]

            def inside(t):
                token = sublane + t * tile
                return jnp.where((token >= first) & (token < end), load(t), LOWEST)

            held = jnp.maximum(inside(first_tile), inside(last_tile))
            held = lax.fori_loop(
                first_tile + 1, last_tile, lambda t, m: jnp.maximum(m, load(t)), held
            )
            maxima.append(jnp.max(held, axis=0, keepdims=True))
    return jnp.concatenate(maxima, axis=0)


def pool_kernel(
    bounds_ref, own_ref, core_ref, far_ref, far_core_ref, table_ref, out_ref, rows_ref, logits_ref
):
    rows = (own_ref, core_ref, far_ref, far_core_ref)
    length = own_ref.shape[0]

    @pl.when(pl.program_id(0) == 0)
    def _():
        for r, row in enumerate(rows):
            rows_ref[r * length : (r + 1) * length, :] = row[...]

    logits_ref[...] = matmul(rows_ref[...], table_ref[...], NT)
    maxima = passage_maxima(bounds_ref, len(rows), length, logits_ref)
    half = maxima.shape[0] // 2
    own_terms = out_ref.shape[2] // 2
    for slot in range(out_ref.shape[0]):
        at = slice(slot * own_terms, (slot + 1) * own_terms)
        to = slot - slot % NEAR + jnp.bitwise_xor(lax.axis_index("zh"), slot % NEAR)
        out_ref[to] = jnp.concatenate([maxima[:half, at], maxima[half:, at]], axis=1)


def place_kernel(maxima_ref, bias_ref, mask_ref, docs_ref, out_ref):
    raw = maxima_ref[...] + bias_ref[...]
    weighted = jnp.log1p(jnp.maximum(raw, 0.0))
    own_terms, passages = out_ref.shape
    columns = lax.broadcasted_iota(jnp.int32, (weighted.shape[0], passages), 1)
    terms = []
    rest = weighted
    for _ in range(3):
        terms.append(rest.astype(jnp.bfloat16))
        rest = rest - terms[-1].astype(jnp.float32)
    placed = jnp.zeros((own_terms, passages), jnp.float32)
    for half in range(2):
        place = (docs_ref[half] == columns).astype(jnp.float32).astype(jnp.bfloat16)
        at = slice(half * own_terms, (half + 1) * own_terms)
        sums = [matmul(term, place, TN)[at] for term in terms]
        placed = placed + (sums[0] + sums[1] + sums[2])
    out_ref[...] = placed * mask_ref[...]


def vmem():
    return pl.BlockSpec(memory_space=pltpu.VMEM)


def hbm():
    return pl.BlockSpec(memory_space=pltpu.HBM)


def smem():
    return pl.BlockSpec(memory_space=pltpu.SMEM)


def grant(mib):
    return pltpu.CompilerParams(vmem_limit_bytes=mib << 20)


def cost(flops, nbytes):
    return pl.CostEstimate(flops=flops, bytes_accessed=nbytes, transcendentals=0)


def exchange(copies, axis):
    return lax.all_to_all(copies, axis, split_axis=0, concat_axis=0, tiled=True)


def swap(block, axis, d=1):
    return lax.ppermute(block, axis, [(i, i ^ d) for i in range(lax.axis_size(axis))])


def others(block, axis):
    return [swap(block, axis, d) for d in range(1, lax.axis_size(axis))]


def on_device(
    hidden,
    segment_ids,
    block_lists,
    doc_ids,
    attn_gain,
    qkv_weight,
    attn_out,
    mlp_gain,
    ffn_in,
    ffn_out,
    final_gain,
    head_dense,
    head_gain,
    decoder,
    decoder_bias,
):
    near = ("y", "zh")
    slices = lax.axis_size(near)
    near_row = lax.axis_index(("zl", "core"))
    rows_here = lax.axis_size(("zl", "core"))
    tensor = lax.axis_size("term")
    tokens = hidden[0]
    length, width = tokens.shape
    groups, span = decoder.shape[1], decoder.shape[3]
    own_terms = groups * span
    head_width = qkv_weight.shape[2]
    passages = block_lists.shape[0]
    near_rows = jnp.stack([jnp.bitwise_xor(near_row, d) for d in range(rows_here)])

    own_slice = decoder.reshape(own_terms, width)
    rotary = jnp.asarray(rotary_table(length))
    half = head_width // 2
    chunk = head_width + half * width // length
    merged = pl.pallas_call(
        attention_kernel,
        out_shape=jax.ShapeDtypeStruct((tensor, chunk, length), jnp.bfloat16),
        in_specs=[hbm()] * 6,
        out_specs=hbm(),
        scratch_shapes=[
            pltpu.VMEM((width,), jnp.float32),
            pltpu.VMEM((length, width), jnp.bfloat16),
            pltpu.VMEM((8, length), jnp.int32),
            pltpu.VMEM((3, head_width, width), jnp.bfloat16),
            pltpu.VMEM(rotary.shape, jnp.bfloat16),
            pltpu.VMEM((head_width, length), jnp.bfloat16),
            pltpu.SemaphoreType.DMA((37,)),
        ],
        compiler_params=grant(60),
        cost_estimate=cost(1200000000, 2000000),
        name="attention",
    )(attn_gain, tokens, segment_ids, jnp.swapaxes(qkv_weight, 1, 2), rotary, attn_out)
    across = swap(own_slice, "zh", 2)
    late_slice, merged = lax.optimization_barrier((own_slice, merged))
    pieces = [own_slice, swap(late_slice, "zh", 1), across, swap(late_slice, "zh", 3)]
    part = jnp.concatenate(pieces, axis=0)
    merged, part = lax.optimization_barrier((exchange(merged, "term"), part))
    table = lax.all_gather(part, "y", axis=0, tiled=True)
    other = swap(merged[:, head_width:], "core")
    after_attn, partial = pl.pallas_call(
        ffn_kernel,
        out_shape=(
            jax.ShapeDtypeStruct((length // tensor, width), jnp.float32),
            jax.ShapeDtypeStruct((length, width), jnp.bfloat16),
        ),
        in_specs=[vmem()] * 6,
        out_specs=(vmem(), vmem()),
        scratch_shapes=[
            pltpu.VMEM((width, width), jnp.bfloat16),
            pltpu.VMEM((length, width), jnp.float32),
        ],
        compiler_params=grant(20),
        cost_estimate=cost(700000000, 4000000),
        name="ffn",
    )(tokens, merged, other, mlp_gain, jnp.swapaxes(ffn_in, 1, 2), ffn_out)
    bounds, mask = pl.pallas_call(
        prep_kernel,
        out_shape=(
            jax.ShapeDtypeStruct((segment_ids.shape[0], 2 * PASS_DEV), jnp.int32),
            jax.ShapeDtypeStruct((own_terms, passages), jnp.float32),
        ),
        in_specs=[vmem()] * 3,
        out_specs=(vmem(), vmem()),
        compiler_params=grant(20),
        cost_estimate=cost(1000000, 1000000),
        name="prep",
    )(segment_ids, block_lists, doc_ids[:, None])
    partials = exchange(partial.reshape(tensor, -1, width), "term")
    partials, bounds, mask = lax.optimization_barrier((partials, bounds, mask))
    headed = pl.pallas_call(
        head_kernel,
        out_shape=jax.ShapeDtypeStruct((tensor, length // tensor, width), jnp.bfloat16),
        in_specs=[vmem()] * 5,
        out_specs=vmem(),
        compiler_params=grant(20),
        cost_estimate=cost(800000000, 5000000),
        name="head",
    )(after_attn, partials, final_gain, head_dense, head_gain)

    headed = exchange(headed, "term").reshape(length, width)

    far = swap(headed, "zl")
    core = swap(headed, "core")
    far_core = swap(far, "core")
    terms_here = slices * own_terms
    step = terms_here // 2
    pooled = pl.pallas_call(
        pool_kernel,
        out_shape=jax.ShapeDtypeStruct((slices, 2 * PASS_DEV, 2 * own_terms), jnp.float32),
        grid=(terms_here // step,),
        in_specs=[smem()]
        + [pl.BlockSpec((length, width), lambda j: (0, 0))] * rows_here
        + [pl.BlockSpec((step, width), lambda j: (j, 0))],
        out_specs=pl.BlockSpec(
            (step // own_terms, 2 * PASS_DEV, 2 * own_terms), lambda j: (j, 0, 0)
        ),
        scratch_shapes=[
            pltpu.VMEM((rows_here * length, width), jnp.bfloat16),
            pltpu.VMEM((rows_here * length, step), jnp.float32),
        ],
        compiler_params=grant(56),
        cost_estimate=cost(3300000000, 6000000),
        name="pool",
    )(bounds, headed, core, far, far_core, table)
    received = exchange(pooled, near)

    bias = decoder_bias.reshape(1, own_terms).astype(jnp.float32)
    docs = doc_ids.reshape(slices, rows_here, PASS_DEV)
    docs = jnp.stack([docs[:, near_rows[d]] for d in range(rows_here)], axis=1)
    docs = jnp.transpose(docs.reshape(slices, 2, 2 * PASS_DEV), (1, 0, 2)).reshape(2, -1, 1)
    placed = pl.pallas_call(
        place_kernel,
        out_shape=jax.ShapeDtypeStruct((own_terms, passages), jnp.float32),
        in_specs=[vmem()] * 4,
        out_specs=vmem(),
        cost_estimate=cost(200000000, 1000000),
        compiler_params=grant(16),
        name="place",
    )(
        received.reshape(-1, 2 * own_terms),
        jnp.concatenate([bias, bias], axis=1),
        mask,
        docs,
    )
    return placed.reshape(1, groups, 1, span, passages)


def solution(mesh):
    shape = (8, 4, 2, 2, mesh.devices.shape[1])
    fine = Mesh(mesh.devices.reshape(shape), ("y", "zh", "zl", "core", "term"))
    dp = ("y", "zh", "zl", "core")
    in_specs = (
        P(dp, None, None),
        P(),
        P(),
        P(),
        P(),
        P(None, None, "term"),
        P("term", None),
        P(),
        P(None, None, "term"),
        P("term", None),
        P(),
        P(),
        P(),
        P("term", None, dp, None, None),
        P("term", None, dp, None),
    )
    out_specs = P("term", None, dp, None, None)
    return jax.shard_map(
        on_device, mesh=fine, in_specs=in_specs, out_specs=out_specs, check_vma=False
    )
```

```python
import functools

import jax
import jax.numpy as jnp
import numpy as np
from jax import lax
from jax.experimental import pallas as pl
from jax.experimental.pallas import tpu as pltpu
from jax.sharding import Mesh
from jax.sharding import PartitionSpec as P

BLOCK = 128
HALF_WIN = 64
PASS_DEV = 4
HEAD_DIM = 64
HALF_HEAD = 32
SPAN = 8
NEAR = 4
LOWEST = -3.0e38

NT = (((1,), (1,)), ((), ()))
TN = (((0,), (0,)), ((), ()))


def rotary_table(length):
    frequency = 10000.0 ** (-2.0 * np.arange(HALF_HEAD, dtype=np.float64) / HEAD_DIM)
    angles = frequency[:, None] * np.arange(length, dtype=np.float64)[None, :]
    terms = []
    for whole in (np.cos(angles), np.sin(angles)):
        rest = whole.astype(np.float32)
        for _ in range(3):
            term = rest.astype(jnp.bfloat16)
            terms.append(term)
            rest = rest - term.astype(np.float32)
    return np.concatenate(terms, axis=0)


def layer_norm(values, gain_row):
    average = jnp.mean(values, axis=-1, keepdims=True)
    centered = values - average
    spread = jnp.mean(centered * centered, axis=-1, keepdims=True)
    return centered * lax.rsqrt(spread + 1e-05) * gain_row


def gelu(values):
    return 0.5 * values * (1.0 + lax.erf(values * np.float32(0.5**0.5)))


def matmul(left, right, dims):
    return lax.dot_general(left, right, dims, preferred_element_type=jnp.float32)


def row_index(d=0):
    near = lax.axis_index("zl") * lax.axis_size("core") + lax.axis_index("core")
    own = lax.axis_index("y") * lax.axis_size("zh") + lax.axis_index("zh")
    return own * lax.axis_size("zl") * lax.axis_size("core") + jnp.bitwise_xor(near, d)


def attention_kernel(
    gain_hbm,
    hidden_hbm,
    segment_hbm,
    weight_hbm,
    table_hbm,
    out_weight_hbm,
    out_hbm,
    gain_ref,
    hidden_ref,
    segment_ref,
    weight_ref,
    table_ref,
    half_ref,
    context_ref,
    sems,
):
    length = hidden_ref.shape[0]
    row = row_index()
    tile = pl.multiple_of(lax.shift_left(lax.shift_right_logical(row, 3), 3), 8)
    sem = iter(range(sems.shape[0]))

    def fetch(source, to):
        return pltpu.make_async_copy(source, to, sems.at[next(sem)])

    share = length // 4
    cuts = [slice(i * share, (i + 1) * share) for i in range(4)]
    hidden_copies = [fetch(hidden_hbm.at[cut, :], hidden_ref.at[cut, :]) for cut in cuts]
    hidden_copies.append(fetch(gain_hbm, gain_ref))
    segment_copy = fetch(segment_hbm.at[pl.ds(tile, 8), :], segment_ref)
    table_copy = fetch(table_hbm, table_ref)
    head_width, length = context_ref.shape
    half = head_width // 2
    weight_copies = [
        fetch(weight_hbm.at[slot, cut, :], weight_ref.at[slot, cut, :])
        for slot in range(3)
        for cut in (slice(0, half), slice(half, 2 * half))
    ]
    own_rows = pl.ds(pl.multiple_of(lax.axis_index("core") * half, half), half)
    half_copy = fetch(out_weight_hbm.at[own_rows, :], half_ref)
    copies = hidden_copies + [segment_copy, table_copy] + weight_copies + [half_copy]
    for copy in copies:
        copy.start()
    segment_copy.wait()
    segments = segment_ref[pl.ds(row - tile, 1), :]
    starts = jnp.zeros_like(segments)
    for passage in range(PASS_DEV - 1):
        held = jnp.sum((segments == passage).astype(jnp.int32), axis=1, keepdims=True)
        starts = starts + jnp.where(segments > passage, held, 0)
    lane = lax.broadcasted_iota(jnp.int32, (1, length), 1)
    positions = lane - starts
    sublane = lax.broadcasted_iota(jnp.int32, (length, length), 0)
    table_copy.wait()
    chosen = (sublane == positions).astype(jnp.float32).astype(jnp.bfloat16)
    parts = matmul(table_ref[...], chosen, (((1,), (0,)), ((), ())))
    part = [parts[i * HALF_HEAD : (i + 1) * HALF_HEAD] for i in range(6)]
    cosine = part[0] + part[1] + part[2]
    sine = part[3] + part[4] + part[5]
    lengths = jnp.zeros_like(segments)
    for passage in range(PASS_DEV):
        held = jnp.sum((segments == passage).astype(jnp.int32), axis=1, keepdims=True)
        lengths = jnp.where(segments == passage, held, lengths)
    low = jnp.maximum(starts, lane - HALF_WIN)
    high = jnp.minimum(starts + lengths - 1, lane + HALF_WIN)
    allowed = (sublane >= low) & (sublane <= high)

    for copy in hidden_copies:
        copy.wait()
    gain = gain_ref[...].reshape(1, -1)
    normed = layer_norm(hidden_ref[...].astype(jnp.float32), gain).astype(jnp.bfloat16)
    for copy in weight_copies:
        copy.wait()
    half_copy.wait()
    sent_copies = [
        fetch(
            half_ref.at[:, column * length : (column + 1) * length],
            out_hbm.at[place, head_width + column * half : head_width + (column + 1) * half, :],
        )
        for column in range(half_ref.shape[1] // length)
        for place in range(out_hbm.shape[0])
    ]
    for copy in sent_copies:
        copy.start()
    queries = matmul(weight_ref[0], normed, NT)
    key_cols = matmul(weight_ref[1], normed, NT)
    values = matmul(weight_ref[2], normed, NT).astype(jnp.bfloat16)

    def rotate(block):
        first, second = block[:HALF_HEAD], block[HALF_HEAD:]
        turned = jnp.concatenate(
            [first * cosine - second * sine, second * cosine + first * sine], axis=0
        )
        return turned.astype(jnp.bfloat16)

    for head in range(head_width // HEAD_DIM):
        at = slice(head * HEAD_DIM, (head + 1) * HEAD_DIM)
        scores = matmul(rotate(key_cols[at]), rotate(queries[at]), TN) * np.float32(HEAD_DIM**-0.5)
        raised = jnp.where(allowed, jnp.exp(scores), 0.0)
        probabilities = (raised / jnp.sum(raised, axis=0, keepdims=True)).astype(jnp.bfloat16)
        context = matmul(values[at], probabilities, (((1,), (0,)), ((), ()))).astype(jnp.bfloat16)
        context_ref[at, :] = context
        for place in range(out_hbm.shape[0]):
            sent = fetch(context_ref.at[at, :], out_hbm.at[place, at, :])
            sent.start()
            sent_copies.append(sent)
    for copy in sent_copies:
        copy.wait()


def ffn_kernel(
    hidden_ref, merged_ref, other_ref, gain_ref, in_ref, down_ref, after_ref, out_ref, weight_ref, all_ref
):
    length, width = hidden_ref.shape
    shards = merged_ref.shape[0]
    head_width = width // shards
    half = head_width // 2
    for shard in range(shards):
        for column in range(width // length):
            to = slice(column * length, (column + 1) * length)
            at = slice(column * half, (column + 1) * half)
            mine = merged_ref[shard, head_width + column * half : head_width + (column + 1) * half]
            for core, block in (
                (lax.axis_index("core"), mine),
                (1 - lax.axis_index("core"), other_ref[shard, at, :]),
            ):
                first = pl.multiple_of(shard * head_width + core * half, half)
                weight_ref[pl.ds(first, half), to] = block
    context = jnp.concatenate([merged_ref[shard, :head_width] for shard in range(shards)], axis=0)
    after_attn = hidden_ref[...].astype(jnp.float32) + matmul(context, weight_ref[...], TN)
    all_ref[...] = after_attn
    share = after_ref.shape[0]
    after_ref[...] = all_ref[pl.ds(pl.multiple_of(lax.axis_index("term") * share, share), share), :]
    mixed = layer_norm(after_attn, gain_ref[...].reshape(1, -1)).astype(jnp.bfloat16)
    inner_up = matmul(in_ref[0], mixed, NT)
    gate_part = matmul(in_ref[1], mixed, NT)
    activated = (gelu(inner_up) * gate_part).astype(jnp.bfloat16)
    out_ref[...] = matmul(activated, down_ref[...], TN).astype(jnp.bfloat16)


def head_kernel(after_ref, partial_ref, final_ref, dense_ref, head_ref, out_ref):
    after_ffn = after_ref[...]
    for shard in range(partial_ref.shape[0]):
        after_ffn = after_ffn + partial_ref[shard].astype(jnp.float32)
    normed = layer_norm(after_ffn, final_ref[...].reshape(1, -1)).astype(jnp.bfloat16)
    dense = matmul(normed, dense_ref[...], (((1,), (0,)), ((), ())))
    headed = layer_norm(gelu(dense), head_ref[...].reshape(1, -1)).astype(jnp.bfloat16)
    for copy in range(out_ref.shape[0]):
        out_ref[copy] = headed


def prep_kernel(segment_ref, list_ref, docs_ref, bounds_ref, mask_ref):
    segments = segment_ref[...]
    slot = lax.broadcasted_iota(jnp.int32, bounds_ref.shape, 1)
    bounds = jnp.zeros(bounds_ref.shape, jnp.int32)
    for passage in range(1, PASS_DEV + 1):
        before = jnp.sum((segments < passage).astype(jnp.int32), axis=1, keepdims=True)
        bounds = jnp.where(slot == passage, before, bounds)
    bounds_ref[...] = bounds
    own_terms, passages = mask_ref.shape
    groups = own_terms // SPAN
    stride = segment_ref.shape[0] * SPAN // BLOCK
    first_block = lax.axis_index("term") * groups * stride + row_index() * SPAN // BLOCK
    blocks = list_ref[...] - first_block
    bits = jnp.zeros(blocks.shape, jnp.float32)
    for group in range(groups):
        bits = jnp.where(blocks == group * stride, np.float32(2**group), bits)
    ones = jnp.ones((SPAN, bits.shape[1]), jnp.bfloat16)
    codes = matmul(ones, bits.astype(jnp.bfloat16), NT).astype(jnp.bfloat16)
    columns = lax.broadcasted_iota(jnp.int32, (passages, passages), 1)
    place = (docs_ref[...] == columns).astype(jnp.float32).astype(jnp.bfloat16)
    placed = matmul(codes, place, (((1,), (0,)), ((), ()))).astype(jnp.int32)
    for group in range(groups):
        held = jnp.bitwise_and(lax.shift_right_logical(placed, group), 1)
        mask_ref[group * SPAN : (group + 1) * SPAN, :] = held.astype(jnp.float32)


def passage_maxima(bounds_ref, rows, length, logits_ref):
    tile = 8
    sublane = lax.broadcasted_iota(jnp.int32, (tile, logits_ref.shape[1]), 0)
    maxima = []
    for r in range(rows):
        row = row_index(r)
        for passage in range(PASS_DEV):
            first = bounds_ref[row, passage]
            end = bounds_ref[row, passage + 1]
            first_tile = lax.shift_right_logical(first, 3)
            last_tile = lax.shift_right_logical(end - 1, 3)

            def load(t):
                return logits_ref[pl.ds(pl.multiple_of(r * length + t * tile, tile), tile), :]

            def inside(t):
                token = sublane + t * tile
                return jnp.where((token >= first) & (token < end), load(t), LOWEST)

            held = jnp.maximum(inside(first_tile), inside(last_tile))
            held = lax.fori_loop(
                first_tile + 1, last_tile, lambda t, m: jnp.maximum(m, load(t)), held
            )
            maxima.append(jnp.max(held, axis=0, keepdims=True))
    return jnp.concatenate(maxima, axis=0)


def pool_kernel(
    bounds_ref, own_ref, core_ref, far_ref, far_core_ref, table_ref, out_ref, rows_ref, logits_ref
):
    rows = (own_ref, core_ref, far_ref, far_core_ref)
    length = own_ref.shape[0]

    @pl.when(pl.program_id(0) == 0)
    def _():
        for r, row in enumerate(rows):
            rows_ref[r * length : (r + 1) * length, :] = row[...]

    logits_ref[...] = matmul(rows_ref[...], table_ref[...], NT)
    maxima = passage_maxima(bounds_ref, len(rows), length, logits_ref)
    half = maxima.shape[0] // 2
    own_terms = out_ref.shape[2] // 2
    for slot in range(out_ref.shape[0]):
        at = slice(slot * own_terms, (slot + 1) * own_terms)
        to = slot - slot % NEAR + jnp.bitwise_xor(lax.axis_index("zh"), slot % NEAR)
        out_ref[to] = jnp.concatenate([maxima[:half, at], maxima[half:, at]], axis=1)


def place_kernel(maxima_ref, bias_ref, mask_ref, docs_ref, out_ref):
    raw = maxima_ref[...] + bias_ref[...]
    weighted = jnp.log1p(jnp.maximum(raw, 0.0))
    own_terms, passages = out_ref.shape
    columns = lax.broadcasted_iota(jnp.int32, (weighted.shape[0], passages), 1)
    terms = []
    rest = weighted
    for _ in range(3):
        terms.append(rest.astype(jnp.bfloat16))
        rest = rest - terms[-1].astype(jnp.float32)
    placed = jnp.zeros((own_terms, passages), jnp.float32)
    for half in range(2):
        place = (docs_ref[half] == columns).astype(jnp.float32).astype(jnp.bfloat16)
        at = slice(half * own_terms, (half + 1) * own_terms)
        sums = [matmul(term, place, TN)[at] for term in terms]
        placed = placed + (sums[0] + sums[1] + sums[2])
    out_ref[...] = placed * mask_ref[...]


def vmem():
    return pl.BlockSpec(memory_space=pltpu.VMEM)


def hbm():
    return pl.BlockSpec(memory_space=pltpu.HBM)


def smem():
    return pl.BlockSpec(memory_space=pltpu.SMEM)


def grant(mib):
    return pltpu.CompilerParams(vmem_limit_bytes=mib << 20)


def cost(flops, nbytes):
    return pl.CostEstimate(flops=flops, bytes_accessed=nbytes, transcendentals=0)


def exchange(copies, axis):
    return lax.all_to_all(copies, axis, split_axis=0, concat_axis=0, tiled=True)


def swap(block, axis, d=1):
    return lax.ppermute(block, axis, [(i, i ^ d) for i in range(lax.axis_size(axis))])


def others(block, axis):
    return [swap(block, axis, d) for d in range(1, lax.axis_size(axis))]


def on_device(
    hidden,
    segment_ids,
    block_lists,
    doc_ids,
    attn_gain,
    qkv_weight,
    attn_out,
    mlp_gain,
    ffn_in,
    ffn_out,
    final_gain,
    head_dense,
    head_gain,
    decoder,
    decoder_bias,
):
    near = ("y", "zh")
    slices = lax.axis_size(near)
    near_row = lax.axis_index(("zl", "core"))
    rows_here = lax.axis_size(("zl", "core"))
    tensor = lax.axis_size("term")
    tokens = hidden[0]
    length, width = tokens.shape
    groups, span = decoder.shape[1], decoder.shape[3]
    own_terms = groups * span
    head_width = qkv_weight.shape[2]
    passages = block_lists.shape[0]
    near_rows = jnp.stack([jnp.bitwise_xor(near_row, d) for d in range(rows_here)])

    own_slice = decoder.reshape(own_terms, width)
    rotary = jnp.asarray(rotary_table(length))
    half = head_width // 2
    chunk = head_width + half * width // length
    merged = pl.pallas_call(
        attention_kernel,
        out_shape=jax.ShapeDtypeStruct((tensor, chunk, length), jnp.bfloat16),
        in_specs=[hbm()] * 6,
        out_specs=hbm(),
        scratch_shapes=[
            pltpu.VMEM((width,), jnp.float32),
            pltpu.VMEM((length, width), jnp.bfloat16),
            pltpu.VMEM((8, length), jnp.int32),
            pltpu.VMEM((3, head_width, width), jnp.bfloat16),
            pltpu.VMEM(rotary.shape, jnp.bfloat16),
            pltpu.VMEM((half, width), jnp.bfloat16),
            pltpu.VMEM((head_width, length), jnp.bfloat16),
            pltpu.SemaphoreType.DMA((38,)),
        ],
        compiler_params=grant(60),
        cost_estimate=cost(1200000000, 2000000),
        name="attention",
    )(attn_gain, tokens, segment_ids, jnp.swapaxes(qkv_weight, 1, 2), rotary, attn_out)
    across = swap(own_slice, "zh", 2)
    late_slice, merged = lax.optimization_barrier((own_slice, merged))
    pieces = [own_slice, swap(late_slice, "zh", 1), across, swap(late_slice, "zh", 3)]
    part = jnp.concatenate(pieces, axis=0)
    merged, part = lax.optimization_barrier((exchange(merged, "term"), part))
    table = lax.all_gather(part, "y", axis=0, tiled=True)
    other = swap(merged[:, head_width:], "core")
    after_attn, partial = pl.pallas_call(
        ffn_kernel,
        out_shape=(
            jax.ShapeDtypeStruct((length // tensor, width), jnp.float32),
            jax.ShapeDtypeStruct((length, width), jnp.bfloat16),
        ),
        in_specs=[vmem()] * 6,
        out_specs=(vmem(), vmem()),
        scratch_shapes=[
            pltpu.VMEM((width, width), jnp.bfloat16),
            pltpu.VMEM((length, width), jnp.float32),
        ],
        compiler_params=grant(20),
        cost_estimate=cost(700000000, 4000000),
        name="ffn",
    )(tokens, merged, other, mlp_gain, jnp.swapaxes(ffn_in, 1, 2), ffn_out)
    bounds, mask = pl.pallas_call(
        prep_kernel,
        out_shape=(
            jax.ShapeDtypeStruct((segment_ids.shape[0], 2 * PASS_DEV), jnp.int32),
            jax.ShapeDtypeStruct((own_terms, passages), jnp.float32),
        ),
        in_specs=[vmem()] * 3,
        out_specs=(vmem(), vmem()),
        compiler_params=grant(20),
        cost_estimate=cost(1000000, 1000000),
        name="prep",
    )(segment_ids, block_lists, doc_ids[:, None])
    partials = exchange(partial.reshape(tensor, -1, width), "term")
    partials, bounds, mask = lax.optimization_barrier((partials, bounds, mask))
    headed = pl.pallas_call(
        head_kernel,
        out_shape=jax.ShapeDtypeStruct((tensor, length // tensor, width), jnp.bfloat16),
        in_specs=[vmem()] * 5,
        out_specs=vmem(),
        compiler_params=grant(20),
        cost_estimate=cost(800000000, 5000000),
        name="head",
    )(after_attn, partials, final_gain, head_dense, head_gain)

    headed = exchange(headed, "term").reshape(length, width)

    far = swap(headed, "zl")
    core = swap(headed, "core")
    far_core = swap(far, "core")
    terms_here = slices * own_terms
    step = terms_here // 2
    pooled = pl.pallas_call(
        pool_kernel,
        out_shape=jax.ShapeDtypeStruct((slices, 2 * PASS_DEV, 2 * own_terms), jnp.float32),
        grid=(terms_here // step,),
        in_specs=[smem()]
        + [pl.BlockSpec((length, width), lambda j: (0, 0))] * rows_here
        + [pl.BlockSpec((step, width), lambda j: (j, 0))],
        out_specs=pl.BlockSpec(
            (step // own_terms, 2 * PASS_DEV, 2 * own_terms), lambda j: (j, 0, 0)
        ),
        scratch_shapes=[
            pltpu.VMEM((rows_here * length, width), jnp.bfloat16),
            pltpu.VMEM((rows_here * length, step), jnp.float32),
        ],
        compiler_params=grant(56),
        cost_estimate=cost(3300000000, 6000000),
        name="pool",
    )(bounds, headed, core, far, far_core, table)
    received = exchange(pooled, near)

    bias = decoder_bias.reshape(1, own_terms).astype(jnp.float32)
    docs = doc_ids.reshape(slices, rows_here, PASS_DEV)
    docs = jnp.stack([docs[:, near_rows[d]] for d in range(rows_here)], axis=1)
    docs = jnp.transpose(docs.reshape(slices, 2, 2 * PASS_DEV), (1, 0, 2)).reshape(2, -1, 1)
    placed = pl.pallas_call(
        place_kernel,
        out_shape=jax.ShapeDtypeStruct((own_terms, passages), jnp.float32),
        in_specs=[vmem()] * 4,
        out_specs=vmem(),
        cost_estimate=cost(200000000, 1000000),
        compiler_params=grant(16),
        name="place",
    )(
        received.reshape(-1, 2 * own_terms),
        jnp.concatenate([bias, bias], axis=1),
        mask,
        docs,
    )
    return placed.reshape(1, groups, 1, span, passages)


def solution(mesh):
    shape = (8, 4, 2, 2, mesh.devices.shape[1])
    fine = Mesh(mesh.devices.reshape(shape), ("y", "zh", "zl", "core", "term"))
    dp = ("y", "zh", "zl", "core")
    in_specs = (
        P(dp, None, None),
        P(),
        P(),
        P(),
        P(),
        P(None, None, "term"),
        P("term", None),
        P(),
        P(None, None, "term"),
        P("term", None),
        P(),
        P(),
        P(),
        P("term", None, dp, None, None),
        P("term", None, dp, None),
    )
    out_specs = P("term", None, dp, None, None)
    return jax.shard_map(
        on_device, mesh=fine, in_specs=in_specs, out_specs=out_specs, check_vma=False
    )
```
